32 devices in a mesh: tilt: 4 (over z), tile: 8 (over y, x, core).
Axes of the slice: x: 2, y: 2, z: 4, core: 2. Of those that a mesh axis runs over, the one named last changes fastest.
Arguments:
- volumes: bfloat16 [48, 128, 64, 128], P('tile', 'tilt'), may hold values from -0.75 to 0.75
- angles: float32 [8], replicated, may hold values from -1.05 to 1.05
- defocus: float32 [8], P('tilt'), may hold values from 0.01 to 0.1
- row_offsets: int32 [48, 8], P('tile', 'tilt'), may hold values from 0 to 1023, as said below
- col_offsets: int32 [48, 8], P('tile', 'tilt'), may hold values from 0 to 128
- measured: float32 [8, 1024, 256], P('tilt', 'tile'), may hold values from -6 to 6
Outputs:
- residual: float32 [8, 1024, 256], P('tilt', 'tile')
- volume_step: float32 [48, 128, 64, 128], P('tile', 'tilt')
The draws below stay inside these ranges and needn't reach their ends.
Inputs may be any that keep to these rules, and one draw needn't show every extreme that they name: row_offsets[b, t] // 128 is the strip that holds the window's top row. Among the 6 boxes of one index of tile and the 2 tilts of one index of tilt, at most 2 windows have their top row in the same strip; in every draw, for every index of tilt, one strip receives exactly 2 such windows from every index of tile.
All inputs are finite; a program needn't handle non-finite values.
Results may differ from the reference program's by a relative error of at most 0.0047.
Values may be sent and summed in bfloat16 or wider, within the bound.
No kernel may reach another device: no remote copies, remote signals or barrier semaphores. Data moves between devices by JAX's collectives and lax.ppermute only.
A program may use at most 64 MiB of HBM per device.

```python
import math
import jax
import jax.numpy as jnp
from jax import lax

BY = 128
BX = 128
BZ = 64
HR = 8
TILT_DEV = 2
BOX_DEV = 6
STRIP = 128
IMG_W = 256
TILTS = 8
BOXES = 48
IMG_H = 1024
CAP = 2


def draw_row_offsets(key, part):
    tile_count = BOXES // BOX_DEV
    group_count = TILTS // TILT_DEV
    item_count = BOX_DEV * TILT_DEV
    hot_key, block_key, offset_key = jax.random.split(jax.random.fold_in(key, 17), 3)
    busiest = jax.random.randint(hot_key, (group_count,), 0, tile_count, dtype=jnp.int32)
    others = (busiest[:, None] + 1 + jnp.arange((tile_count - 1) * CAP, dtype=jnp.int32)[None, :] // CAP) % tile_count
    block_keys = jax.random.split(block_key, tile_count * group_count)

    def one_block(block_seed, group_index):
        order_key, pick_key = jax.random.split(block_seed)
        item_order = jax.random.permutation(order_key, item_count)
        picked = jax.random.permutation(pick_key, others[group_index])[:item_count - CAP]
        ordered = jnp.concatenate([jnp.full((CAP,), busiest[group_index], jnp.int32), picked.astype(jnp.int32)])
        return jnp.zeros((item_count,), jnp.int32).at[item_order].set(ordered)
    group_of = jnp.tile(jnp.arange(group_count, dtype=jnp.int32), tile_count)
    targets = jax.vmap(one_block)(block_keys, group_of)
    targets = targets.reshape(tile_count, group_count, TILT_DEV, BOX_DEV).transpose(0, 3, 1, 2).reshape(BOXES, TILTS)
    within = jax.random.randint(offset_key, (BOXES, TILTS), 0, STRIP, dtype=jnp.int32)
    return targets * STRIP + within


def place_ends(entries, stream_key, least, largest):
    spot = [jax.random.randint(jax.random.fold_in(stream_key, axis), (), 0, length) for axis, length in enumerate(entries.shape)]
    main_axis = entries.shape.index(max(entries.shape))
    next_to = spot[:main_axis] + [(spot[main_axis] + 1) % entries.shape[main_axis]] + spot[main_axis + 1:]
    return entries.at[tuple(spot)].set(least).at[tuple(next_to)].set(largest)


def block_scale(key, dims, shards, smallest, largest):
    gain, own = 1.0, jax.random.fold_in(key, 6)
    for axis_at, parts in shards:
        heights = jnp.exp(jax.random.uniform(jax.random.fold_in(own, axis_at), (parts,), jnp.float32, smallest / len(shards), largest / len(shards)))
        gain = gain * jnp.repeat(heights, dims[axis_at] // parts).reshape([-1 if axis == axis_at else 1 for axis in range(len(dims))])
    return gain


def scatter_about(own_key, dims, deviation, reach, shards=(), kind=jnp.bfloat16):
    values = jax.random.normal(own_key, dims, jnp.float32) * deviation
    if len(shards) > 0:
        values = block_scale(own_key, dims, shards, -0.22, 0.18) * values
    return jnp.clip(values, min=-reach, max=reach).astype(kind)


def setup_inputs(seed: int = 0) -> dict:
    seeds = jax.random.split(jax.random.key(seed), 7)
    volumes = scatter_about(seeds[0], (BOXES, BY, BZ, BX), 0.125, 0.75, ((0, 8), (1, 4)))
    angles = jnp.clip(jax.random.uniform(seeds[1], (TILTS,), jnp.float32, -1.05, 1.05), -1.05, 1.05)
    defocus = jnp.clip(jnp.exp(math.log(0.1) - 2.3025851 * jax.random.uniform(seeds[2], (TILTS,), jnp.float32) ** block_scale(seeds[2], (TILTS,), ((0, 4),), -0.2, 0.2)), 0.01, 0.1)
    row_offsets = draw_row_offsets(jax.random.fold_in(seeds[6], 71), 0)
    col_offsets = place_ends(jax.random.randint(seeds[4], (BOXES, TILTS), 0, IMG_W - BX + 1), jax.random.fold_in(seeds[4], 1), 0, IMG_W - BX).astype(jnp.int32)
    measured = scatter_about(seeds[5], (TILTS, IMG_H, IMG_W), 1.0, 6.0, ((0, 4), (1, 8)), jnp.float32)
    return dict(volumes=volumes, angles=angles, defocus=defocus, row_offsets=row_offsets, col_offsets=col_offsets, measured=measured)


def shear_shift(tilt_angle, depth_values, box_depth):
    return (depth_values - (box_depth - 1) / 2.0) * jnp.sin(tilt_angle)


def tap_weight(offset, layer_shift):
    return jnp.maximum(0.0, 1.0 - jnp.abs(offset - layer_shift))


def point_spread(rho_sq, defocus, radius):
    spread_scale = float(radius * radius)
    return jnp.exp(-rho_sq / (2.0 * spread_scale)) * jnp.cos(defocus * rho_sq) / spread_scale


def rounded_weights(lower_tap, shifts):
    near_half = lax.optimization_barrier(tap_weight(lower_tap, shifts).astype(jnp.bfloat16))
    far_half = lax.optimization_barrier(tap_weight(lower_tap + 1.0, shifts).astype(jnp.bfloat16))
    return near_half.astype(jnp.float32), far_half.astype(jnp.float32)


def project_boxes(volumes, angles):
    margin = BZ // 2 + 2
    layers = jnp.pad(volumes, ((0, 0), (0, 0), (0, 0), (margin, margin))).transpose(2, 0, 1, 3)
    depth_values = jnp.arange(BZ, dtype=jnp.float32)

    def one_tilt(tilt_angle):
        shifts = shear_shift(tilt_angle, depth_values, BZ)
        lower_tap = jnp.floor(shifts)
        near_weight, far_weight = rounded_weights(lower_tap, shifts)
        starts = (margin - lower_tap).astype(jnp.int32)

        def add_layer(summed, inputs):
            depth_layer, begin_column, near_scale, far_scale = inputs
            near_layer = lax.dynamic_slice_in_dim(depth_layer, begin_column, BX, 2).astype(jnp.float32)
            far_layer = lax.dynamic_slice_in_dim(depth_layer, begin_column - 1, BX, 2).astype(jnp.float32)
            return summed + near_scale * near_layer + far_scale * far_layer, None

        summed, _ = lax.scan(add_layer, jnp.zeros((BOXES, BY, BX), jnp.float32), (layers, starts, near_weight, far_weight))
        return summed.astype(jnp.bfloat16)

    return lax.map(one_tilt, angles)


def back_project(back_windows, angles):
    margin = BZ // 2 + 2
    padded = jnp.pad(back_windows, ((0, 0), (0, 0), (0, 0), (margin, margin)))

    def one_layer(depth_value):
        shifts = shear_shift(angles, depth_value, BZ)
        lower_tap = jnp.floor(shifts)
        near_weight, far_weight = rounded_weights(lower_tap, shifts)
        starts = (margin + lower_tap).astype(jnp.int32)

        def add_tilt(summed, inputs):
            window_set, begin_column, near_scale, far_scale = inputs
            near_layer = lax.dynamic_slice_in_dim(window_set, begin_column, BX, 2).astype(jnp.float32)
            far_layer = lax.dynamic_slice_in_dim(window_set, begin_column + 1, BX, 2).astype(jnp.float32)
            return summed + near_scale * near_layer + far_scale * far_layer, None

        summed, _ = lax.scan(add_tilt, jnp.zeros((BOXES, BY, BX), jnp.float32), (padded, starts, near_weight, far_weight))
        return summed

    layers = lax.map(one_layer, jnp.arange(BZ, dtype=jnp.float32))
    return layers.transpose(1, 2, 0, 3) * (1.0 / TILTS)


def convolve(image_field, spread):
    result = lax.conv_general_dilated(
        image_field.astype(jnp.float32)[None],
        spread.astype(jnp.float32)[:, None],
        (1, 1),
        ((HR, HR), (HR, HR)),
        dimension_numbers=("NCHW", "OIHW", "NCHW"),
        feature_group_count=TILTS,
        precision=lax.Precision.HIGHEST,
    )
    return result[0]


def reference(volumes, angles, defocus, row_offsets, col_offsets, measured):
    windows = project_boxes(volumes, angles)
    canvas = jnp.zeros((TILTS, IMG_H + BY, IMG_W), jnp.float32)

    def place_item(item_index, current):
        tilt_index = (item_index // BOXES).astype(jnp.int32)
        box_index = (item_index % BOXES).astype(jnp.int32)
        corner = (tilt_index, row_offsets[box_index, tilt_index].astype(jnp.int32), col_offsets[box_index, tilt_index].astype(jnp.int32))
        patch_values = lax.dynamic_slice(current, corner, (1, BY, BX))
        return lax.dynamic_update_slice(current, patch_values + windows[tilt_index, box_index][None].astype(jnp.float32), corner)

    canvas = lax.fori_loop(0, TILTS * BOXES, place_item, canvas)
    predicted = canvas[:, :IMG_H].astype(jnp.bfloat16)
    offsets = jnp.arange(-HR, HR + 1, dtype=jnp.float32)
    rho_sq = offsets[:, None] ** 2 + offsets[None, :] ** 2
    spread = point_spread(rho_sq[None], defocus[:, None, None], HR).astype(jnp.bfloat16)
    residual = measured - convolve(predicted, spread)
    back_half = convolve(residual.astype(jnp.bfloat16), spread).astype(jnp.bfloat16)
    extended = jnp.concatenate([back_half, jnp.zeros((TILTS, BY, IMG_W), jnp.bfloat16)], axis=1)

    def cut_tilt(tilt_index, rows_here, columns_here):
        def cut_box(row_start, column_start):
            return lax.dynamic_slice(extended, (tilt_index, row_start.astype(jnp.int32), column_start.astype(jnp.int32)), (1, BY, BX))[0]

        return jax.vmap(cut_box)(rows_here, columns_here)

    back_windows = jax.vmap(cut_tilt)(jnp.arange(TILTS, dtype=jnp.int32), row_offsets.T, col_offsets.T)
    return residual, back_project(back_windows, angles)
```

```python
import functools

import jax
import jax.numpy as jnp
from jax import lax
from jax.experimental import pallas as pl
from jax.experimental.pallas import tpu as pltpu
from jax.sharding import PartitionSpec as P

HR = 8
REACH = 2 * HR
BF = jnp.bfloat16
F32 = jnp.float32
ABSENT = -1024


def ring(block, axis, distance):
    count = lax.axis_size(axis)
    return lax.ppermute(block, axis, [(i, (i + distance) % count) for i in range(count)])


def shift_tables(angles, depth):
    layers = jnp.arange(depth, dtype=F32)
    shifts = (layers[None, :] - (depth - 1) / 2.0) * jnp.sin(angles)[:, None]
    lower = jnp.floor(shifts)

    def weight(offset):
        return jnp.maximum(0.0, 1.0 - jnp.abs(offset - shifts))

    return lower.reshape(-1), weight(lower).reshape(-1), weight(lower + 1.0).reshape(-1)


def iota_apart(shape, plus, minus):
    ahead = lax.broadcasted_iota(jnp.int32, shape, plus)
    behind = lax.broadcasted_iota(jnp.int32, shape, minus)
    return (ahead - behind).astype(F32).astype(BF)


def tap_block(apart, lower, near, far):
    shape = apart.shape
    place = apart - jnp.full(shape, lower, F32).astype(BF)
    near_block = jnp.full(shape, near, F32).astype(BF)
    far_block = jnp.full(shape, far, F32).astype(BF)
    zero = jnp.zeros(shape, BF)
    return jnp.where(place == 0, near_block, jnp.where(place == 1, far_block, zero))


def project_kernel(low_ref, near_ref, far_ref, vol_ref, *refs, depth, tilts, groups):
    outs, (wide, lhs, table, total) = refs[:groups], refs[groups:]
    step = pl.program_id(0)
    me = lax.axis_index("tilt")
    rows, layers, width = vol_ref.shape
    wide[...] = vol_ref[...].reshape(rows * layers, width).astype(F32)
    for z in range(layers):
        lhs[:, z * width : (z + 1) * width] = wide[pl.ds(z, rows, stride=layers), :].astype(BF)

    @pl.when(step == 0)
    def _():
        total[...] = jnp.zeros_like(total)

    apart = iota_apart((width, width), 1, 0)
    for k in range(groups):
        group = lax.rem(me + k, groups)
        buffer = k % 2
        for z in range(layers):
            for t in range(tilts):
                entry = (group * tilts + t) * depth + step * layers + z
                table[buffer, z * width : (z + 1) * width, t * width : (t + 1) * width] = tap_block(
                    apart, low_ref[entry], near_ref[entry], far_ref[entry]
                )
        span = slice(k * tilts * width, (k + 1) * tilts * width)
        total[:, span] += jnp.dot(lhs[...], table[buffer], preferred_element_type=F32)

    @pl.when(step == pl.num_programs(0) - 1)
    def _():
        for k in range(groups):
            for t in range(tilts):
                start = (k * tilts + t) * width
                outs[k][t] = total[:, start : start + width].astype(BF)


def project(volume, tables, tilts, groups):
    rows, depth, width = volume.shape
    layers = min(16, depth)
    scalars = pl.BlockSpec(memory_space=pltpu.SMEM)
    return pl.pallas_call(
        functools.partial(project_kernel, depth=depth, tilts=tilts, groups=groups),
        out_shape=[jax.ShapeDtypeStruct((tilts, rows, width), BF)] * groups,
        grid=(depth // layers,),
        in_specs=[scalars] * 3 + [pl.BlockSpec((rows, layers, width), lambda i: (0, i, 0))],
        out_specs=[pl.BlockSpec((tilts, rows, width), lambda i: (0, 0, 0))] * groups,
        scratch_shapes=[
            pltpu.VMEM((rows * layers, width), F32),
            pltpu.VMEM((rows, layers * width), BF),
            pltpu.VMEM((2, layers * width, tilts * width), BF),
            pltpu.VMEM((rows, groups * tilts * width), F32),
        ],
        name="project",
    )(*tables, volume)


def back_kernel(low_ref, near_ref, far_ref, *refs, depth, tilts, groups, scale):
    windows, out_ref, table = refs[:groups], refs[groups], refs[groups + 1]
    step = pl.program_id(0)
    me = lax.axis_index("tilt")
    rows, layers, width = out_ref.shape
    apart = iota_apart((width, width), 0, 1)
    lhs = jnp.concatenate([windows[k][t] for k in range(groups) for t in range(tilts)], axis=1)
    flat = out_ref.reshape(rows * layers, width)
    for pair in range(layers // 2):
        buffer = pair % 2
        for half in range(2):
            z = 2 * pair + half
            for k in range(groups):
                group = lax.rem(me + groups - k, groups)
                for t in range(tilts):
                    entry = (group * tilts + t) * depth + step * layers + z
                    start = (k * tilts + t) * width
                    table[buffer, start : start + width, half * width : (half + 1) * width] = (
                        tap_block(apart, low_ref[entry], near_ref[entry], far_ref[entry])
                    )
        result = jnp.dot(lhs, table[buffer], preferred_element_type=F32) * scale
        for half in range(2):
            flat[pl.ds(2 * pair + half, rows, stride=layers), :] = result[
                :, half * width : (half + 1) * width
            ]


def back_project(windows, tables, depth, scale):
    groups = len(windows)
    tilts, rows, width = windows[0].shape
    layers = min(8, depth)
    scalars = pl.BlockSpec(memory_space=pltpu.SMEM)
    return pl.pallas_call(
        functools.partial(back_kernel, depth=depth, tilts=tilts, groups=groups, scale=scale),
        out_shape=jax.ShapeDtypeStruct((rows, depth, width), F32),
        grid=(depth // layers,),
        in_specs=[scalars] * 3
        + [pl.BlockSpec((tilts, rows, width), lambda i: (0, 0, 0))] * groups,
        out_specs=pl.BlockSpec((rows, layers, width), lambda i: (0, i, 0)),
        scratch_shapes=[pltpu.VMEM((2, groups * tilts * width, 2 * width), BF)],
        name="back_project",
    )(*tables, *windows)


def rank_items(row_ref, slot_ref, strip_rows, capacity, tile_count):
    boxes, tilts = row_ref.shape
    slots = tile_count * capacity

    def clear(i, carry):
        slot_ref[i] = -1
        return carry

    lax.fori_loop(0, slots, clear, 0)
    for t in range(tilts):
        for b in range(boxes):
            first = lax.div(row_ref[b, t], strip_rows) * capacity
            place = first
            for r in range(capacity - 1):
                taken = slot_ref[first + r] >= 0
                place = jnp.where(taken & (place == first + r), place + 1, place)
            slot_ref[place] = t * boxes + b


def pack_kernel(row_ref, col_ref, *refs, groups, tile_count, strip_rows, capacity):
    slabs, outs, slot_ref = refs[:groups], refs[groups : groups + tile_count], refs[-1]
    boxes, tilts = row_ref.shape
    _, slab_rows, width = slabs[0].shape
    height = slab_rows * groups
    my_tilt, my_tile = lax.axis_index("tilt"), lax.axis_index("tile")
    rank_items(row_ref, slot_ref, strip_rows, capacity, tile_count)

    def item_at(strip, r):
        inside = (strip >= 0) & (strip < tile_count)
        spot = jnp.where(inside, strip, 0) * capacity + r
        return jnp.where(inside, slot_ref[spot], -1)

    def slab_of(k, item, begin, size):
        block = slabs[k][jnp.maximum(item, 0), pl.ds(begin, size), :]
        return jnp.where(item >= 0, block, jnp.zeros_like(block))

    for d in range(tile_count):
        out = outs[d]
        strip = lax.rem(my_tile + d, tile_count)
        metas = []

        def note(item):
            there = jnp.maximum(item, 0)
            t, b = lax.div(there, boxes), lax.rem(there, boxes)
            within = lax.rem(row_ref[b, t], strip_rows) + t * strip_rows
            metas.append(jnp.where(item >= 0, within, ABSENT).astype(F32))
            metas.append(col_ref[b, t].astype(F32))

        for r in range(capacity):
            item = item_at(strip, r)
            note(item)
            for k in range(groups):
                source = lax.rem(my_tilt + groups - k, groups)
                begin = pl.multiple_of(r * height + source * slab_rows, slab_rows)
                out[pl.ds(begin, slab_rows), :] = slab_of(k, item, 0, slab_rows)
        base = capacity * height
        for r in range(capacity):
            item = item_at(strip + 2, r)
            note(item)
            for k in range(groups):
                source = lax.rem(my_tilt + groups - k, groups)

                @pl.when(source == 0)
                def _():
                    out[base + r * REACH : base + (r + 1) * REACH, :] = slab_of(k, item, 0, REACH)

        base += capacity * REACH
        for r in range(capacity):
            item = item_at(strip - 2, r)
            note(item)
            for k in range(groups):
                source = lax.rem(my_tilt + groups - k, groups)

                @pl.when(source == groups - 1)
                def _():
                    out[base + r * REACH : base + (r + 1) * REACH, :] = slab_of(
                        k, item, slab_rows - REACH, REACH
                    )

        base += capacity * REACH
        meta_rows = out.shape[0] - base
        row_at = lax.broadcasted_iota(jnp.int32, (meta_rows, width), 0)
        block = jnp.zeros((meta_rows, width), F32)
        for i, value in enumerate(metas):
            block = jnp.where(row_at == i, value, block)
        out[base:, :] = block.astype(BF)


def pack(slabs, rows, cols, tile_count, strip_rows, capacity):
    groups = len(slabs)
    boxes, tilts = rows.shape
    slabs = [s.reshape(tilts * boxes, -1, s.shape[-1]) for s in slabs]
    slab_rows, width = slabs[0].shape[1:]
    meta_rows = -(-6 * capacity // 16) * 16
    length = capacity * (slab_rows * groups + 2 * REACH) + meta_rows
    return pl.pallas_call(
        functools.partial(
            pack_kernel,
            groups=groups,
            tile_count=tile_count,
            strip_rows=strip_rows,
            capacity=capacity,
        ),
        out_shape=[jax.ShapeDtypeStruct((length, width), BF)] * tile_count,
        in_specs=[pl.BlockSpec(memory_space=pltpu.SMEM)] * 2
        + [pl.BlockSpec(memory_space=pltpu.VMEM)] * groups,
        out_specs=[pl.BlockSpec(memory_space=pltpu.VMEM)] * tile_count,
        scratch_shapes=[pltpu.SMEM((tile_count * capacity,), jnp.int32)],
        name="pack",
    )(rows, cols, *slabs)


def hi_lo(block):
    high = block.astype(BF)
    return high, (block - high.astype(F32)).astype(BF)


def place_kernel(measured_ref, after_ref, *refs, tilts, strip_rows, height, capacity, tile_count):
    parcels = refs[:tile_count]
    canvas_ref, next_ref, prev_ref, placed, onehot = refs[tile_count:]
    length, width = parcels[0].shape
    rows, image_width = canvas_ref.shape[1:]
    column = iota_apart((width, image_width), 1, 0)
    apart = iota_apart((rows, height), 0, 1)
    edge_apart = iota_apart((REACH, REACH), 0, 1)
    base = capacity * height
    meta = base + 2 * capacity * REACH

    def spread_out(parcel, begin, size, q):
        picks = (column == parcel[meta + 2 * q + 1 : meta + 2 * q + 2, :width_in(column)][:, :1]).astype(BF)
        return jnp.dot(parcel[begin : begin + size, :], picks, preferred_element_type=F32).astype(BF)

    def width_in(_):
        return width

    def row_of(parcel, q, t):
        own = parcel[meta + 2 * q : meta + 2 * q + 1, :].astype(F32) - float(t * strip_rows)
        return jnp.where((own >= 0) & (own < strip_rows), own, float(ABSENT))

    index = 0
    for parcel in parcels:
        for r in range(capacity):
            placed[index * height : (index + 1) * height, :] = spread_out(parcel, r * height, height, r)
            for t in range(tilts):
                target = (row_of(parcel, r, t) + float(REACH)).astype(BF)
                onehot[t * rows : (t + 1) * rows, index * height : (index + 1) * height] = (
                    apart == target
                ).astype(BF)
            index += 1
    total = jnp.dot(onehot[...], placed[...], preferred_element_type=F32)
    for t in range(tilts):
        canvas_ref[t] = total[t * rows : (t + 1) * rows]
    for side in range(2):
        blocks = [[] for _ in range(tilts)]
        values = []
        for parcel in parcels:
            for r in range(capacity):
                q = (1 + side) * capacity + r
                begin = base + side * capacity * REACH + r * REACH
                values.append(spread_out(parcel, begin, REACH, q))
                for t in range(tilts):
                    offset = 0.0 if side == 0 else float(height - strip_rows * 2)
                    target = row_of(parcel, q, t)[:, :REACH]
                    if side == 1:
                        target = target + float(height - 2 * strip_rows)
                    blocks[t].append((edge_apart == target.astype(BF)).astype(BF))
        tall = jnp.concatenate(values, axis=0)
        for t in range(tilts):
            picks = jnp.concatenate(blocks[t], axis=1)
            edge = jnp.dot(picks, tall, preferred_element_type=F32)
            begin = rows - REACH if side == 0 else 0
            canvas_ref[t, begin : begin + REACH, :] = edge
    reach = strip_rows + REACH
    for t in range(tilts):
        next_ref[t, :reach, :] = canvas_ref[t, strip_rows : strip_rows + reach, :].astype(BF)
        prev_ref[t, :reach, :] = canvas_ref[t, REACH : REACH + reach, :].astype(BF)
        high, low = hi_lo(measured_ref[t, strip_rows - HR :, :])
        next_ref[t, reach:, :] = jnp.concatenate([high, low], axis=0)
        high, low = hi_lo(after_ref[t, :HR, :])
        prev_ref[t, reach:, :] = jnp.concatenate([high, low], axis=0)


def place(measured, after, parcels, height, capacity):
    tilts, strip_rows, image_width = measured.shape
    tile_count = len(parcels)
    width = parcels[0].shape[1]
    rows = 2 * strip_rows + 2 * REACH
    halo = strip_rows + REACH + 2 * HR
    whole = pl.BlockSpec(memory_space=pltpu.VMEM)
    return pl.pallas_call(
        functools.partial(
            place_kernel,
            tilts=tilts,
            strip_rows=strip_rows,
            height=height,
            capacity=capacity,
            tile_count=tile_count,
        ),
        out_shape=[
            jax.ShapeDtypeStruct((tilts, rows, image_width), F32),
            jax.ShapeDtypeStruct((tilts, halo, image_width), BF),
            jax.ShapeDtypeStruct((tilts, halo, image_width), BF),
        ],
        in_specs=[whole] * (2 + tile_count),
        out_specs=[whole] * 3,
        scratch_shapes=[
            pltpu.VMEM((tile_count * capacity * height, image_width), BF),
            pltpu.VMEM((tilts * rows, tile_count * capacity * height), BF),
        ],
        name="place",
    )(measured, after, *parcels)


def transfer_kernel(defocus_ref, out_ref):
    tilts, _, image_width, _ = out_ref.shape
    lanes = 128
    row = lax.broadcasted_iota(jnp.int32, (8, lanes), 0)
    lane = lax.broadcasted_iota(jnp.int32, (8, lanes), 1)
    down = lax.broadcasted_iota(jnp.int32, (8, lanes), 0)
    for t in range(tilts):
        for i in range(HR + 1):
            rho_sq = (i * i + lane * lane).astype(F32)
            value = jnp.exp(-rho_sq / (2.0 * HR * HR)) * jnp.cos(defocus_ref[t] * rho_sq) / float(HR * HR)
            value = jnp.where(lane <= HR, value, 0.0)
            for begin in range(0, image_width, 16):
                for column in range(0, image_width, lanes):
                    if begin - column > lanes + HR or column - begin > 16 + HR:
                        out_ref[t, i, begin : begin + 16, column : column + lanes] = jnp.zeros(
                            (16, lanes), BF
                        )
                        continue
                    parts = []
                    for half in range(2):
                        apart = jnp.abs(down + (begin + 8 * half - column) - lane)
                        parts.append(
                            jnp.take_along_axis(value, jnp.minimum(apart, lanes - 1), axis=1)
                        )
                    out_ref[t, i, begin : begin + 16, column : column + lanes] = jnp.concatenate(
                        parts, axis=0
                    ).astype(BF)


def transfer_tables(defocus, image_width):
    return pl.pallas_call(
        transfer_kernel,
        out_shape=jax.ShapeDtypeStruct((defocus.shape[0], HR + 1, image_width, image_width), BF),
        in_specs=[pl.BlockSpec(memory_space=pltpu.SMEM)],
        out_specs=pl.BlockSpec(memory_space=pltpu.VMEM),
        name="transfer",
    )(defocus)


def convolve(source, table_ref, t, height):
    total = None
    for i in range(2 * HR + 1):
        part = jnp.dot(
            source[t, i : i + height, :].astype(BF),
            table_ref[t, abs(i - HR)],
            preferred_element_type=F32,
        )
        total = part if total is None else total + part
    return total


def filter_kernel(
    canvas_ref, above_ref, below_ref, measured_ref, after_ref, table_ref, *refs, height, capacity
):
    tile_count = (len(refs) - 4) // 2
    parcels, residual_ref, outs = refs[:tile_count], refs[tile_count], refs[tile_count + 1 : -3]
    predicted, residual, back = refs[-3:]
    tilts, strip_rows, image_width = measured_ref.shape
    rows = canvas_ref.shape[1]
    my_tile = lax.axis_index("tile")
    first = my_tile * strip_rows
    image_rows = tile_count * strip_rows
    reach = strip_rows + REACH

    def inside(count, start):
        at = lax.broadcasted_iota(jnp.int32, (count, image_width), 0) + (first + start)
        return (at >= 0) & (at < image_rows)

    at_top, at_end = my_tile == 0, my_tile == tile_count - 1
    for t in range(tilts):
        upper = jnp.where(at_top, 0.0, above_ref[t, :reach, :].astype(F32))
        lower = jnp.where(at_end, 0.0, below_ref[t, :reach, :].astype(F32))
        field = canvas_ref[t] + jnp.concatenate([upper, lower], axis=0)
        field = jnp.where(inside(rows, -REACH), field, 0.0)
        predicted[t] = field.astype(BF).astype(F32)
        known = jnp.concatenate(
            [
                above_ref[t, reach : reach + HR, :].astype(F32)
                + above_ref[t, reach + HR :, :].astype(F32),
                measured_ref[t],
                after_ref[t],
                below_ref[t, reach : reach + HR, :].astype(F32)
                + below_ref[t, reach + HR :, :].astype(F32),
            ],
            axis=0,
        )
        count = rows - 2 * HR
        rest = known - convolve(predicted, table_ref, t, count)
        residual_ref[t] = rest[HR : HR + strip_rows]
        rest = jnp.where(inside(count, -HR), rest, 0.0)
        residual[t] = rest.astype(BF).astype(F32)
        count -= 2 * HR
        image = convolve(residual, table_ref, t, count)
        back[t * count : (t + 1) * count, :] = jnp.where(inside(count, 0), image, 0.0).astype(BF)
    width = parcels[0].shape[1]
    count = 2 * strip_rows
    apart = iota_apart((height, count), 1, 0)
    column = iota_apart((image_width, width), 0, 1)
    meta = capacity * (height + 2 * REACH)
    for parcel, out in zip(parcels, outs, strict=True):
        for r in range(capacity):
            top = parcel[meta + 2 * r : meta + 2 * r + 1, :].astype(F32)
            picks = []
            for t in range(tilts):
                own = top - float(t * strip_rows)
                own = jnp.where((own >= 0) & (own < strip_rows), own, float(ABSENT)).astype(BF)
                picks.append((apart == own[:, :1]).astype(BF))
            cut = jnp.dot(
                jnp.concatenate(picks, axis=1), back[...], preferred_element_type=F32
            ).astype(BF)
            left = parcel[meta + 2 * r + 1 : meta + 2 * r + 2, :]
            columns = (column == left).astype(BF)
            out[r * height : (r + 1) * height, :] = jnp.dot(
                cut, columns, preferred_element_type=F32
            ).astype(BF)


def filter_and_cut(canvas, above, below, measured, after, table, parcels, height, capacity):
    tilts, strip_rows, image_width = measured.shape
    tile_count = len(parcels)
    width = parcels[0].shape[1]
    rows = canvas.shape[1]
    whole = pl.BlockSpec(memory_space=pltpu.VMEM)
    results = pl.pallas_call(
        functools.partial(filter_kernel, height=height, capacity=capacity),
        out_shape=[jax.ShapeDtypeStruct(measured.shape, F32)]
        + [jax.ShapeDtypeStruct((capacity * height, width), BF)] * tile_count,
        in_specs=[whole] * (6 + tile_count),
        out_specs=[whole] * (1 + tile_count),
        scratch_shapes=[
            pltpu.VMEM((tilts, rows, image_width), F32),
            pltpu.VMEM((tilts, rows - 2 * HR, image_width), F32),
            pltpu.VMEM((tilts * 2 * strip_rows, image_width), BF),
        ],
        name="filter_and_cut",
    )(canvas, above, below, measured, after, table, *parcels)
    return results[0], results[1:]


def unpack_kernel(row_ref, *refs, groups, tile_count, strip_rows, capacity):
    parcels, outs, slot_ref = refs[:tile_count], refs[tile_count : tile_count + groups], refs[-1]
    _, slab_rows, _ = outs[0].shape
    height = slab_rows * groups
    my_tilt, my_tile = lax.axis_index("tilt"), lax.axis_index("tile")
    rank_items(row_ref, slot_ref, strip_rows, capacity, tile_count)
    for d in range(tile_count):
        strip = lax.rem(my_tile + d, tile_count)
        for r in range(capacity):
            item = slot_ref[strip * capacity + r]

            @pl.when(item >= 0)
            def _():
                for k in range(groups):
                    slab = lax.rem(my_tilt + k, groups)
                    begin = pl.multiple_of(r * height + slab * slab_rows, slab_rows)
                    outs[k][item] = parcels[d][pl.ds(begin, slab_rows), :]


def unpack(parcels, rows, slab_rows, groups, strip_rows, capacity):
    boxes, tilts = rows.shape
    tile_count = len(parcels)
    width = parcels[0].shape[1]
    whole = pl.BlockSpec(memory_space=pltpu.VMEM)
    return pl.pallas_call(
        functools.partial(
            unpack_kernel,
            groups=groups,
            tile_count=tile_count,
            strip_rows=strip_rows,
            capacity=capacity,
        ),
        out_shape=[jax.ShapeDtypeStruct((tilts * boxes, slab_rows, width), BF)] * groups,
        in_specs=[pl.BlockSpec(memory_space=pltpu.SMEM)] + [whole] * tile_count,
        out_specs=[whole] * groups,
        scratch_shapes=[pltpu.SMEM((tile_count * capacity,), jnp.int32)],
        name="unpack",
    )(rows, *parcels)


def shards(volumes, angles, defocus, row_offsets, col_offsets, measured):
    boxes, slab_rows, depth, width = volumes.shape
    tilts, strip_rows, image_width = measured.shape
    tile_count, groups = lax.axis_size("tile"), lax.axis_size("tilt")
    height = slab_rows * groups
    capacity = max(2, -(-boxes * tilts // tile_count))
    tables = shift_tables(angles, depth)
    after = ring(measured, "tile", -1)
    kernel = transfer_tables(defocus, image_width)
    slabs = project(volumes.reshape(boxes * slab_rows, depth, width), tables, tilts, groups)
    slabs = [slab if k == 0 else ring(slab, "tilt", k) for k, slab in enumerate(slabs)]
    parcels = pack(slabs, row_offsets, col_offsets, tile_count, strip_rows, capacity)
    parcels = [p if d == 0 else ring(p, "tile", d) for d, p in enumerate(parcels)]
    canvas, onward, backward = place(measured, after, parcels, height, capacity)
    above, below = ring(onward, "tile", 1), ring(backward, "tile", -1)
    residual, cuts = filter_and_cut(
        canvas, above, below, measured, after, kernel, parcels, height, capacity
    )
    cuts = [c if d == 0 else ring(c, "tile", -d) for d, c in enumerate(cuts)]
    windows = unpack(cuts, row_offsets, slab_rows, groups, strip_rows, capacity)
    windows = [
        w.reshape(tilts, boxes * slab_rows, width) if k == 0 else
        ring(w, "tilt", k).reshape(tilts, boxes * slab_rows, width)
        for k, w in enumerate(windows)
    ]
    step = back_project(windows, tables, depth, 1.0 / (tilts * groups))
    return residual, step.reshape(boxes, slab_rows, depth, width)


def solution(mesh):
    in_specs = (
        P("tile", "tilt", None, None),
        P(),
        P("tilt"),
        P("tile", "tilt"),
        P("tile", "tilt"),
        P("tilt", "tile", None),
    )
    out_specs = (P("tilt", "tile", None), P("tile", "tilt", None, None))
    return jax.shard_map(shards, mesh=mesh, in_specs=in_specs, out_specs=out_specs, check_vma=False)
```

```python
import functools

import jax
import jax.numpy as jnp
from jax import lax
from jax.experimental import pallas as pl
from jax.experimental.pallas import tpu as pltpu
from jax.sharding import PartitionSpec as P

HR = 8
REACH = 2 * HR
BF = jnp.bfloat16
F32 = jnp.float32
ABSENT = -1024


def ring(block, axis, distance):
    count = lax.axis_size(axis)
    return lax.ppermute(block, axis, [(i, (i + distance) % count) for i in range(count)])


def shift_tables(angles, depth):
    layers = jnp.arange(depth, dtype=F32)
    shifts = (layers[None, :] - (depth - 1) / 2.0) * jnp.sin(angles)[:, None]
    lower = jnp.floor(shifts)

    def weight(offset):
        return jnp.maximum(0.0, 1.0 - jnp.abs(offset - shifts))

    return lower.reshape(-1), weight(lower).reshape(-1), weight(lower + 1.0).reshape(-1)


def iota_apart(shape, plus, minus):
    ahead = lax.broadcasted_iota(jnp.int32, shape, plus)
    behind = lax.broadcasted_iota(jnp.int32, shape, minus)
    return (ahead - behind).astype(F32).astype(BF)


def tap_block(apart, lower, near, far):
    shape = apart.shape

    def filled(value):
        return jnp.full(shape, value, F32).astype(BF)

    beyond = jnp.where(apart == filled(lower + 1.0), filled(far), jnp.zeros(shape, BF))
    return jnp.where(apart == filled(lower), filled(near), beyond)


def project_kernel(low_ref, near_ref, far_ref, vol_ref, *refs, depth, tilts, groups):
    outs, (wide, lhs, total) = refs[:groups], refs[groups:]
    step = pl.program_id(0)
    me = lax.axis_index("tilt")
    rows, layers, width = vol_ref.shape
    wide[...] = vol_ref[...].reshape(rows * layers, width).astype(F32)
    for z in range(layers):
        lhs[:, z * width : (z + 1) * width] = wide[pl.ds(z, rows, stride=layers), :].astype(BF)

    @pl.when(step == 0)
    def _():
        total[...] = jnp.zeros_like(total)

    apart = iota_apart((width, width), 1, 0)

    def block(k, z, t):
        entry = (lax.rem(me + k, groups) * tilts + t) * depth + step * layers + z
        return tap_block(apart, low_ref[entry], near_ref[entry], far_ref[entry])

    for z in range(0, layers, 2):
        for k in range(groups):
            table = jnp.concatenate(
                [
                    jnp.concatenate([block(k, z + half, t) for t in range(tilts)], axis=1)
                    for half in range(2)
                ],
                axis=0,
            )
            span = slice(k * tilts * width, (k + 1) * tilts * width)
            total[:, span] += jnp.dot(
                lhs[:, z * width : (z + 2) * width], table, preferred_element_type=F32
            )

    @pl.when(step == pl.num_programs(0) - 1)
    def _():
        for k in range(groups):
            for t in range(tilts):
                start = (k * tilts + t) * width
                outs[k][t] = total[:, start : start + width].astype(BF)


def project(volume, tables, tilts, groups):
    rows, depth, width = volume.shape
    layers = min(16, depth)
    scalars = pl.BlockSpec(memory_space=pltpu.SMEM)
    return pl.pallas_call(
        functools.partial(project_kernel, depth=depth, tilts=tilts, groups=groups),
        out_shape=[jax.ShapeDtypeStruct((tilts, rows, width), BF)] * groups,
        grid=(depth // layers,),
        in_specs=[scalars] * 3 + [pl.BlockSpec((rows, layers, width), lambda i: (0, i, 0))],
        out_specs=[pl.BlockSpec((tilts, rows, width), lambda i: (0, 0, 0))] * groups,
        scratch_shapes=[
            pltpu.VMEM((rows * layers, width), F32),
            pltpu.VMEM((rows, layers * width), BF),
            pltpu.VMEM((rows, groups * tilts * width), F32),
        ],
        name="project",
    )(*tables, volume)


def back_kernel(low_ref, near_ref, far_ref, *refs, depth, tilts, groups, scale):
    windows, out_ref, lhs = refs[:groups], refs[groups], refs[groups + 1]
    step = pl.program_id(0)
    me = lax.axis_index("tilt")
    rows, layers, width = out_ref.shape
    apart = iota_apart((width, width), 0, 1)

    @pl.when(step == 0)
    def _():
        for k in range(groups):
            for t in range(tilts):
                start = (k * tilts + t) * width
                lhs[:, start : start + width] = windows[k][t]

    def block(k, t, z):
        entry = (lax.rem(me + groups - k, groups) * tilts + t) * depth + step * layers + z
        return tap_block(apart, low_ref[entry], near_ref[entry], far_ref[entry])

    flat = out_ref.reshape(rows * layers, width)
    for z in range(0, layers, 2):
        table = jnp.concatenate(
            [
                jnp.concatenate([block(k, t, z + half) for half in range(2)], axis=1)
                for k in range(groups)
                for t in range(tilts)
            ],
            axis=0,
        )
        result = jnp.dot(lhs[...], table, preferred_element_type=F32) * scale
        for half in range(2):
            flat[pl.ds(z + half, rows, stride=layers), :] = result[
                :, half * width : (half + 1) * width
            ]


def back_project(windows, tables, depth, scale):
    groups = len(windows)
    tilts, rows, width = windows[0].shape
    layers = min(8, depth)
    scalars = pl.BlockSpec(memory_space=pltpu.SMEM)
    return pl.pallas_call(
        functools.partial(back_kernel, depth=depth, tilts=tilts, groups=groups, scale=scale),
        out_shape=jax.ShapeDtypeStruct((rows, depth, width), F32),
        grid=(depth // layers,),
        in_specs=[scalars] * 3
        + [pl.BlockSpec((tilts, rows, width), lambda i: (0, 0, 0))] * groups,
        out_specs=pl.BlockSpec((rows, layers, width), lambda i: (0, i, 0)),
        scratch_shapes=[pltpu.VMEM((rows, groups * tilts * width), BF)],
        name="back_project",
    )(*tables, *windows)


def rank_items(row_ref, slot_ref, strip_rows, capacity, tile_count):
    boxes, tilts = row_ref.shape
    slots = tile_count * capacity

    def clear(i, carry):
        slot_ref[i] = -1
        return carry

    lax.fori_loop(0, slots, clear, 0)
    for t in range(tilts):
        for b in range(boxes):
            first = lax.div(row_ref[b, t], strip_rows) * capacity
            place = first
            for r in range(capacity - 1):
                taken = slot_ref[first + r] >= 0
                place = jnp.where(taken & (place == first + r), place + 1, place)
            slot_ref[place] = t * boxes + b


def pack_kernel(row_ref, col_ref, *refs, groups, tile_count, strip_rows, capacity):
    slabs, outs, slot_ref = refs[:groups], refs[groups : groups + tile_count], refs[-1]
    boxes, tilts = row_ref.shape
    _, slab_rows, width = slabs[0].shape
    height = slab_rows * groups
    my_tilt, my_tile = lax.axis_index("tilt"), lax.axis_index("tile")
    rank_items(row_ref, slot_ref, strip_rows, capacity, tile_count)

    def item_at(strip, r):
        inside = (strip >= 0) & (strip < tile_count)
        spot = jnp.where(inside, strip, 0) * capacity + r
        return jnp.where(inside, slot_ref[spot], -1)

    def slab_of(k, item, begin, size):
        block = slabs[k][jnp.maximum(item, 0), pl.ds(begin, size), :]
        return jnp.where(item >= 0, block, jnp.zeros_like(block))

    for d in range(tile_count):
        out = outs[d]
        strip = lax.rem(my_tile + d, tile_count)
        metas = []

        def note(item):
            there = jnp.maximum(item, 0)
            t, b = lax.div(there, boxes), lax.rem(there, boxes)
            within = lax.rem(row_ref[b, t], strip_rows) + t * strip_rows
            metas.append(jnp.where(item >= 0, within, ABSENT).astype(F32))
            metas.append(col_ref[b, t].astype(F32))

        for r in range(capacity):
            item = item_at(strip, r)
            note(item)
            for k in range(groups):
                source = lax.rem(my_tilt + groups - k, groups)
                begin = pl.multiple_of(r * height + source * slab_rows, slab_rows)
                out[pl.ds(begin, slab_rows), :] = slab_of(k, item, 0, slab_rows)
        base = capacity * height
        for r in range(capacity):
            item = item_at(strip + 2, r)
            note(item)
            for k in range(groups):
                source = lax.rem(my_tilt + groups - k, groups)

                @pl.when(source == 0)
                def _():
                    out[base + r * REACH : base + (r + 1) * REACH, :] = slab_of(k, item, 0, REACH)

        base += capacity * REACH
        for r in range(capacity):
            item = item_at(strip - 2, r)
            note(item)
            for k in range(groups):
                source = lax.rem(my_tilt + groups - k, groups)

                @pl.when(source == groups - 1)
                def _():
                    out[base + r * REACH : base + (r + 1) * REACH, :] = slab_of(
                        k, item, slab_rows - REACH, REACH
                    )

        base += capacity * REACH
        meta_rows = out.shape[0] - base
        row_at = lax.broadcasted_iota(jnp.int32, (meta_rows, width), 0)
        block = jnp.zeros((meta_rows, width), F32)
        for i, value in enumerate(metas):
            block = jnp.where(row_at == i, value, block)
        out[base:, :] = block.astype(BF)


def pack(slabs, rows, cols, tile_count, strip_rows, capacity):
    groups = len(slabs)
    boxes, tilts = rows.shape
    slabs = [s.reshape(tilts * boxes, -1, s.shape[-1]) for s in slabs]
    slab_rows, width = slabs[0].shape[1:]
    meta_rows = -(-6 * capacity // 16) * 16
    length = capacity * (slab_rows * groups + 2 * REACH) + meta_rows
    return pl.pallas_call(
        functools.partial(
            pack_kernel,
            groups=groups,
            tile_count=tile_count,
            strip_rows=strip_rows,
            capacity=capacity,
        ),
        out_shape=[jax.ShapeDtypeStruct((length, width), BF)] * tile_count,
        in_specs=[pl.BlockSpec(memory_space=pltpu.SMEM)] * 2
        + [pl.BlockSpec(memory_space=pltpu.VMEM)] * groups,
        out_specs=[pl.BlockSpec(memory_space=pltpu.VMEM)] * tile_count,
        scratch_shapes=[pltpu.SMEM((tile_count * capacity,), jnp.int32)],
        name="pack",
    )(rows, cols, *slabs)


def hi_lo(block):
    high = block.astype(BF)
    return high, (block - high.astype(F32)).astype(BF)


def place_kernel(measured_ref, after_ref, *refs, tilts, strip_rows, height, capacity, tile_count):
    parcels = refs[:tile_count]
    canvas_ref, next_ref, prev_ref, placed, onehot = refs[tile_count:]
    length, width = parcels[0].shape
    rows, image_width = canvas_ref.shape[1:]
    column = iota_apart((width, image_width), 1, 0)
    apart = iota_apart((rows, height), 0, 1)
    edge_apart = iota_apart((REACH, REACH), 0, 1)
    base = capacity * height
    meta = base + 2 * capacity * REACH

    def spread_out(parcel, begin, size, q):
        left = parcel[meta + 2 * q + 1 : meta + 2 * q + 2, :1]
        picks = (column == left).astype(BF)
        return jnp.dot(parcel[begin : begin + size, :], picks, preferred_element_type=F32).astype(BF)

    def row_of(parcel, q, t):
        own = parcel[meta + 2 * q : meta + 2 * q + 1, :].astype(F32) - float(t * strip_rows)
        return jnp.where((own >= 0) & (own < strip_rows), own, float(ABSENT))

    index = 0
    for parcel in parcels:
        for r in range(capacity):
            placed[index * height : (index + 1) * height, :] = spread_out(parcel, r * height, height, r)
            for t in range(tilts):
                target = (row_of(parcel, r, t) + float(REACH)).astype(BF)
                onehot[t * rows : (t + 1) * rows, index * height : (index + 1) * height] = (
                    apart == target
                ).astype(BF)
            index += 1
    total = jnp.dot(onehot[...], placed[...], preferred_element_type=F32)
    for t in range(tilts):
        canvas_ref[t] = total[t * rows : (t + 1) * rows]
    for side in range(2):
        blocks = [[] for _ in range(tilts)]
        values = []
        for parcel in parcels:
            for r in range(capacity):
                q = (1 + side) * capacity + r
                begin = base + side * capacity * REACH + r * REACH
                values.append(spread_out(parcel, begin, REACH, q))
                for t in range(tilts):
                    target = row_of(parcel, q, t)[:, :REACH]
                    if side == 1:
                        target = target + float(height - 2 * strip_rows)
                    blocks[t].append((edge_apart == target.astype(BF)).astype(BF))
        tall = jnp.concatenate(values, axis=0)
        for t in range(tilts):
            picks = jnp.concatenate(blocks[t], axis=1)
            edge = jnp.dot(picks, tall, preferred_element_type=F32)
            begin = rows - REACH if side == 0 else 0
            canvas_ref[t, begin : begin + REACH, :] = edge
    reach = strip_rows + REACH
    for t in range(tilts):
        next_ref[t, :reach, :] = canvas_ref[t, strip_rows : strip_rows + reach, :].astype(BF)
        prev_ref[t, :reach, :] = canvas_ref[t, REACH : REACH + reach, :].astype(BF)
        high, low = hi_lo(measured_ref[t, strip_rows - HR :, :])
        next_ref[t, reach:, :] = jnp.concatenate([high, low], axis=0)
        high, low = hi_lo(after_ref[t, :HR, :])
        prev_ref[t, reach:, :] = jnp.concatenate([high, low], axis=0)


def place(measured, after, parcels, height, capacity):
    tilts, strip_rows, image_width = measured.shape
    tile_count = len(parcels)
    width = parcels[0].shape[1]
    rows = 2 * strip_rows + 2 * REACH
    halo = strip_rows + REACH + 2 * HR
    whole = pl.BlockSpec(memory_space=pltpu.VMEM)
    return pl.pallas_call(
        functools.partial(
            place_kernel,
            tilts=tilts,
            strip_rows=strip_rows,
            height=height,
            capacity=capacity,
            tile_count=tile_count,
        ),
        out_shape=[
            jax.ShapeDtypeStruct((tilts, rows, image_width), F32),
            jax.ShapeDtypeStruct((tilts, halo, image_width), BF),
            jax.ShapeDtypeStruct((tilts, halo, image_width), BF),
        ],
        in_specs=[whole] * (2 + tile_count),
        out_specs=[whole] * 3,
        scratch_shapes=[
            pltpu.VMEM((tile_count * capacity * height, image_width), BF),
            pltpu.VMEM((tilts * rows, tile_count * capacity * height), BF),
        ],
        name="place",
    )(measured, after, *parcels)


def transfer_kernel(defocus_ref, out_ref):
    tilts, _, image_width, _ = out_ref.shape
    lanes = 128
    row = lax.broadcasted_iota(jnp.int32, (8, lanes), 0)
    lane = lax.broadcasted_iota(jnp.int32, (8, lanes), 1)
    down = lax.broadcasted_iota(jnp.int32, (8, lanes), 0)
    for t in range(tilts):
        for i in range(HR + 1):
            rho_sq = (i * i + lane * lane).astype(F32)
            value = jnp.exp(-rho_sq / (2.0 * HR * HR)) * jnp.cos(defocus_ref[t] * rho_sq) / float(HR * HR)
            value = jnp.where(lane <= HR, value, 0.0)
            for begin in range(0, image_width, 16):
                for column in range(0, image_width, lanes):
                    if begin - column > lanes + HR or column - begin > 16 + HR:
                        out_ref[t, i, begin : begin + 16, column : column + lanes] = jnp.zeros(
                            (16, lanes), BF
                        )
                        continue
                    parts = []
                    for half in range(2):
                        apart = jnp.abs(down + (begin + 8 * half - column) - lane)
                        parts.append(
                            jnp.take_along_axis(value, jnp.minimum(apart, lanes - 1), axis=1)
                        )
                    out_ref[t, i, begin : begin + 16, column : column + lanes] = jnp.concatenate(
                        parts, axis=0
                    ).astype(BF)


def transfer_tables(defocus, image_width):
    return pl.pallas_call(
        transfer_kernel,
        out_shape=jax.ShapeDtypeStruct((defocus.shape[0], HR + 1, image_width, image_width), BF),
        in_specs=[pl.BlockSpec(memory_space=pltpu.SMEM)],
        out_specs=pl.BlockSpec(memory_space=pltpu.VMEM),
        name="transfer",
    )(defocus)


def convolve(source, parts, table_ref, t, height):
    rows = source.shape[0]
    for i in range(HR + 1):
        parts[i, :rows, :] = jnp.dot(source, table_ref[t, i], preferred_element_type=F32)
    total = parts[0, HR : HR + height, :]
    for i in range(1, HR + 1):
        total = total + (
            parts[i, HR + i : HR + i + height, :] + parts[i, HR - i : HR - i + height, :]
        )
    return total


def filter_kernel(
    canvas_ref, above_ref, below_ref, measured_ref, after_ref, table_ref, *refs, height, capacity
):
    tile_count = (len(refs) - 3) // 2
    parcels, residual_ref, outs = refs[:tile_count], refs[tile_count], refs[tile_count + 1 : -2]
    parts, back = refs[-2:]
    tilts, strip_rows, image_width = measured_ref.shape
    rows = canvas_ref.shape[1]
    my_tile = lax.axis_index("tile")
    first = my_tile * strip_rows
    image_rows = tile_count * strip_rows
    reach = strip_rows + REACH

    def inside(count, start):
        at = lax.broadcasted_iota(jnp.int32, (count, image_width), 0) + (first + start)
        return (at >= 0) & (at < image_rows)

    at_top, at_end = my_tile == 0, my_tile == tile_count - 1
    for t in range(tilts):
        upper = jnp.where(at_top, 0.0, above_ref[t, :reach, :].astype(F32))
        lower = jnp.where(at_end, 0.0, below_ref[t, :reach, :].astype(F32))
        field = canvas_ref[t] + jnp.concatenate([upper, lower], axis=0)
        field = jnp.where(inside(rows, -REACH), field, 0.0)
        known = jnp.concatenate(
            [
                above_ref[t, reach : reach + HR, :].astype(F32)
                + above_ref[t, reach + HR :, :].astype(F32),
                measured_ref[t],
                after_ref[t],
                below_ref[t, reach : reach + HR, :].astype(F32)
                + below_ref[t, reach + HR :, :].astype(F32),
            ],
            axis=0,
        )
        count = rows - 2 * HR
        rest = known - convolve(field.astype(BF), parts, table_ref, t, count)
        residual_ref[t] = rest[HR : HR + strip_rows]
        rest = jnp.where(inside(count, -HR), rest, 0.0)
        count -= 2 * HR
        image = convolve(rest.astype(BF), parts, table_ref, t, count)
        back[t * count : (t + 1) * count, :] = jnp.where(inside(count, 0), image, 0.0).astype(BF)
    width = parcels[0].shape[1]
    count = 2 * strip_rows
    apart = iota_apart((height, count), 1, 0)
    column = iota_apart((image_width, width), 0, 1)
    meta = capacity * (height + 2 * REACH)
    for parcel, out in zip(parcels, outs, strict=True):
        for r in range(capacity):
            top = parcel[meta + 2 * r : meta + 2 * r + 1, :].astype(F32)
            picks = []
            for t in range(tilts):
                own = top - float(t * strip_rows)
                own = jnp.where((own >= 0) & (own < strip_rows), own, float(ABSENT)).astype(BF)
                picks.append((apart == own[:, :1]).astype(BF))
            cut = jnp.dot(
                jnp.concatenate(picks, axis=1), back[...], preferred_element_type=F32
            ).astype(BF)
            left = parcel[meta + 2 * r + 1 : meta + 2 * r + 2, :]
            columns = (column == left).astype(BF)
            out[r * height : (r + 1) * height, :] = jnp.dot(
                cut, columns, preferred_element_type=F32
            ).astype(BF)


def filter_and_cut(canvas, above, below, measured, after, table, parcels, height, capacity):
    tilts, strip_rows, image_width = measured.shape
    tile_count = len(parcels)
    width = parcels[0].shape[1]
    rows = canvas.shape[1]
    whole = pl.BlockSpec(memory_space=pltpu.VMEM)
    results = pl.pallas_call(
        functools.partial(filter_kernel, height=height, capacity=capacity),
        out_shape=[jax.ShapeDtypeStruct(measured.shape, F32)]
        + [jax.ShapeDtypeStruct((capacity * height, width), BF)] * tile_count,
        in_specs=[whole] * (6 + tile_count),
        out_specs=[whole] * (1 + tile_count),
        scratch_shapes=[
            pltpu.VMEM((HR + 1, rows, image_width), F32),
            pltpu.VMEM((tilts * 2 * strip_rows, image_width), BF),
        ],
        name="filter_and_cut",
    )(canvas, above, below, measured, after, table, *parcels)
    return results[0], results[1:]


def unpack_kernel(row_ref, *refs, groups, tile_count, strip_rows, capacity):
    parcels, outs, slot_ref = refs[:tile_count], refs[tile_count : tile_count + groups], refs[-1]
    _, slab_rows, _ = outs[0].shape
    height = slab_rows * groups
    my_tilt, my_tile = lax.axis_index("tilt"), lax.axis_index("tile")
    rank_items(row_ref, slot_ref, strip_rows, capacity, tile_count)
    for d in range(tile_count):
        strip = lax.rem(my_tile + d, tile_count)
        for r in range(capacity):
            item = slot_ref[strip * capacity + r]

            @pl.when(item >= 0)
            def _():
                for k in range(groups):
                    slab = lax.rem(my_tilt + k, groups)
                    begin = pl.multiple_of(r * height + slab * slab_rows, slab_rows)
                    outs[k][item] = parcels[d][pl.ds(begin, slab_rows), :]


def unpack(parcels, rows, slab_rows, groups, strip_rows, capacity):
    boxes, tilts = rows.shape
    tile_count = len(parcels)
    width = parcels[0].shape[1]
    whole = pl.BlockSpec(memory_space=pltpu.VMEM)
    return pl.pallas_call(
        functools.partial(
            unpack_kernel,
            groups=groups,
            tile_count=tile_count,
            strip_rows=strip_rows,
            capacity=capacity,
        ),
        out_shape=[jax.ShapeDtypeStruct((tilts * boxes, slab_rows, width), BF)] * groups,
        in_specs=[pl.BlockSpec(memory_space=pltpu.SMEM)] + [whole] * tile_count,
        out_specs=[whole] * groups,
        scratch_shapes=[pltpu.SMEM((tile_count * capacity,), jnp.int32)],
        name="unpack",
    )(rows, *parcels)


def shards(volumes, angles, defocus, row_offsets, col_offsets, measured):
    boxes, slab_rows, depth, width = volumes.shape
    tilts, strip_rows, image_width = measured.shape
    tile_count, groups = lax.axis_size("tile"), lax.axis_size("tilt")
    height = slab_rows * groups
    capacity = max(2, -(-boxes * tilts // tile_count))
    tables = shift_tables(angles, depth)
    after = ring(measured, "tile", -1)
    kernel = transfer_tables(defocus, image_width)
    slabs = project(volumes.reshape(boxes * slab_rows, depth, width), tables, tilts, groups)
    slabs = [slab if k == 0 else ring(slab, "tilt", k) for k, slab in enumerate(slabs)]
    parcels = pack(slabs, row_offsets, col_offsets, tile_count, strip_rows, capacity)
    parcels = [p if d == 0 else ring(p, "tile", d) for d, p in enumerate(parcels)]
    canvas, onward, backward = place(measured, after, parcels, height, capacity)
    above, below = ring(onward, "tile", 1), ring(backward, "tile", -1)
    residual, cuts = filter_and_cut(
        canvas, above, below, measured, after, kernel, parcels, height, capacity
    )
    cuts = [c if d == 0 else ring(c, "tile", -d) for d, c in enumerate(cuts)]
    windows = unpack(cuts, row_offsets, slab_rows, groups, strip_rows, capacity)
    windows = [
        w.reshape(tilts, boxes * slab_rows, width) if k == 0 else
        ring(w, "tilt", k).reshape(tilts, boxes * slab_rows, width)
        for k, w in enumerate(windows)
    ]
    step = back_project(windows, tables, depth, 1.0 / (tilts * groups))
    return residual, step.reshape(boxes, slab_rows, depth, width)


def solution(mesh):
    in_specs = (
        P("tile", "tilt", None, None),
        P(),
        P("tilt"),
        P("tile", "tilt"),
        P("tile", "tilt"),
        P("tilt", "tile", None),
    )
    out_specs = (P("tilt", "tile", None), P("tile", "tilt", None, None))
    return jax.shard_map(shards, mesh=mesh, in_specs=in_specs, out_specs=out_specs, check_vma=False)
```

```python
import functools

import jax
import jax.numpy as jnp
from jax import lax
from jax.experimental import pallas as pl
from jax.experimental.pallas import tpu as pltpu
from jax.sharding import PartitionSpec as P

HR = 8
REACH = 2 * HR
BF = jnp.bfloat16
F32 = jnp.float32
ABSENT = -1024


def ring(block, axis, distance):
    count = lax.axis_size(axis)
    return lax.ppermute(block, axis, [(i, (i + distance) % count) for i in range(count)])


def near(block):
    return pltpu.with_memory_space_constraint(block, pltpu.VMEM)


def quotient(value, size):
    if size & (size - 1) == 0:
        return lax.shift_right_logical(value, size.bit_length() - 1)
    return lax.div(value, size)


def ones_where(mask):
    return jnp.where(mask, jnp.ones(mask.shape, BF), jnp.zeros(mask.shape, BF))


def shift_tables(angles, depth):
    layers = jnp.arange(depth, dtype=F32)
    shifts = (layers[None, :] - (depth - 1) / 2.0) * jnp.sin(angles)[:, None]
    lower = jnp.floor(shifts)

    def weight(offset):
        return jnp.maximum(0.0, 1.0 - jnp.abs(offset - shifts))

    return lower.reshape(-1), weight(lower).reshape(-1), weight(lower + 1.0).reshape(-1)


def iota_apart(shape, plus, minus):
    ahead = lax.broadcasted_iota(jnp.int32, shape, plus)
    behind = lax.broadcasted_iota(jnp.int32, shape, minus)
    return (ahead - behind).astype(F32).astype(BF)


def tap_block(apart, lower, near, far):
    shape = apart.shape

    def filled(value):
        return jnp.full(shape, value, F32).astype(BF)

    beyond = jnp.where(apart == filled(lower + 1.0), filled(far), jnp.zeros(shape, BF))
    return jnp.where(apart == filled(lower), filled(near), beyond)


def slots_of_items(row_ref, strip_rows, capacity):
    tilts, boxes = row_ref.shape
    strips = [quotient(row_ref[t, b], strip_rows) for t in range(tilts) for b in range(boxes)]
    slots = []
    for n, strip in enumerate(strips):
        place = strip * capacity
        for other in strips[:n]:
            place = place + jnp.where(other == strip, 1, 0)
        slots.append(place)
    return strips, slots


def splat_rows(values, rows, width):
    row_at = lax.broadcasted_iota(jnp.int32, (rows, width), 0)
    block = jnp.zeros((rows, width), F32)
    for i, value in enumerate(values):
        block = jnp.where(row_at == i, value.astype(F32), block)
    return block.astype(BF)


def project_kernel(
    row_ref, low_ref, near_ref, far_ref, vol_ref, *refs, depth, tilts, groups, ks, first, strip_rows, capacity
):
    outs, total = refs[: len(ks)], refs[-1]
    step = pl.program_id(0)
    me = lax.axis_index("tilt")
    if first:
        lhs, wide = refs[len(ks)], refs[len(ks) + 1]
        rows, layers, width = vol_ref.shape
        wide[...] = vol_ref[...].reshape(rows * layers, width).astype(F32)
        for z in range(layers):
            lhs[:, z * width : (z + 1) * width] = wide[pl.ds(z, rows, stride=layers), :].astype(BF)
    else:
        lhs = vol_ref
        rows = lhs.shape[0]
        width = outs[0].shape[1]
        layers = lhs.shape[1] // width

    @pl.when(step == 0)
    def _():
        total[...] = jnp.zeros_like(total)

    apart = iota_apart((width, width), 1, 0)

    def block(k, z, t):
        entry = (lax.rem(me + k, groups) * tilts + t) * depth + step * layers + z
        return tap_block(apart, low_ref[entry], near_ref[entry], far_ref[entry])

    for z in range(0, layers, 2):
        for i, k in enumerate(ks):
            table = jnp.concatenate(
                [
                    jnp.concatenate([block(k, z + half, t) for t in range(tilts)], axis=1)
                    for half in range(2)
                ],
                axis=0,
            )
            span = slice(i * tilts * width, (i + 1) * tilts * width)
            total[:, span] += jnp.dot(
                lhs[:, z * width : (z + 2) * width], table, preferred_element_type=F32
            )

    @pl.when(step == pl.num_programs(0) - 1)
    def _():
        _, slots = slots_of_items(row_ref, strip_rows, capacity)
        meta = splat_rows(slots, outs[0].shape[0] - tilts * rows, width)
        for i in range(len(ks)):
            for t in range(tilts):
                start = (i * tilts + t) * width
                outs[i][t * rows : (t + 1) * rows, :] = total[:, start : start + width].astype(BF)
            outs[i][tilts * rows :, :] = meta


def project(volume, rows_of, tables, tilts, groups, ks, first, width, strip_rows, capacity):
    rows = volume.shape[0]
    depth = tables[0].shape[0] // (tilts * groups)
    layers = min(16, depth)
    length = tilts * rows + -(-tilts * rows_of.shape[1] // 16) * 16
    scalars = pl.BlockSpec(memory_space=pltpu.SMEM)
    flat = pl.BlockSpec((rows, layers * width), lambda i: (0, i))
    source = pl.BlockSpec((rows, layers, width), lambda i: (0, i, 0)) if first else flat
    return pl.pallas_call(
        functools.partial(
            project_kernel,
            depth=depth,
            tilts=tilts,
            groups=groups,
            ks=ks,
            first=first,
            strip_rows=strip_rows,
            capacity=capacity,
        ),
        out_shape=[jax.ShapeDtypeStruct((length, width), BF)] * len(ks)
        + ([jax.ShapeDtypeStruct((rows, depth * width), BF)] if first else []),
        grid=(depth // layers,),
        in_specs=[scalars] * 4 + [source],
        out_specs=[pl.BlockSpec((length, width), lambda i: (0, 0))] * len(ks)
        + ([flat] if first else []),
        scratch_shapes=([pltpu.VMEM((rows * layers, width), F32)] if first else [])
        + [pltpu.VMEM((rows, len(ks) * tilts * width), F32)],
        name="project_first" if first else "project_rest",
    )(rows_of, *tables, volume)


def back_kernel(
    low_ref, near_ref, far_ref, cut_ref, *refs, depth, tilts, boxes, groups, scale
):
    metas, out_ref, lhs = refs[:groups], refs[groups], refs[groups + 1]
    step = pl.program_id(0)
    me = lax.axis_index("tilt")
    rows, layers, width = out_ref.shape
    slab_rows, length = rows // boxes, cut_ref.shape[1]
    apart = iota_apart((width, width), 0, 1)

    @pl.when(step == 0)
    def _():
        ahead = lax.broadcasted_iota(jnp.int32, (slab_rows, length), 1)
        ahead = (ahead - lax.broadcasted_iota(jnp.int32, (slab_rows, length), 0)).astype(F32)
        for k in range(groups):
            group = lax.rem(me + groups - k, groups)
            for t in range(tilts):
                picks = []
                for b in range(boxes):
                    slot = metas[k][t * boxes + b : t * boxes + b + 1, :1].astype(F32)
                    picks.append(ones_where(ahead == slot * float(slab_rows)))
                start = (k * tilts + t) * width
                lhs[:, start : start + width] = jnp.dot(
                    jnp.concatenate(picks, axis=0), cut_ref[group], preferred_element_type=F32
                ).astype(BF)

    def block(k, t, z):
        entry = (lax.rem(me + groups - k, groups) * tilts + t) * depth + step * layers + z
        return tap_block(apart, low_ref[entry], near_ref[entry], far_ref[entry])

    flat = out_ref.reshape(rows * layers, width)
    for z in range(0, layers, 2):
        table = jnp.concatenate(
            [
                jnp.concatenate([block(k, t, z + half) for half in range(2)], axis=1)
                for k in range(groups)
                for t in range(tilts)
            ],
            axis=0,
        )
        result = jnp.dot(lhs[...], table, preferred_element_type=F32) * scale
        for half in range(2):
            flat[pl.ds(z + half, rows, stride=layers), :] = result[
                :, half * width : (half + 1) * width
            ]


def back_project(cuts, slabs, tables, boxes, tilts, rows, scale):
    groups, _, width = cuts.shape
    depth = tables[0].shape[0] // (tilts * groups)
    layers = min(8, depth)
    meta = slabs[0].shape[0] - tilts * rows
    at = tilts * rows // meta
    scalars = pl.BlockSpec(memory_space=pltpu.SMEM)
    return pl.pallas_call(
        functools.partial(
            back_kernel, depth=depth, tilts=tilts, boxes=boxes, groups=groups, scale=scale
        ),
        out_shape=jax.ShapeDtypeStruct((rows, depth, width), F32),
        grid=(depth // layers,),
        in_specs=[scalars] * 3
        + [pl.BlockSpec(cuts.shape, lambda i: (0, 0, 0))]
        + [pl.BlockSpec((meta, width), lambda i: (at, 0))] * groups,
        out_specs=pl.BlockSpec((rows, layers, width), lambda i: (0, i, 0)),
        scratch_shapes=[pltpu.VMEM((rows, groups * tilts * width), BF)],
        name="back_project",
    )(*tables, cuts, *slabs)


def pack_kernel(row_ref, col_ref, *refs, groups, tile_count, strip_rows, capacity, slab_rows):
    slabs, outs = refs[:groups], refs[groups : groups + tile_count]
    item_ref, within_ref, left_ref = refs[groups + tile_count :]
    tilts, boxes = row_ref.shape
    width = slabs[0].shape[1]
    height = slab_rows * groups
    my_tilt, my_tile = lax.axis_index("tilt"), lax.axis_index("tile")
    strips, slots = slots_of_items(row_ref, strip_rows, capacity)
    margin = 2 * capacity

    def clear(i, carry):
        item_ref[i] = -1
        within_ref[i] = ABSENT
        left_ref[i] = 0
        return carry

    lax.fori_loop(0, tile_count * capacity + 2 * margin, clear, 0)
    for n, (strip, slot) in enumerate(zip(strips, slots, strict=True)):
        t, b = n // boxes, n % boxes
        item_ref[slot + margin] = n
        within_ref[slot + margin] = row_ref[t, b] - strip * strip_rows + t * strip_rows
        left_ref[slot + margin] = col_ref[t, b]
    sources = [lax.rem(my_tilt + groups - k, groups) for k in range(groups)]

    def slab_of(k, item, begin, size):
        start = pl.multiple_of(jnp.maximum(item, 0) * slab_rows + begin, 16)
        block = slabs[k][pl.ds(start, size), :]
        return jnp.where(item >= 0, block, jnp.zeros_like(block))

    for d in range(tile_count):
        out = outs[d]
        strip = lax.rem(my_tile + d, tile_count)
        metas = []

        def item_at(offset, r):
            spot = (strip + offset + 2) * capacity + r
            metas.append(within_ref[spot])
            metas.append(left_ref[spot])
            return item_ref[spot]

        for r in range(capacity):
            item = item_at(0, r)
            for k in range(groups):
                begin = pl.multiple_of(r * height + sources[k] * slab_rows, slab_rows)
                out[pl.ds(begin, slab_rows), :] = slab_of(k, item, 0, slab_rows)
        base = capacity * height
        for offset, wanted, begin in ((2, 0, 0), (-2, groups - 1, slab_rows - REACH)):
            for r in range(capacity):
                item = item_at(offset, r)
                block = slab_of(0, item, begin, REACH)
                for k in range(1, groups):
                    block = jnp.where(sources[k] == wanted, slab_of(k, item, begin, REACH), block)
                out[base : base + REACH, :] = block
                base += REACH
        out[base:, :] = splat_rows(metas, out.shape[0] - base, width)


def pack(slabs, rows_of, cols_of, slab_rows, tile_count, strip_rows, capacity):
    groups = len(slabs)
    width = slabs[0].shape[1]
    meta_rows = -(-6 * capacity // 16) * 16
    length = capacity * (slab_rows * groups + 2 * REACH) + meta_rows
    slots = (tile_count + 4) * capacity
    return pl.pallas_call(
        functools.partial(
            pack_kernel,
            groups=groups,
            tile_count=tile_count,
            strip_rows=strip_rows,
            capacity=capacity,
            slab_rows=slab_rows,
        ),
        out_shape=[jax.ShapeDtypeStruct((length, width), BF)] * tile_count,
        in_specs=[pl.BlockSpec(memory_space=pltpu.SMEM)] * 2
        + [pl.BlockSpec(memory_space=pltpu.VMEM)] * groups,
        out_specs=[pl.BlockSpec(memory_space=pltpu.VMEM)] * tile_count,
        scratch_shapes=[pltpu.SMEM((slots,), jnp.int32)] * 3,
        name="pack",
    )(rows_of, cols_of, slabs[0], *[near(slab) for slab in slabs[1:]])


def hi_lo(block):
    high = block.astype(BF)
    return high, (block - high.astype(F32)).astype(BF)


def place_kernel(measured_ref, after_ref, *refs, tilts, strip_rows, height, capacity, tile_count):
    parcels = refs[:tile_count]
    canvas_ref, next_ref, prev_ref, placed, onehot = refs[tile_count:]
    length, width = parcels[0].shape
    rows, image_width = canvas_ref.shape[1:]
    column = iota_apart((width, image_width), 1, 0)
    apart = iota_apart((rows, height), 0, 1)
    edge_apart = iota_apart((REACH, REACH), 0, 1)
    base = capacity * height
    meta = base + 2 * capacity * REACH

    def spread_out(parcel, begin, size, q):
        left = parcel[meta + 2 * q + 1 : meta + 2 * q + 2, :1]
        picks = ones_where(column == left)
        return jnp.dot(parcel[begin : begin + size, :], picks, preferred_element_type=F32).astype(BF)

    def row_of(parcel, q, t):
        own = parcel[meta + 2 * q : meta + 2 * q + 1, :].astype(F32) - float(t * strip_rows)
        return jnp.where((own >= 0) & (own < strip_rows), own, float(ABSENT))

    index = 0
    for parcel in parcels:
        for r in range(capacity):
            placed[index * height : (index + 1) * height, :] = spread_out(parcel, r * height, height, r)
            for t in range(tilts):
                target = (row_of(parcel, r, t) + float(REACH)).astype(BF)
                onehot[t * rows : (t + 1) * rows, index * height : (index + 1) * height] = (
                    ones_where(apart == target)
                )
            index += 1
    total = jnp.dot(onehot[...], placed[...], preferred_element_type=F32)
    for t in range(tilts):
        canvas_ref[t] = total[t * rows : (t + 1) * rows]
    for side in range(2):
        blocks = [[] for _ in range(tilts)]
        values = []
        for parcel in parcels:
            for r in range(capacity):
                q = (1 + side) * capacity + r
                begin = base + side * capacity * REACH + r * REACH
                values.append(spread_out(parcel, begin, REACH, q))
                for t in range(tilts):
                    target = row_of(parcel, q, t)[:, :REACH]
                    if side == 1:
                        target = target + float(height - 2 * strip_rows)
                    blocks[t].append(ones_where(edge_apart == target.astype(BF)))
        tall = jnp.concatenate(values, axis=0)
        for t in range(tilts):
            picks = jnp.concatenate(blocks[t], axis=1)
            edge = jnp.dot(picks, tall, preferred_element_type=F32)
            begin = rows - REACH if side == 0 else 0
            canvas_ref[t, begin : begin + REACH, :] = edge
    reach = strip_rows + REACH
    for t in range(tilts):
        next_ref[t, :reach, :] = canvas_ref[t, strip_rows : strip_rows + reach, :].astype(BF)
        prev_ref[t, :reach, :] = canvas_ref[t, REACH : REACH + reach, :].astype(BF)
        high, low = hi_lo(measured_ref[t, strip_rows - HR :, :])
        next_ref[t, reach:, :] = jnp.concatenate([high, low], axis=0)
        high, low = hi_lo(after_ref[t, :HR, :])
        prev_ref[t, reach:, :] = jnp.concatenate([high, low], axis=0)


def place(measured, after, parcels, height, capacity):
    tilts, strip_rows, image_width = measured.shape
    tile_count = len(parcels)
    width = parcels[0].shape[1]
    rows = 2 * strip_rows + 2 * REACH
    halo = strip_rows + REACH + 2 * HR
    whole = pl.BlockSpec(memory_space=pltpu.VMEM)
    return pl.pallas_call(
        functools.partial(
            place_kernel,
            tilts=tilts,
            strip_rows=strip_rows,
            height=height,
            capacity=capacity,
            tile_count=tile_count,
        ),
        out_shape=[
            jax.ShapeDtypeStruct((tilts, rows, image_width), F32),
            jax.ShapeDtypeStruct((tilts, halo, image_width), BF),
            jax.ShapeDtypeStruct((tilts, halo, image_width), BF),
        ],
        in_specs=[whole] * (2 + tile_count),
        out_specs=[whole] * 3,
        scratch_shapes=[
            pltpu.VMEM((tile_count * capacity * height, image_width), BF),
            pltpu.VMEM((tilts * rows, tile_count * capacity * height), BF),
        ],
        name="place",
    )(measured, near(after), parcels[0], *[near(p) for p in parcels[1:]])


def transfer_kernel(defocus_ref, out_ref):
    tilts, _, image_width, _ = out_ref.shape
    lanes = 128
    row = lax.broadcasted_iota(jnp.int32, (8, lanes), 0)
    lane = lax.broadcasted_iota(jnp.int32, (8, lanes), 1)
    down = lax.broadcasted_iota(jnp.int32, (8, lanes), 0)
    for t in range(tilts):
        for i in range(HR + 1):
            rho_sq = (i * i + lane * lane).astype(F32)
            value = jnp.exp(-rho_sq / (2.0 * HR * HR)) * jnp.cos(defocus_ref[t] * rho_sq) / float(HR * HR)
            value = jnp.where(lane <= HR, value, 0.0)
            for begin in range(0, image_width, 16):
                for column in range(0, image_width, lanes):
                    if begin - column > lanes + HR or column - begin > 16 + HR:
                        out_ref[t, i, begin : begin + 16, column : column + lanes] = jnp.zeros(
                            (16, lanes), BF
                        )
                        continue
                    parts = []
                    for half in range(2):
                        apart = jnp.abs(down + (begin + 8 * half - column) - lane)
                        parts.append(
                            jnp.take_along_axis(value, jnp.minimum(apart, lanes - 1), axis=1)
                        )
                    out_ref[t, i, begin : begin + 16, column : column + lanes] = jnp.concatenate(
                        parts, axis=0
                    ).astype(BF)


def transfer_tables(defocus, image_width):
    return pl.pallas_call(
        transfer_kernel,
        out_shape=jax.ShapeDtypeStruct((defocus.shape[0], HR + 1, image_width, image_width), BF),
        in_specs=[pl.BlockSpec(memory_space=pltpu.SMEM)],
        out_specs=pl.BlockSpec(memory_space=pltpu.VMEM),
        name="transfer",
    )(defocus)


def convolve(source, parts, table_ref, t, height):
    rows = source.shape[0]
    for i in range(HR + 1):
        parts[i, :rows, :] = jnp.dot(source, table_ref[t, i], preferred_element_type=F32)
    total = parts[0, HR : HR + height, :]
    for i in range(1, HR + 1):
        total = total + (
            parts[i, HR + i : HR + i + height, :] + parts[i, HR - i : HR - i + height, :]
        )
    return total


def filter_kernel(
    canvas_ref, above_ref, below_ref, measured_ref, after_ref, table_ref, *refs, height, capacity
):
    tile_count = len(refs) - 4
    parcels, (residual_ref, out_ref, parts, back) = refs[:tile_count], refs[tile_count:]
    groups = out_ref.shape[0]
    slab_rows = height // groups
    tilts, strip_rows, image_width = measured_ref.shape
    rows = canvas_ref.shape[1]
    my_tile = lax.axis_index("tile")
    first = my_tile * strip_rows
    image_rows = tile_count * strip_rows
    reach = strip_rows + REACH

    def inside(count, start):
        at = lax.broadcasted_iota(jnp.int32, (count, image_width), 0) + (first + start)
        return (at >= 0) & (at < image_rows)

    at_top, at_end = my_tile == 0, my_tile == tile_count - 1
    for t in range(tilts):
        upper = jnp.where(at_top, 0.0, above_ref[t, :reach, :].astype(F32))
        lower = jnp.where(at_end, 0.0, below_ref[t, :reach, :].astype(F32))
        field = canvas_ref[t] + jnp.concatenate([upper, lower], axis=0)
        field = jnp.where(inside(rows, -REACH), field, 0.0)
        known = jnp.concatenate(
            [
                above_ref[t, reach : reach + HR, :].astype(F32)
                + above_ref[t, reach + HR :, :].astype(F32),
                measured_ref[t],
                after_ref[t],
                below_ref[t, reach : reach + HR, :].astype(F32)
                + below_ref[t, reach + HR :, :].astype(F32),
            ],
            axis=0,
        )
        count = rows - 2 * HR
        rest = known - convolve(field.astype(BF), parts, table_ref, t, count)
        residual_ref[t] = rest[HR : HR + strip_rows]
        rest = jnp.where(inside(count, -HR), rest, 0.0)
        count -= 2 * HR
        image = convolve(rest.astype(BF), parts, table_ref, t, count)
        back[t * count : (t + 1) * count, :] = jnp.where(inside(count, 0), image, 0.0).astype(BF)
    width = parcels[0].shape[1]
    count = 2 * strip_rows
    apart = iota_apart((height, count), 1, 0)
    column = iota_apart((image_width, width), 0, 1)
    meta = capacity * (height + 2 * REACH)
    for d, parcel in enumerate(parcels):
        sender = lax.rem(my_tile + tile_count - d, tile_count)
        for r in range(capacity):
            top = parcel[meta + 2 * r : meta + 2 * r + 1, :].astype(F32)
            picks = []
            for t in range(tilts):
                own = top - float(t * strip_rows)
                own = jnp.where((own >= 0) & (own < strip_rows), own, float(ABSENT)).astype(BF)
                picks.append(ones_where(apart == own[:, :1]))
            cut = jnp.dot(
                jnp.concatenate(picks, axis=1), back[...], preferred_element_type=F32
            ).astype(BF)
            left = parcel[meta + 2 * r + 1 : meta + 2 * r + 2, :]
            columns = ones_where(column == left)
            window = jnp.dot(cut, columns, preferred_element_type=F32).astype(BF)
            for i in range(groups):
                out_ref[i, sender, r * slab_rows : (r + 1) * slab_rows, :] = window[
                    i * slab_rows : (i + 1) * slab_rows
                ]


def filter_and_cut(canvas, above, below, measured, after, table, parcels, height, capacity, groups):
    tilts, strip_rows, image_width = measured.shape
    tile_count = len(parcels)
    width = parcels[0].shape[1]
    rows = canvas.shape[1]
    whole = pl.BlockSpec(memory_space=pltpu.VMEM)
    slots = (groups, tile_count, capacity * height // groups, width)
    return pl.pallas_call(
        functools.partial(filter_kernel, height=height, capacity=capacity),
        out_shape=[jax.ShapeDtypeStruct(measured.shape, F32), jax.ShapeDtypeStruct(slots, BF)],
        in_specs=[whole] * (6 + tile_count),
        out_specs=[whole] * 2,
        scratch_shapes=[
            pltpu.VMEM((HR + 1, rows, image_width), F32),
            pltpu.VMEM((tilts * 2 * strip_rows, image_width), BF),
        ],
        name="filter_and_cut",
    )(canvas, near(above), near(below), measured, near(after), table, parcels[0], *[near(p) for p in parcels[1:]])


def shards(volumes, angles, defocus, row_offsets, col_offsets, measured):
    boxes, slab_rows, depth, width = volumes.shape
    tilts, strip_rows, image_width = measured.shape
    tile_count, groups = lax.axis_size("tile"), lax.axis_size("tilt")
    height, rows = slab_rows * groups, boxes * slab_rows
    capacity = max(2, -(-boxes * tilts // tile_count))
    assert tilts * strip_rows <= 256 and tile_count * capacity <= 256
    tables = shift_tables(angles, depth)
    rows_of, cols_of = row_offsets.T, col_offsets.T
    after = ring(measured, "tile", -1)
    kernel = transfer_tables(defocus, image_width)
    slabs = [None] * groups
    volume = volumes.reshape(rows, depth, width)
    half = groups // 2 + 1
    early, late = tuple(range(1, half)), (*range(half, groups), 0)
    sizes = (width, strip_rows, capacity)
    *parts, flat = project(volume, rows_of, tables, tilts, groups, early, True, *sizes)
    for k, part in zip(early, parts, strict=True):
        slabs[k] = ring(part, "tilt", k)
    parts = project(flat, rows_of, tables, tilts, groups, late, False, *sizes)
    for k, part in zip(late, parts, strict=True):
        slabs[k] = ring(part, "tilt", k) if k else part
    parcels = pack(slabs, rows_of, cols_of, slab_rows, tile_count, strip_rows, capacity)
    parcels = [p if d == 0 else ring(p, "tile", d) for d, p in enumerate(parcels)]
    canvas, onward, backward = place(measured, after, parcels, height, capacity)
    above, below = ring(onward, "tile", 1), ring(backward, "tile", -1)
    residual, cuts = filter_and_cut(
        canvas, above, below, measured, after, kernel, parcels, height, capacity, groups
    )
    cuts = cuts.reshape(groups * tile_count, capacity * slab_rows, width)
    cuts = lax.all_to_all(cuts, ("tilt", "tile"), split_axis=0, concat_axis=0, tiled=True)
    cuts = cuts.reshape(groups, tile_count * capacity * slab_rows, width)
    step = back_project(cuts, slabs, tables, boxes, tilts, rows, 1.0 / (tilts * groups))
    return residual, step.reshape(boxes, slab_rows, depth, width)


def solution(mesh):
    in_specs = (
        P("tile", "tilt", None, None),
        P(),
        P("tilt"),
        P("tile", "tilt"),
        P("tile", "tilt"),
        P("tilt", "tile", None),
    )
    out_specs = (P("tilt", "tile", None), P("tile", "tilt", None, None))
    return jax.shard_map(shards, mesh=mesh, in_specs=in_specs, out_specs=out_specs, check_vma=False)
```

```python
import functools

import jax
import jax.numpy as jnp
from jax import lax
from jax.experimental import pallas as pl
from jax.experimental.pallas import tpu as pltpu
from jax.sharding import PartitionSpec as P

HR = 8
REACH = 2 * HR
BF = jnp.bfloat16
F32 = jnp.float32
ABSENT = -1024
GRANT = pltpu.CompilerParams(vmem_limit_bytes=32 * 1024 * 1024)


def ring(block, axis, distance):
    count = lax.axis_size(axis)
    return lax.ppermute(block, axis, [(i, (i + distance) % count) for i in range(count)])


def near(block):
    return pltpu.with_memory_space_constraint(block, pltpu.VMEM)


def quotient(value, size):
    if size & (size - 1) == 0:
        return lax.shift_right_logical(value, size.bit_length() - 1)
    return lax.div(value, size)


def ones_where(mask):
    return jnp.where(mask, jnp.ones(mask.shape, BF), jnp.zeros(mask.shape, BF))


def iota_apart(shape, plus, minus):
    ahead = lax.broadcasted_iota(jnp.int32, shape, plus)
    behind = lax.broadcasted_iota(jnp.int32, shape, minus)
    return (ahead - behind).astype(F32).astype(BF)


def note_sines(angle_ref, sine_ref):
    for t in range(sine_ref.shape[0]):
        sine_ref[t] = jnp.sin(jnp.full(sine_ref.shape[1:], angle_ref[t], F32))


def tap_block(apart, sine, layer, depth):
    shift = (layer.astype(F32) - (depth - 1) / 2.0) * sine
    lower = jnp.floor(shift)
    copies = apart.shape[0] // sine.shape[0]

    def filled(value):
        return jnp.concatenate([value.astype(BF)] * copies, axis=0)

    def weight(offset):
        return filled(jnp.maximum(0.0, 1.0 - jnp.abs(offset - shift)))

    beyond = jnp.where(
        apart == filled(lower + 1.0), weight(lower + 1.0), jnp.zeros(apart.shape, BF)
    )
    return jnp.where(apart == filled(lower), weight(lower), beyond)


def slots_of_items(row_ref, strip_rows, capacity):
    tilts, boxes = row_ref.shape
    strips = [quotient(row_ref[t, b], strip_rows) for t in range(tilts) for b in range(boxes)]
    slots = []
    for n, strip in enumerate(strips):
        place = strip * capacity
        for other in strips[:n]:
            place = place + jnp.where(other == strip, 1, 0)
        slots.append(place)
    return strips, slots


def splat_rows(values, rows, width):
    row_at = lax.broadcasted_iota(jnp.int32, (rows, width), 0)
    block = jnp.zeros((rows, width), F32)
    for i, value in enumerate(values):
        block = jnp.where(row_at == i, value.astype(F32), block)
    return block.astype(BF)


def project_kernel(
    row_ref, angle_ref, vol_ref, *refs, depth, tilts, groups, ks, first, strip_rows, capacity
):
    outs, (total, sines) = refs[: len(ks)], refs[-2:]
    step = pl.program_id(0)
    me = lax.axis_index("tilt")
    if first:
        lhs, wide = refs[len(ks)], refs[len(ks) + 1]
        rows, layers, width = vol_ref.shape
        wide[...] = vol_ref[...].reshape(rows * layers, width).astype(F32)
        for z in range(layers):
            lhs[:, z * width : (z + 1) * width] = wide[pl.ds(z, rows, stride=layers), :].astype(BF)
    else:
        lhs = vol_ref
        rows = lhs.shape[0]
        width = outs[0].shape[1]
        layers = lhs.shape[1] // width

    @pl.when(step == 0)
    def _():
        total[...] = jnp.zeros_like(total)
        note_sines(angle_ref, sines)

    apart = iota_apart((width, width), 1, 0)

    def block(k, z, t):
        sine = sines[lax.rem(me + k, groups) * tilts + t]
        return tap_block(apart, sine, step * layers + z, depth)

    for z in range(0, layers, 2):
        for i, k in enumerate(ks):
            table = jnp.concatenate(
                [
                    jnp.concatenate([block(k, z + half, t) for t in range(tilts)], axis=1)
                    for half in range(2)
                ],
                axis=0,
            )
            span = slice(i * tilts * width, (i + 1) * tilts * width)
            total[:, span] += jnp.dot(
                lhs[:, z * width : (z + 2) * width], table, preferred_element_type=F32
            )

    @pl.when(step == pl.num_programs(0) - 1)
    def _():
        _, slots = slots_of_items(row_ref, strip_rows, capacity)
        meta = splat_rows(slots, outs[0].shape[0] - tilts * rows, width)
        for i in range(len(ks)):
            for t in range(tilts):
                start = (i * tilts + t) * width
                outs[i][t * rows : (t + 1) * rows, :] = total[:, start : start + width].astype(BF)
            outs[i][tilts * rows :, :] = meta


def project(volume, rows_of, angles, tilts, groups, ks, first, depth, width, strip_rows, capacity):
    rows = volume.shape[0]
    layers = min(16, depth)
    length = tilts * rows + -(-tilts * rows_of.shape[1] // 16) * 16
    scalars = pl.BlockSpec(memory_space=pltpu.SMEM)
    flat = pl.BlockSpec((rows, layers * width), lambda i: (0, i))
    source = pl.BlockSpec((rows, layers, width), lambda i: (0, i, 0)) if first else flat
    return pl.pallas_call(
        functools.partial(
            project_kernel,
            depth=depth,
            tilts=tilts,
            groups=groups,
            ks=ks,
            first=first,
            strip_rows=strip_rows,
            capacity=capacity,
        ),
        out_shape=[jax.ShapeDtypeStruct((length, width), BF)] * len(ks)
        + ([jax.ShapeDtypeStruct((rows, depth * width), BF)] if first else []),
        grid=(depth // layers,),
        in_specs=[scalars] * 2 + [source],
        out_specs=[pl.BlockSpec((length, width), lambda i: (0, 0))] * len(ks)
        + ([flat] if first else []),
        scratch_shapes=([pltpu.VMEM((rows * layers, width), F32)] if first else [])
        + [
            pltpu.VMEM((rows, len(ks) * tilts * width), F32),
            pltpu.VMEM((groups * tilts, 16, width), F32),
        ],
        compiler_params=GRANT,
        name="project_first" if first else "project_rest",
    )(rows_of, angles, volume)


def back_kernel(
    angle_ref, cut_ref, *refs, depth, tilts, boxes, groups, scale
):
    metas, (out_ref, lhs, sines) = refs[:groups], refs[groups:]
    step = pl.program_id(0)
    me = lax.axis_index("tilt")
    rows, layers, width = out_ref.shape
    slab_rows, length = rows // boxes, cut_ref.shape[1]
    apart = iota_apart((width, width), 0, 1)

    @pl.when(step == 0)
    def _():
        note_sines(angle_ref, sines)
        ahead = lax.broadcasted_iota(jnp.int32, (slab_rows, length), 1)
        ahead = (ahead - lax.broadcasted_iota(jnp.int32, (slab_rows, length), 0)).astype(F32)
        for k in range(groups):
            group = lax.rem(me + groups - k, groups)
            for t in range(tilts):
                picks = []
                for b in range(boxes):
                    slot = metas[k][t * boxes + b : t * boxes + b + 1, :1].astype(F32)
                    picks.append(ones_where(ahead == slot * float(slab_rows)))
                start = (k * tilts + t) * width
                lhs[:, start : start + width] = jnp.dot(
                    jnp.concatenate(picks, axis=0), cut_ref[group], preferred_element_type=F32
                ).astype(BF)

    def block(k, t, z):
        sine = sines[lax.rem(me + groups - k, groups) * tilts + t]
        return tap_block(apart, sine, step * layers + z, depth)

    flat = out_ref.reshape(rows * layers, width)
    for z in range(0, layers, 2):
        table = jnp.concatenate(
            [
                jnp.concatenate([block(k, t, z + half) for half in range(2)], axis=1)
                for k in range(groups)
                for t in range(tilts)
            ],
            axis=0,
        )
        result = jnp.dot(lhs[...], table, preferred_element_type=F32) * scale
        for half in range(2):
            flat[pl.ds(z + half, rows, stride=layers), :] = result[
                :, half * width : (half + 1) * width
            ]


def back_project(cuts, slabs, angles, boxes, tilts, rows, depth, scale):
    groups, _, width = cuts.shape
    layers = min(8, depth)
    meta = slabs[0].shape[0] - tilts * rows
    at = tilts * rows // meta
    scalars = pl.BlockSpec(memory_space=pltpu.SMEM)
    return pl.pallas_call(
        functools.partial(
            back_kernel, depth=depth, tilts=tilts, boxes=boxes, groups=groups, scale=scale
        ),
        out_shape=jax.ShapeDtypeStruct((rows, depth, width), F32),
        grid=(depth // layers,),
        in_specs=[scalars]
        + [pl.BlockSpec(cuts.shape, lambda i: (0, 0, 0))]
        + [pl.BlockSpec((meta, width), lambda i: (at, 0))] * groups,
        out_specs=pl.BlockSpec((rows, layers, width), lambda i: (0, i, 0)),
        scratch_shapes=[
            pltpu.VMEM((rows, groups * tilts * width), BF),
            pltpu.VMEM((groups * tilts, 16, width), F32),
        ],
        compiler_params=GRANT,
        name="back_project",
    )(angles, cuts, *slabs)


def pack_kernel(row_ref, col_ref, *refs, groups, tile_count, strip_rows, capacity, slab_rows):
    slabs, outs = refs[:groups], refs[groups : groups + tile_count]
    item_ref, within_ref, left_ref = refs[groups + tile_count :]
    _, boxes = row_ref.shape
    width = slabs[0].shape[1]
    height = slab_rows * groups
    my_tilt, my_tile = lax.axis_index("tilt"), lax.axis_index("tile")
    strips, slots = slots_of_items(row_ref, strip_rows, capacity)
    margin = 2 * capacity

    def clear(i, carry):
        item_ref[i] = -1
        within_ref[i] = ABSENT
        left_ref[i] = 0
        return carry

    lax.fori_loop(0, tile_count * capacity + 2 * margin, clear, 0)
    for n, (strip, slot) in enumerate(zip(strips, slots, strict=True)):
        t, b = n // boxes, n % boxes
        item_ref[slot + margin] = n
        within_ref[slot + margin] = row_ref[t, b] - strip * strip_rows + t * strip_rows
        left_ref[slot + margin] = col_ref[t, b]
    sources = [lax.rem(my_tilt + groups - k, groups) for k in range(groups)]

    def slab_of(k, item, begin, size):
        start = pl.multiple_of(jnp.maximum(item, 0) * slab_rows + begin, 16)
        block = slabs[k][pl.ds(start, size), :]
        return jnp.where(item >= 0, block, jnp.zeros_like(block))

    for d in range(tile_count):
        out = outs[d]
        strip = lax.rem(my_tile + d, tile_count)
        metas = []

        def item_at(offset, r):
            spot = (strip + offset + 2) * capacity + r
            metas.append(within_ref[spot])
            metas.append(left_ref[spot])
            return item_ref[spot]

        for r in range(capacity):
            item = item_at(0, r)
            for k in range(groups):
                begin = pl.multiple_of(r * height + sources[k] * slab_rows, slab_rows)
                out[pl.ds(begin, slab_rows), :] = slab_of(k, item, 0, slab_rows)
        base = capacity * height
        for offset, wanted, begin in ((2, 0, 0), (-2, groups - 1, slab_rows - REACH)):
            for r in range(capacity):
                item = item_at(offset, r)
                block = slab_of(0, item, begin, REACH)
                for k in range(1, groups):
                    block = jnp.where(sources[k] == wanted, slab_of(k, item, begin, REACH), block)
                out[base : base + REACH, :] = block
                base += REACH
        out[base:, :] = splat_rows(metas, out.shape[0] - base, width)


def pack(slabs, rows_of, cols_of, slab_rows, tile_count, strip_rows, capacity):
    groups = len(slabs)
    width = slabs[0].shape[1]
    meta_rows = -(-6 * capacity // 16) * 16
    length = capacity * (slab_rows * groups + 2 * REACH) + meta_rows
    slots = (tile_count + 4) * capacity
    return pl.pallas_call(
        functools.partial(
            pack_kernel,
            groups=groups,
            tile_count=tile_count,
            strip_rows=strip_rows,
            capacity=capacity,
            slab_rows=slab_rows,
        ),
        out_shape=[jax.ShapeDtypeStruct((length, width), BF)] * tile_count,
        in_specs=[pl.BlockSpec(memory_space=pltpu.SMEM)] * 2
        + [pl.BlockSpec(memory_space=pltpu.VMEM)] * groups,
        out_specs=[pl.BlockSpec(memory_space=pltpu.VMEM)] * tile_count,
        scratch_shapes=[pltpu.SMEM((slots,), jnp.int32)] * 3,
        compiler_params=GRANT,
        name="pack",
    )(rows_of, cols_of, slabs[0], *[near(slab) for slab in slabs[1:]])


def hi_lo(block):
    high = block.astype(BF)
    return high, (block - high.astype(F32)).astype(BF)


def place_kernel(measured_ref, after_ref, *refs, tilts, strip_rows, height, capacity, tile_count):
    parcels = refs[:tile_count]
    canvas_ref, next_ref, prev_ref, placed, onehot = refs[tile_count:]
    _, width = parcels[0].shape
    rows, image_width = canvas_ref.shape[1:]
    column = iota_apart((width, image_width), 1, 0)
    apart = iota_apart((rows, height), 0, 1)
    edge_apart = iota_apart((REACH, REACH), 0, 1)
    base = capacity * height
    meta = base + 2 * capacity * REACH

    def spread_out(parcel, begin, size, q):
        left = parcel[meta + 2 * q + 1 : meta + 2 * q + 2, :1]
        picks = ones_where(column == left)
        return jnp.dot(parcel[begin : begin + size, :], picks, preferred_element_type=F32).astype(BF)

    def row_of(parcel, q, t):
        own = parcel[meta + 2 * q : meta + 2 * q + 1, :].astype(F32) - float(t * strip_rows)
        return jnp.where((own >= 0) & (own < strip_rows), own, float(ABSENT))

    index = 0
    for parcel in parcels:
        for r in range(capacity):
            placed[index * height : (index + 1) * height, :] = spread_out(parcel, r * height, height, r)
            for t in range(tilts):
                target = (row_of(parcel, r, t) + float(REACH)).astype(BF)
                onehot[t * rows : (t + 1) * rows, index * height : (index + 1) * height] = (
                    ones_where(apart == target)
                )
            index += 1
    total = jnp.dot(onehot[...], placed[...], preferred_element_type=F32)
    for t in range(tilts):
        canvas_ref[t] = total[t * rows : (t + 1) * rows]
    for side in range(2):
        blocks = [[] for _ in range(tilts)]
        values = []
        for parcel in parcels:
            for r in range(capacity):
                q = (1 + side) * capacity + r
                begin = base + side * capacity * REACH + r * REACH
                values.append(spread_out(parcel, begin, REACH, q))
                for t in range(tilts):
                    target = row_of(parcel, q, t)[:, :REACH]
                    if side == 1:
                        target = target + float(height - 2 * strip_rows)
                    blocks[t].append(ones_where(edge_apart == target.astype(BF)))
        tall = jnp.concatenate(values, axis=0)
        for t in range(tilts):
            picks = jnp.concatenate(blocks[t], axis=1)
            edge = jnp.dot(picks, tall, preferred_element_type=F32)
            begin = rows - REACH if side == 0 else 0
            canvas_ref[t, begin : begin + REACH, :] = edge
    reach = strip_rows + REACH
    for t in range(tilts):
        next_ref[t, :reach, :] = canvas_ref[t, strip_rows : strip_rows + reach, :].astype(BF)
        prev_ref[t, :reach, :] = canvas_ref[t, REACH : REACH + reach, :].astype(BF)
        high, low = hi_lo(measured_ref[t, strip_rows - HR :, :])
        next_ref[t, reach:, :] = jnp.concatenate([high, low], axis=0)
        high, low = hi_lo(after_ref[t, :HR, :])
        prev_ref[t, reach:, :] = jnp.concatenate([high, low], axis=0)


def place(measured, after, parcels, height, capacity):
    tilts, strip_rows, image_width = measured.shape
    tile_count = len(parcels)
    rows = 2 * strip_rows + 2 * REACH
    halo = strip_rows + REACH + 2 * HR
    whole = pl.BlockSpec(memory_space=pltpu.VMEM)
    return pl.pallas_call(
        functools.partial(
            place_kernel,
            tilts=tilts,
            strip_rows=strip_rows,
            height=height,
            capacity=capacity,
            tile_count=tile_count,
        ),
        out_shape=[
            jax.ShapeDtypeStruct((tilts, rows, image_width), F32),
            jax.ShapeDtypeStruct((tilts, halo, image_width), BF),
            jax.ShapeDtypeStruct((tilts, halo, image_width), BF),
        ],
        in_specs=[whole] * (2 + tile_count),
        out_specs=[whole] * 3,
        scratch_shapes=[
            pltpu.VMEM((tile_count * capacity * height, image_width), BF),
            pltpu.VMEM((tilts * rows, tile_count * capacity * height), BF),
        ],
        compiler_params=GRANT,
        name="place",
    )(measured, near(after), parcels[0], *[near(p) for p in parcels[1:]])


def transfer_kernel(defocus_ref, out_ref):
    tilts, _, image_width, _ = out_ref.shape
    lanes = 128
    row = lax.broadcasted_iota(jnp.int32, (8, lanes), 0)
    lane = lax.broadcasted_iota(jnp.int32, (8, lanes), 1)
    down = lax.broadcasted_iota(jnp.int32, (8, lanes), 0)
    for t in range(tilts):
        for i in range(HR + 1):
            rho_sq = (i * i + lane * lane).astype(F32)
            value = jnp.exp(-rho_sq / (2.0 * HR * HR)) * jnp.cos(defocus_ref[t] * rho_sq) / float(HR * HR)
            value = jnp.where(lane <= HR, value, 0.0)
            for begin in range(0, image_width, 16):
                for column in range(0, image_width, lanes):
                    if begin - column > lanes + HR or column - begin > 16 + HR:
                        out_ref[t, i, begin : begin + 16, column : column + lanes] = jnp.zeros(
                            (16, lanes), BF
                        )
                        continue
                    parts = []
                    for half in range(2):
                        apart = jnp.abs(down + (begin + 8 * half - column) - lane)
                        parts.append(
                            jnp.take_along_axis(value, jnp.minimum(apart, lanes - 1), axis=1)
                        )
                    out_ref[t, i, begin : begin + 16, column : column + lanes] = jnp.concatenate(
                        parts, axis=0
                    ).astype(BF)


def transfer_tables(defocus, image_width):
    return pl.pallas_call(
        transfer_kernel,
        out_shape=jax.ShapeDtypeStruct((defocus.shape[0], HR + 1, image_width, image_width), BF),
        in_specs=[pl.BlockSpec(memory_space=pltpu.SMEM)],
        out_specs=pl.BlockSpec(memory_space=pltpu.VMEM),
        compiler_params=GRANT,
        name="transfer",
    )(defocus)


def convolve(source, parts, table_ref, t, height):
    rows = source.shape[0]
    for i in range(HR + 1):
        parts[i, :rows, :] = jnp.dot(source, table_ref[t, i], preferred_element_type=F32)
    total = parts[0, HR : HR + height, :]
    for i in range(1, HR + 1):
        total = total + (
            parts[i, HR + i : HR + i + height, :] + parts[i, HR - i : HR - i + height, :]
        )
    return total


def filter_kernel(
    canvas_ref, above_ref, below_ref, measured_ref, after_ref, table_ref, *refs, height, capacity
):
    tile_count = len(refs) - 4
    parcels, (residual_ref, out_ref, parts, back) = refs[:tile_count], refs[tile_count:]
    groups = out_ref.shape[0]
    slab_rows = height // groups
    tilts, strip_rows, image_width = measured_ref.shape
    rows = canvas_ref.shape[1]
    my_tile = lax.axis_index("tile")
    first = my_tile * strip_rows
    image_rows = tile_count * strip_rows
    reach = strip_rows + REACH

    def inside(count, start):
        at = lax.broadcasted_iota(jnp.int32, (count, image_width), 0) + (first + start)
        return (at >= 0) & (at < image_rows)

    at_top, at_end = my_tile == 0, my_tile == tile_count - 1
    for t in range(tilts):
        upper = jnp.where(at_top, 0.0, above_ref[t, :reach, :].astype(F32))
        lower = jnp.where(at_end, 0.0, below_ref[t, :reach, :].astype(F32))
        field = canvas_ref[t] + jnp.concatenate([upper, lower], axis=0)
        field = jnp.where(inside(rows, -REACH), field, 0.0)
        known = jnp.concatenate(
            [
                above_ref[t, reach : reach + HR, :].astype(F32)
                + above_ref[t, reach + HR :, :].astype(F32),
                measured_ref[t],
                after_ref[t],
                below_ref[t, reach : reach + HR, :].astype(F32)
                + below_ref[t, reach + HR :, :].astype(F32),
            ],
            axis=0,
        )
        count = rows - 2 * HR
        rest = known - convolve(field.astype(BF), parts, table_ref, t, count)
        residual_ref[t] = rest[HR : HR + strip_rows]
        rest = jnp.where(inside(count, -HR), rest, 0.0)
        count -= 2 * HR
        image = convolve(rest.astype(BF), parts, table_ref, t, count)
        back[t * count : (t + 1) * count, :] = jnp.where(inside(count, 0), image, 0.0).astype(BF)
    width = parcels[0].shape[1]
    count = 2 * strip_rows
    apart = iota_apart((height, count), 1, 0)
    column = iota_apart((image_width, width), 0, 1)
    meta = capacity * (height + 2 * REACH)
    for d, parcel in enumerate(parcels):
        sender = lax.rem(my_tile + tile_count - d, tile_count)
        for r in range(capacity):
            top = parcel[meta + 2 * r : meta + 2 * r + 1, :].astype(F32)
            picks = []
            for t in range(tilts):
                own = top - float(t * strip_rows)
                own = jnp.where((own >= 0) & (own < strip_rows), own, float(ABSENT)).astype(BF)
                picks.append(ones_where(apart == own[:, :1]))
            cut = jnp.dot(
                jnp.concatenate(picks, axis=1), back[...], preferred_element_type=F32
            ).astype(BF)
            left = parcel[meta + 2 * r + 1 : meta + 2 * r + 2, :]
            columns = ones_where(column == left)
            window = jnp.dot(cut, columns, preferred_element_type=F32).astype(BF)
            for i in range(groups):
                out_ref[i, sender, r * slab_rows : (r + 1) * slab_rows, :] = window[
                    i * slab_rows : (i + 1) * slab_rows
                ]


def filter_and_cut(canvas, above, below, measured, after, table, parcels, height, capacity, groups):
    tilts, strip_rows, image_width = measured.shape
    tile_count = len(parcels)
    width = parcels[0].shape[1]
    rows = canvas.shape[1]
    whole = pl.BlockSpec(memory_space=pltpu.VMEM)
    slots = (groups, tile_count, capacity * height // groups, width)
    return pl.pallas_call(
        functools.partial(filter_kernel, height=height, capacity=capacity),
        out_shape=[jax.ShapeDtypeStruct(measured.shape, F32), jax.ShapeDtypeStruct(slots, BF)],
        in_specs=[whole] * (6 + tile_count),
        out_specs=[whole] * 2,
        scratch_shapes=[
            pltpu.VMEM((HR + 1, rows, image_width), F32),
            pltpu.VMEM((tilts * 2 * strip_rows, image_width), BF),
        ],
        compiler_params=GRANT,
        name="filter_and_cut",
    )(near(canvas), near(above), near(below), measured, near(after), near(table), parcels[0], *[near(p) for p in parcels[1:]])


def shards(volumes, angles, defocus, row_offsets, col_offsets, measured):
    boxes, slab_rows, depth, width = volumes.shape
    tilts, strip_rows, image_width = measured.shape
    tile_count, groups = lax.axis_size("tile"), lax.axis_size("tilt")
    height, rows = slab_rows * groups, boxes * slab_rows
    capacity = max(2, -(-boxes * tilts // tile_count))
    assert tilts * strip_rows <= 256 and tile_count * capacity <= 256
    rows_of, cols_of = row_offsets.T, col_offsets.T
    after = ring(measured, "tile", -1)
    kernel = transfer_tables(defocus, image_width)
    slabs = [None] * groups
    volume = volumes.reshape(rows, depth, width)
    half = groups // 2 + 1
    early, late = tuple(range(1, half)), (*range(half, groups), 0)
    sizes = (depth, width, strip_rows, capacity)
    *parts, flat = project(volume, rows_of, angles, tilts, groups, early, True, *sizes)
    for k, part in zip(early, parts, strict=True):
        slabs[k] = ring(part, "tilt", k)
    parts = project(flat, rows_of, angles, tilts, groups, late, False, *sizes)
    for k, part in zip(late, parts, strict=True):
        slabs[k] = ring(part, "tilt", k) if k else part
    parcels = pack(slabs, rows_of, cols_of, slab_rows, tile_count, strip_rows, capacity)
    parcels = [p if d == 0 else ring(p, "tile", d) for d, p in enumerate(parcels)]
    canvas, onward, backward = place(measured, after, parcels, height, capacity)
    above, below = ring(onward, "tile", 1), ring(backward, "tile", -1)
    residual, cuts = filter_and_cut(
        canvas, above, below, measured, after, kernel, parcels, height, capacity, groups
    )
    cuts = cuts.reshape(groups * tile_count, capacity * slab_rows, width)
    cuts = lax.all_to_all(cuts, ("tilt", "tile"), split_axis=0, concat_axis=0, tiled=True)
    cuts = cuts.reshape(groups, tile_count * capacity * slab_rows, width)
    step = back_project(cuts, slabs, angles, boxes, tilts, rows, depth, 1.0 / (tilts * groups))
    return residual, step.reshape(boxes, slab_rows, depth, width)


def solution(mesh):
    in_specs = (
        P("tile", "tilt", None, None),
        P(),
        P("tilt"),
        P("tile", "tilt"),
        P("tile", "tilt"),
        P("tilt", "tile", None),
    )
    out_specs = (P("tilt", "tile", None), P("tile", "tilt", None, None))

    return jax.shard_map(shards, mesh=mesh, in_specs=in_specs, out_specs=out_specs, check_vma=False)
```

```python
import functools

import jax
import jax.numpy as jnp
from jax import lax
from jax.experimental import pallas as pl
from jax.experimental.pallas import tpu as pltpu
from jax.sharding import PartitionSpec as P

HR = 8
REACH = 2 * HR
BF = jnp.bfloat16
F32 = jnp.float32
ABSENT = -1024
GRANT = pltpu.CompilerParams(vmem_limit_bytes=32 * 1024 * 1024)


def ring(block, axis, distance):
    count = lax.axis_size(axis)
    return lax.ppermute(block, axis, [(i, (i + distance) % count) for i in range(count)])


def swap(block, axis, distance):
    count = lax.axis_size(axis)
    assert count & (count - 1) == 0
    return lax.ppermute(block, axis, [(i, i ^ distance) for i in range(count)])


def far(block):
    return pltpu.with_memory_space_constraint(block, pltpu.HBM)


def near(block):
    return pltpu.with_memory_space_constraint(block, pltpu.VMEM)


def quotient(value, size):
    if size & (size - 1) == 0:
        return lax.shift_right_logical(value, size.bit_length() - 1)
    return lax.div(value, size)


def ones_where(mask):
    return jnp.where(mask, jnp.ones(mask.shape, BF), jnp.zeros(mask.shape, BF))


def iota_apart(shape, plus, minus):
    ahead = lax.broadcasted_iota(jnp.int32, shape, plus)
    behind = lax.broadcasted_iota(jnp.int32, shape, minus)
    return (ahead - behind).astype(F32).astype(BF)


def note_sines(angle_ref, sine_ref):
    for t in range(sine_ref.shape[0]):
        sine_ref[t] = jnp.sin(jnp.full(sine_ref.shape[1:], angle_ref[t], F32))


def tap_block(apart, sine, layer, depth):
    shift = (layer.astype(F32) - (depth - 1) / 2.0) * sine
    lower = jnp.floor(shift)
    copies = apart.shape[0] // (2 * sine.shape[0])

    def filled(value):
        return jnp.concatenate([jnp.concatenate([value] * 2, axis=0).astype(BF)] * copies, axis=0)

    def weight(offset):
        return filled(jnp.maximum(0.0, 1.0 - jnp.abs(offset - shift)))

    beyond = jnp.where(
        apart == filled(lower + 1.0), weight(lower + 1.0), jnp.zeros(apart.shape, BF)
    )
    return jnp.where(apart == filled(lower), weight(lower), beyond)


def slots_of_items(row_ref, strip_rows, capacity):
    tilts, boxes = row_ref.shape
    strips = [quotient(row_ref[t, b], strip_rows) for t in range(tilts) for b in range(boxes)]
    slots = []
    for n, strip in enumerate(strips):
        place = strip * capacity
        for other in strips[:n]:
            place = place + jnp.where(other == strip, 1, 0)
        slots.append(place)
    return strips, slots


def splat_rows(values, rows, width):
    row_at = lax.broadcasted_iota(jnp.int32, (rows, width), 0)
    block = jnp.zeros((rows, width), F32)
    for i, value in enumerate(values):
        block = jnp.where(row_at == i, value.astype(F32), block)
    return block.astype(BF)


def project_kernel(
    row_ref, angle_ref, vol_ref, *refs, depth, tilts, groups, ks, first, strip_rows, capacity
):
    outs, (total, sines) = refs[: len(ks)], refs[-2:]
    step = pl.program_id(0)
    me = lax.axis_index("tilt")
    if first:
        lhs, wide = refs[len(ks)], refs[len(ks) + 1]
        rows, layers, width = vol_ref.shape
        wide[...] = vol_ref[...].reshape(rows * layers, width).astype(F32)

        def pair_at(z):
            pair = [wide[pl.ds(z + h, rows, stride=layers), :].astype(BF) for h in range(2)]
            pair = jnp.concatenate(pair, axis=1)
            lhs[:, z * width : (z + 2) * width] = pair
            return pair
    else:
        lhs = vol_ref
        rows = lhs.shape[0]
        width = outs[0].shape[1]
        layers = lhs.shape[1] // width

        def pair_at(z):
            return lhs[:, z * width : (z + 2) * width]

    @pl.when(step == 0)
    def _():
        total[...] = jnp.zeros_like(total)
        note_sines(angle_ref, sines)

    apart = iota_apart((width, width), 1, 0)

    def block(k, z, t):
        sine = sines[(me ^ k) * tilts + t]
        return tap_block(apart, sine, step * layers + z, depth)

    following = pair_at(0)
    for z in range(0, layers, 2):
        pair = following
        if z + 2 < layers:
            following = pair_at(z + 2)
        for i, k in enumerate(ks):
            table = jnp.concatenate(
                [
                    jnp.concatenate([block(k, z + half, t) for t in range(tilts)], axis=1)
                    for half in range(2)
                ],
                axis=0,
            )
            span = slice(i * tilts * width, (i + 1) * tilts * width)
            total[:, span] += jnp.dot(pair, table, preferred_element_type=F32)

    @pl.when(step == pl.num_programs(0) - 1)
    def _():
        _, slots = slots_of_items(row_ref, strip_rows, capacity)
        meta = splat_rows(slots, outs[0].shape[0] - tilts * rows, width)
        for i in range(len(ks)):
            for t in range(tilts):
                start = (i * tilts + t) * width
                outs[i][t * rows : (t + 1) * rows, :] = total[:, start : start + width].astype(BF)
            outs[i][tilts * rows :, :] = meta


def project(volume, rows_of, angles, tilts, groups, ks, first, depth, width, strip_rows, capacity):
    rows = volume.shape[0]
    layers = min(16, depth)
    length = tilts * rows + -(-tilts * rows_of.shape[1] // 16) * 16
    scalars = pl.BlockSpec(memory_space=pltpu.SMEM)
    flat = pl.BlockSpec((rows, layers * width), lambda i: (0, i))
    source = pl.BlockSpec((rows, layers, width), lambda i: (0, i, 0)) if first else flat
    return pl.pallas_call(
        functools.partial(
            project_kernel,
            depth=depth,
            tilts=tilts,
            groups=groups,
            ks=ks,
            first=first,
            strip_rows=strip_rows,
            capacity=capacity,
        ),
        out_shape=[jax.ShapeDtypeStruct((length, width), BF)] * len(ks)
        + ([jax.ShapeDtypeStruct((rows, depth * width), BF)] if first else []),
        grid=(depth // layers,),
        in_specs=[scalars] * 2 + [source],
        out_specs=[pl.BlockSpec((length, width), lambda i: (0, 0))] * len(ks)
        + ([flat] if first else []),
        scratch_shapes=([pltpu.VMEM((rows * layers, width), F32)] if first else [])
        + [
            pltpu.VMEM((rows, len(ks) * tilts * width), F32),
            pltpu.VMEM((groups * tilts, 8, width), F32),
        ],
        compiler_params=GRANT,
        name="project_first" if first else "project_rest",
    )(rows_of, angles, volume)


def back_kernel(
    angle_ref, cut_ref, *refs, depth, tilts, boxes, groups, scale
):
    metas, (out_ref, lhs, sines) = refs[:groups], refs[groups:]
    step = pl.program_id(0)
    me = lax.axis_index("tilt")
    rows, layers, width = out_ref.shape
    slab_rows, length = rows // boxes, cut_ref.shape[1]
    apart = iota_apart((width, width), 0, 1)

    @pl.when(step == 0)
    def _():
        note_sines(angle_ref, sines)
        ahead = lax.broadcasted_iota(jnp.int32, (slab_rows, length), 1)
        ahead = (ahead - lax.broadcasted_iota(jnp.int32, (slab_rows, length), 0)).astype(F32)
        for k in range(groups):
            group = (me ^ k)
            for t in range(tilts):
                picks = []
                for b in range(boxes):
                    slot = metas[k][t * boxes + b : t * boxes + b + 1, :1].astype(F32)
                    picks.append(ones_where(ahead == slot * float(slab_rows)))
                start = (k * tilts + t) * width
                lhs[:, start : start + width] = jnp.dot(
                    jnp.concatenate(picks, axis=0), cut_ref[group], preferred_element_type=F32
                ).astype(BF)

    def block(k, t, z):
        sine = sines[(me ^ k) * tilts + t]
        return tap_block(apart, sine, step * layers + z, depth)

    flat = out_ref.reshape(rows * layers, width)
    for z in range(0, layers, 2):
        table = jnp.concatenate(
            [
                jnp.concatenate([block(k, t, z + half) for half in range(2)], axis=1)
                for k in range(groups)
                for t in range(tilts)
            ],
            axis=0,
        )
        result = jnp.dot(lhs[...], table, preferred_element_type=F32) * scale
        for half in range(2):
            flat[pl.ds(z + half, rows, stride=layers), :] = result[
                :, half * width : (half + 1) * width
            ]


def back_project(cuts, slabs, angles, boxes, tilts, rows, depth, scale):
    groups, _, width = cuts.shape
    layers = min(8, depth)
    meta = slabs[0].shape[0] - tilts * rows
    at = tilts * rows // meta
    scalars = pl.BlockSpec(memory_space=pltpu.SMEM)
    return pl.pallas_call(
        functools.partial(
            back_kernel, depth=depth, tilts=tilts, boxes=boxes, groups=groups, scale=scale
        ),
        out_shape=jax.ShapeDtypeStruct((rows, depth, width), F32),
        grid=(depth // layers,),
        in_specs=[scalars]
        + [pl.BlockSpec(cuts.shape, lambda i: (0, 0, 0))]
        + [pl.BlockSpec((meta, width), lambda i: (at, 0))] * groups,
        out_specs=pl.BlockSpec((rows, layers, width), lambda i: (0, i, 0)),
        scratch_shapes=[
            pltpu.VMEM((rows, groups * tilts * width), BF),
            pltpu.VMEM((groups * tilts, 8, width), F32),
        ],
        compiler_params=GRANT,
        name="back_project",
    )(angles, cuts, *slabs)


def pack_kernel(row_ref, col_ref, *refs, groups, tile_count, strip_rows, capacity, slab_rows):
    slabs, outs = refs[:groups], refs[groups : groups + tile_count]
    item_ref, within_ref, left_ref = refs[groups + tile_count :]
    _, boxes = row_ref.shape
    width = slabs[0].shape[1]
    height = slab_rows * groups
    my_tilt, my_tile = lax.axis_index("tilt"), lax.axis_index("tile")
    strips, slots = slots_of_items(row_ref, strip_rows, capacity)
    margin = 2 * capacity

    def clear(i, carry):
        item_ref[i] = -1
        within_ref[i] = ABSENT
        left_ref[i] = 0
        return carry

    lax.fori_loop(0, tile_count * capacity + 2 * margin, clear, 0)
    for n, (strip, slot) in enumerate(zip(strips, slots, strict=True)):
        t, b = n // boxes, n % boxes
        item_ref[slot + margin] = n
        within_ref[slot + margin] = row_ref[t, b] - strip * strip_rows + t * strip_rows
        left_ref[slot + margin] = col_ref[t, b]
    sources = [my_tilt ^ k for k in range(groups)]

    def slab_of(k, item, begin, size):
        start = pl.multiple_of(jnp.maximum(item, 0) * slab_rows + begin, 16)
        block = slabs[k][pl.ds(start, size), :]
        return jnp.where(item >= 0, block, jnp.zeros_like(block))

    for d in range(tile_count):
        out = outs[d]
        strip = my_tile ^ d
        metas = []

        def item_at(offset, r):
            spot = (strip + offset + 2) * capacity + r
            metas.append(within_ref[spot])
            metas.append(left_ref[spot])
            return item_ref[spot]

        for r in range(capacity):
            item = item_at(0, r)
            for k in range(groups):
                begin = pl.multiple_of(r * height + sources[k] * slab_rows, slab_rows)
                out[pl.ds(begin, slab_rows), :] = slab_of(k, item, 0, slab_rows)
        base = capacity * height
        for offset, wanted, begin in ((2, 0, 0), (-2, groups - 1, slab_rows - REACH)):
            for r in range(capacity):
                item = item_at(offset, r)
                block = slab_of(0, item, begin, REACH)
                for k in range(1, groups):
                    block = jnp.where(sources[k] == wanted, slab_of(k, item, begin, REACH), block)
                out[base : base + REACH, :] = block
                base += REACH
        out[base:, :] = splat_rows(metas, out.shape[0] - base, width)


def pack(slabs, rows_of, cols_of, slab_rows, tile_count, strip_rows, capacity):
    groups = len(slabs)
    width = slabs[0].shape[1]
    meta_rows = -(-6 * capacity // 16) * 16
    length = capacity * (slab_rows * groups + 2 * REACH) + meta_rows
    slots = (tile_count + 4) * capacity
    return pl.pallas_call(
        functools.partial(
            pack_kernel,
            groups=groups,
            tile_count=tile_count,
            strip_rows=strip_rows,
            capacity=capacity,
            slab_rows=slab_rows,
        ),
        out_shape=[jax.ShapeDtypeStruct((length, width), BF)] * tile_count,
        in_specs=[pl.BlockSpec(memory_space=pltpu.SMEM)] * 2
        + [pl.BlockSpec(memory_space=pltpu.VMEM)] * groups,
        out_specs=[pl.BlockSpec(memory_space=pltpu.VMEM)] * tile_count,
        scratch_shapes=[pltpu.SMEM((slots,), jnp.int32)] * 3,
        compiler_params=GRANT,
        name="pack",
    )(rows_of, cols_of, slabs[0], *[near(slab) for slab in slabs[1:]])


def hi_lo(block):
    high = block.astype(BF)
    return high, (block - high.astype(F32)).astype(BF)


def place_kernel(measured_ref, after_ref, *refs, tilts, strip_rows, height, capacity, tile_count):
    parcels = refs[:tile_count]
    canvas_ref, next_ref, prev_ref, placed, onehot = refs[tile_count:]
    _, width = parcels[0].shape
    rows, image_width = canvas_ref.shape[1:]
    column = iota_apart((width, image_width), 1, 0)
    apart = iota_apart((rows, height), 0, 1)
    edge_apart = iota_apart((REACH, REACH), 0, 1)
    base = capacity * height
    meta = base + 2 * capacity * REACH

    def spread_out(parcel, begin, size, q):
        left = parcel[meta + 2 * q + 1 : meta + 2 * q + 2, :1]
        picks = ones_where(column == left)
        return jnp.dot(parcel[begin : begin + size, :], picks, preferred_element_type=F32).astype(BF)

    def row_of(parcel, q, t):
        own = parcel[meta + 2 * q : meta + 2 * q + 1, :].astype(F32) - float(t * strip_rows)
        return jnp.where((own >= 0) & (own < strip_rows), own, float(ABSENT))

    index = 0
    for parcel in parcels:
        for r in range(capacity):
            placed[index * height : (index + 1) * height, :] = spread_out(parcel, r * height, height, r)
            for t in range(tilts):
                target = (row_of(parcel, r, t) + float(REACH)).astype(BF)
                onehot[t * rows : (t + 1) * rows, index * height : (index + 1) * height] = (
                    ones_where(apart == target)
                )
            index += 1
    total = jnp.dot(onehot[...], placed[...], preferred_element_type=F32)
    for t in range(tilts):
        canvas_ref[t] = total[t * rows : (t + 1) * rows]
    for side in range(2):
        blocks = [[] for _ in range(tilts)]
        values = []
        for parcel in parcels:
            for r in range(capacity):
                q = (1 + side) * capacity + r
                begin = base + side * capacity * REACH + r * REACH
                values.append(spread_out(parcel, begin, REACH, q))
                for t in range(tilts):
                    target = row_of(parcel, q, t)[:, :REACH]
                    if side == 1:
                        target = target + float(height - 2 * strip_rows)
                    blocks[t].append(ones_where(edge_apart == target.astype(BF)))
        tall = jnp.concatenate(values, axis=0)
        for t in range(tilts):
            picks = jnp.concatenate(blocks[t], axis=1)
            edge = jnp.dot(picks, tall, preferred_element_type=F32)
            begin = rows - REACH if side == 0 else 0
            canvas_ref[t, begin : begin + REACH, :] = edge
    reach = strip_rows + REACH
    for t in range(tilts):
        next_ref[t, :reach, :] = canvas_ref[t, strip_rows : strip_rows + reach, :].astype(BF)
        prev_ref[t, :reach, :] = canvas_ref[t, REACH : REACH + reach, :].astype(BF)
        high, low = hi_lo(measured_ref[t, strip_rows - HR :, :])
        next_ref[t, reach:, :] = jnp.concatenate([high, low], axis=0)
        high, low = hi_lo(after_ref[t, :HR, :])
        prev_ref[t, reach:, :] = jnp.concatenate([high, low], axis=0)


def place(measured, after, parcels, height, capacity):
    tilts, strip_rows, image_width = measured.shape
    tile_count = len(parcels)
    rows = 2 * strip_rows + 2 * REACH
    halo = strip_rows + REACH + 2 * HR
    whole = pl.BlockSpec(memory_space=pltpu.VMEM)
    return pl.pallas_call(
        functools.partial(
            place_kernel,
            tilts=tilts,
            strip_rows=strip_rows,
            height=height,
            capacity=capacity,
            tile_count=tile_count,
        ),
        out_shape=[
            jax.ShapeDtypeStruct((tilts, rows, image_width), F32),
            jax.ShapeDtypeStruct((tilts, halo, image_width), BF),
            jax.ShapeDtypeStruct((tilts, halo, image_width), BF),
        ],
        in_specs=[whole] * (2 + tile_count),
        out_specs=[whole] * 3,
        scratch_shapes=[
            pltpu.VMEM((tile_count * capacity * height, image_width), BF),
            pltpu.VMEM((tilts * rows, tile_count * capacity * height), BF),
        ],
        compiler_params=GRANT,
        name="place",
    )(measured, near(after), parcels[0], *[near(p) for p in parcels[1:]])


def transfer_kernel(defocus_ref, out_ref):
    tilts, _, image_width, _ = out_ref.shape
    lanes = 128
    row = lax.broadcasted_iota(jnp.int32, (8, lanes), 0)
    lane = lax.broadcasted_iota(jnp.int32, (8, lanes), 1)
    down = lax.broadcasted_iota(jnp.int32, (8, lanes), 0)
    for t in range(tilts):
        for i in range(HR + 1):
            rho_sq = (i * i + lane * lane).astype(F32)
            value = jnp.exp(-rho_sq / (2.0 * HR * HR)) * jnp.cos(defocus_ref[t] * rho_sq) / float(HR * HR)
            value = jnp.where(lane <= HR, value, 0.0)
            for begin in range(0, image_width, 16):
                for column in range(0, image_width, lanes):
                    if begin - column > lanes + HR or column - begin > 16 + HR:
                        out_ref[t, i, begin : begin + 16, column : column + lanes] = jnp.zeros(
                            (16, lanes), BF
                        )
                        continue
                    parts = []
                    for half in range(2):
                        apart = jnp.abs(down + (begin + 8 * half - column) - lane)
                        parts.append(
                            jnp.take_along_axis(value, jnp.minimum(apart, lanes - 1), axis=1)
                        )
                    out_ref[t, i, begin : begin + 16, column : column + lanes] = jnp.concatenate(
                        parts, axis=0
                    ).astype(BF)


def transfer_tables(defocus, image_width):
    return pl.pallas_call(
        transfer_kernel,
        out_shape=jax.ShapeDtypeStruct((defocus.shape[0], HR + 1, image_width, image_width), BF),
        in_specs=[pl.BlockSpec(memory_space=pltpu.SMEM)],
        out_specs=pl.BlockSpec(memory_space=pltpu.VMEM),
        compiler_params=GRANT,
        name="transfer",
    )(defocus)


def convolve(source, parts, table_ref, t, height):
    rows = source.shape[0]
    for i in range(HR + 1):
        parts[i, :rows, :] = jnp.dot(source, table_ref[t, i], preferred_element_type=F32)
    total = parts[0, HR : HR + height, :]
    for i in range(1, HR + 1):
        total = total + (
            parts[i, HR + i : HR + i + height, :] + parts[i, HR - i : HR - i + height, :]
        )
    return total


def filter_kernel(
    canvas_ref, above_ref, below_ref, measured_ref, after_ref, table_ref, *refs, height, capacity
):
    tile_count = len(refs) - 4
    parcels, (residual_ref, out_ref, parts, back) = refs[:tile_count], refs[tile_count:]
    groups = out_ref.shape[0]
    slab_rows = height // groups
    tilts, strip_rows, image_width = measured_ref.shape
    rows = canvas_ref.shape[1]
    my_tile = lax.axis_index("tile")
    first = my_tile * strip_rows
    image_rows = tile_count * strip_rows
    reach = strip_rows + REACH

    def inside(count, start):
        at = lax.broadcasted_iota(jnp.int32, (count, image_width), 0) + (first + start)
        return (at >= 0) & (at < image_rows)

    at_top, at_end = my_tile == 0, my_tile == tile_count - 1
    for t in range(tilts):
        upper = jnp.where(at_top, 0.0, above_ref[t, :reach, :].astype(F32))
        lower = jnp.where(at_end, 0.0, below_ref[t, :reach, :].astype(F32))
        field = canvas_ref[t] + jnp.concatenate([upper, lower], axis=0)
        field = jnp.where(inside(rows, -REACH), field, 0.0)
        known = jnp.concatenate(
            [
                above_ref[t, reach : reach + HR, :].astype(F32)
                + above_ref[t, reach + HR :, :].astype(F32),
                measured_ref[t],
                after_ref[t],
                below_ref[t, reach : reach + HR, :].astype(F32)
                + below_ref[t, reach + HR :, :].astype(F32),
            ],
            axis=0,
        )
        count = rows - 2 * HR
        rest = known - convolve(field.astype(BF), parts, table_ref, t, count)
        residual_ref[t] = rest[HR : HR + strip_rows]
        rest = jnp.where(inside(count, -HR), rest, 0.0)
        count -= 2 * HR
        image = convolve(rest.astype(BF), parts, table_ref, t, count)
        back[t * count : (t + 1) * count, :] = jnp.where(inside(count, 0), image, 0.0).astype(BF)
    width = parcels[0].shape[1]
    count = 2 * strip_rows
    apart = iota_apart((height, count), 1, 0)
    column = iota_apart((image_width, width), 0, 1)
    meta = capacity * (height + 2 * REACH)
    for d, parcel in enumerate(parcels):
        sender = my_tile ^ d
        for r in range(capacity):
            top = parcel[meta + 2 * r : meta + 2 * r + 1, :].astype(F32)
            picks = []
            for t in range(tilts):
                own = top - float(t * strip_rows)
                own = jnp.where((own >= 0) & (own < strip_rows), own, float(ABSENT)).astype(BF)
                picks.append(ones_where(apart == own[:, :1]))
            cut = jnp.dot(
                jnp.concatenate(picks, axis=1), back[...], preferred_element_type=F32
            ).astype(BF)
            left = parcel[meta + 2 * r + 1 : meta + 2 * r + 2, :]
            columns = ones_where(column == left)
            window = jnp.dot(cut, columns, preferred_element_type=F32).astype(BF)
            for i in range(groups):
                out_ref[i, sender, r * slab_rows : (r + 1) * slab_rows, :] = window[
                    i * slab_rows : (i + 1) * slab_rows
                ]


def filter_and_cut(canvas, above, below, measured, after, table, parcels, height, capacity, groups):
    tilts, strip_rows, image_width = measured.shape
    tile_count = len(parcels)
    width = parcels[0].shape[1]
    rows = canvas.shape[1]
    whole = pl.BlockSpec(memory_space=pltpu.VMEM)
    slots = (groups, tile_count, capacity * height // groups, width)
    return pl.pallas_call(
        functools.partial(filter_kernel, height=height, capacity=capacity),
        out_shape=[jax.ShapeDtypeStruct(measured.shape, F32), jax.ShapeDtypeStruct(slots, BF)],
        in_specs=[whole] * (6 + tile_count),
        out_specs=[whole] * 2,
        scratch_shapes=[
            pltpu.VMEM((HR + 1, rows, image_width), F32),
            pltpu.VMEM((tilts * 2 * strip_rows, image_width), BF),
        ],
        compiler_params=GRANT,
        name="filter_and_cut",
    )(near(canvas), near(above), near(below), measured, near(after), near(table), parcels[0], *[near(p) for p in parcels[1:]])


def shards(volumes, angles, defocus, row_offsets, col_offsets, measured):
    boxes, slab_rows, depth, width = volumes.shape
    tilts, strip_rows, image_width = measured.shape
    tile_count, groups = lax.axis_size("tile"), lax.axis_size("tilt")
    height, rows = slab_rows * groups, boxes * slab_rows
    capacity = max(2, -(-boxes * tilts // tile_count))
    assert tilts * strip_rows <= 256 and tile_count * capacity <= 256
    rows_of, cols_of, angles = far(row_offsets.T), far(col_offsets.T), far(angles)
    after = ring(measured, "tile", -1)
    kernel = transfer_tables(defocus, image_width)
    slabs = [None] * groups
    volume = far(volumes.reshape(rows, depth, width))
    half = groups // 2 + 1
    early, late = tuple(range(1, half)), (*range(half, groups), 0)
    sizes = (depth, width, strip_rows, capacity)
    *parts, flat = project(volume, rows_of, angles, tilts, groups, early, True, *sizes)
    for k, part in zip(early, parts, strict=True):
        slabs[k] = swap(part, "tilt", k)
    parts = project(flat, rows_of, angles, tilts, groups, late, False, *sizes)
    for k, part in zip(late, parts, strict=True):
        slabs[k] = swap(part, "tilt", k) if k else part
    parcels = pack(slabs, rows_of, cols_of, slab_rows, tile_count, strip_rows, capacity)
    parcels = [p if d == 0 else swap(p, "tile", d) for d, p in enumerate(parcels)]
    canvas, onward, backward = place(measured, after, parcels, height, capacity)
    above, below = ring(onward, "tile", 1), ring(backward, "tile", -1)
    residual, cuts = filter_and_cut(
        canvas, above, below, measured, after, kernel, parcels, height, capacity, groups
    )
    cuts = cuts.reshape(groups * tile_count, capacity * slab_rows, width)
    cuts = lax.all_to_all(cuts, ("tilt", "tile"), split_axis=0, concat_axis=0, tiled=True)
    cuts = cuts.reshape(groups, tile_count * capacity * slab_rows, width)
    step = back_project(cuts, slabs, angles, boxes, tilts, rows, depth, 1.0 / (tilts * groups))
    return residual, step.reshape(boxes, slab_rows, depth, width)


def solution(mesh):
    in_specs = (
        P("tile", "tilt", None, None),
        P(),
        P("tilt"),
        P("tile", "tilt"),
        P("tile", "tilt"),
        P("tilt", "tile", None),
    )
    out_specs = (P("tilt", "tile", None), P("tile", "tilt", None, None))

    return jax.shard_map(shards, mesh=mesh, in_specs=in_specs, out_specs=out_specs, check_vma=False)
```

```python
import functools

import jax
import jax.numpy as jnp
from jax import lax
from jax.experimental import pallas as pl
from jax.experimental.pallas import tpu as pltpu
from jax.sharding import PartitionSpec as P

HR = 8
REACH = 2 * HR
BF = jnp.bfloat16
F32 = jnp.float32
ABSENT = -1024
GRANT = pltpu.CompilerParams(vmem_limit_bytes=32 * 1024 * 1024)


def ring(block, axis, distance):
    count = lax.axis_size(axis)
    return lax.ppermute(block, axis, [(i, (i + distance) % count) for i in range(count)])


def swap(block, axis, distance):
    count = lax.axis_size(axis)
    assert count & (count - 1) == 0
    return lax.ppermute(block, axis, [(i, i ^ distance) for i in range(count)])


def far(block):
    return pltpu.with_memory_space_constraint(block, pltpu.HBM)


def near(block):
    return pltpu.with_memory_space_constraint(block, pltpu.VMEM)


def quotient(value, size):
    if size & (size - 1) == 0:
        return lax.shift_right_logical(value, size.bit_length() - 1)
    return lax.div(value, size)


def ones_where(mask):
    return jnp.where(mask, jnp.ones(mask.shape, BF), jnp.zeros(mask.shape, BF))


def iota_apart(shape, plus, minus):
    ahead = lax.broadcasted_iota(jnp.int32, shape, plus)
    behind = lax.broadcasted_iota(jnp.int32, shape, minus)
    return (ahead - behind).astype(F32).astype(BF)


def note_sines(angle_ref, sine_ref):
    for t in range(sine_ref.shape[0]):
        sine_ref[t] = jnp.sin(jnp.full(sine_ref.shape[1:], angle_ref[t], F32))


def tap_block(apart, sine, layer, depth):
    shift = (layer.astype(F32) - (depth - 1) / 2.0) * sine
    lower = jnp.floor(shift)
    copies = apart.shape[0] // (2 * sine.shape[0])

    def filled(value):
        return jnp.concatenate([jnp.concatenate([value] * 2, axis=0).astype(BF)] * copies, axis=0)

    def weight(offset):
        return filled(jnp.maximum(0.0, 1.0 - jnp.abs(offset - shift)))

    beyond = jnp.where(
        apart == filled(lower + 1.0), weight(lower + 1.0), jnp.zeros(apart.shape, BF)
    )
    return jnp.where(apart == filled(lower), weight(lower), beyond)


def slots_of_items(row_ref, strip_rows, capacity):
    tilts, boxes = row_ref.shape
    strips = [quotient(row_ref[t, b], strip_rows) for t in range(tilts) for b in range(boxes)]
    slots = []
    for n, strip in enumerate(strips):
        place = strip * capacity
        for other in strips[:n]:
            place = place + jnp.where(other == strip, 1, 0)
        slots.append(place)
    return strips, slots


def splat_rows(values, rows, width):
    row_at = lax.broadcasted_iota(jnp.int32, (rows, width), 0)
    block = jnp.zeros((rows, width), F32)
    for i, value in enumerate(values):
        block = jnp.where(row_at == i, value.astype(F32), block)
    return block.astype(BF)


def project_kernel(
    row_ref, angle_ref, vol_ref, *refs, depth, tilts, groups, ks, first, strip_rows, capacity
):
    outs, (total, sines) = refs[: len(ks)], refs[-2:]
    step = pl.program_id(0)
    me = lax.axis_index("tilt")
    if first:
        lhs, wide = refs[len(ks)], refs[len(ks) + 1]
        rows, layers, width = vol_ref.shape
        wide[...] = vol_ref[...].reshape(rows * layers, width).astype(F32)

        def pair_at(z):
            pair = [wide[pl.ds(z + h, rows, stride=layers), :].astype(BF) for h in range(2)]
            pair = jnp.concatenate(pair, axis=1)
            lhs[:, z * width : (z + 2) * width] = pair
            return pair
    else:
        lhs = vol_ref
        rows = lhs.shape[0]
        width = outs[0].shape[1]
        layers = lhs.shape[1] // width

        def pair_at(z):
            return lhs[:, z * width : (z + 2) * width]

    @pl.when(step == 0)
    def _():
        total[...] = jnp.zeros_like(total)
        note_sines(angle_ref, sines)

    apart = iota_apart((width, width), 1, 0)

    def block(k, z, t):
        sine = sines[(me ^ k) * tilts + t]
        return tap_block(apart, sine, step * layers + z, depth)

    following = pair_at(0)
    for z in range(0, layers, 2):
        pair = following
        if z + 2 < layers:
            following = pair_at(z + 2)
        for i, k in enumerate(ks):
            table = jnp.concatenate(
                [
                    jnp.concatenate([block(k, z + half, t) for t in range(tilts)], axis=1)
                    for half in range(2)
                ],
                axis=0,
            )
            span = slice(i * tilts * width, (i + 1) * tilts * width)
            total[:, span] += jnp.dot(pair, table, preferred_element_type=F32)

    @pl.when(step == pl.num_programs(0) - 1)
    def _():
        _, slots = slots_of_items(row_ref, strip_rows, capacity)
        meta = splat_rows(slots, outs[0].shape[0] - tilts * rows, width)
        for i in range(len(ks)):
            for t in range(tilts):
                start = (i * tilts + t) * width
                outs[i][t * rows : (t + 1) * rows, :] = total[:, start : start + width].astype(BF)
            outs[i][tilts * rows :, :] = meta


def project(volume, rows_of, angles, tilts, groups, ks, first, depth, width, strip_rows, capacity):
    rows = volume.shape[0]
    layers = min(16, depth)
    length = tilts * rows + -(-tilts * rows_of.shape[1] // 16) * 16
    scalars = pl.BlockSpec(memory_space=pltpu.SMEM)
    flat = pl.BlockSpec((rows, layers * width), lambda i: (0, i))
    source = pl.BlockSpec((rows, layers, width), lambda i: (0, i, 0)) if first else flat
    return pl.pallas_call(
        functools.partial(
            project_kernel,
            depth=depth,
            tilts=tilts,
            groups=groups,
            ks=ks,
            first=first,
            strip_rows=strip_rows,
            capacity=capacity,
        ),
        out_shape=[jax.ShapeDtypeStruct((length, width), BF)] * len(ks)
        + ([jax.ShapeDtypeStruct((rows, depth * width), BF)] if first else []),
        grid=(depth // layers,),
        in_specs=[scalars] * 2 + [source],
        out_specs=[pl.BlockSpec((length, width), lambda i: (0, 0))] * len(ks)
        + ([flat] if first else []),
        scratch_shapes=([pltpu.VMEM((rows * layers, width), F32)] if first else [])
        + [
            pltpu.VMEM((rows, len(ks) * tilts * width), F32),
            pltpu.VMEM((groups * tilts, 8, width), F32),
        ],
        compiler_params=GRANT,
        name="project_first" if first else "project_rest",
    )(rows_of, angles, volume)


def back_kernel(
    angle_ref, cut_ref, *refs, depth, tilts, boxes, groups, scale
):
    metas, (out_ref, lhs, sines) = refs[:groups], refs[groups:]
    step = pl.program_id(0)
    me = lax.axis_index("tilt")
    rows, layers, width = out_ref.shape
    slab_rows, length = rows // boxes, cut_ref.shape[1]
    apart = iota_apart((width, width), 0, 1)

    @pl.when(step == 0)
    def _():
        note_sines(angle_ref, sines)
        ahead = lax.broadcasted_iota(jnp.int32, (slab_rows, length), 1)
        ahead = (ahead - lax.broadcasted_iota(jnp.int32, (slab_rows, length), 0)).astype(F32)
        for k in range(groups):
            group = (me ^ k)
            for t in range(tilts):
                picks = []
                for b in range(boxes):
                    slot = metas[k][t * boxes + b : t * boxes + b + 1, :1].astype(F32)
                    picks.append(ones_where(ahead == slot * float(slab_rows)))
                start = (k * tilts + t) * width
                lhs[:, start : start + width] = jnp.dot(
                    jnp.concatenate(picks, axis=0), cut_ref[group], preferred_element_type=F32
                ).astype(BF)

    def block(k, t, z):
        sine = sines[(me ^ k) * tilts + t]
        return tap_block(apart, sine, step * layers + z, depth)

    flat = out_ref.reshape(rows * layers, width)
    for z in range(0, layers, 2):
        table = jnp.concatenate(
            [
                jnp.concatenate([block(k, t, z + half) for half in range(2)], axis=1)
                for k in range(groups)
                for t in range(tilts)
            ],
            axis=0,
        )
        result = jnp.dot(lhs[...], table, preferred_element_type=F32) * scale
        for half in range(2):
            flat[pl.ds(z + half, rows, stride=layers), :] = result[
                :, half * width : (half + 1) * width
            ]


def back_project(cuts, slabs, angles, boxes, tilts, rows, depth, scale):
    groups, _, width = cuts.shape
    layers = min(8, depth)
    meta = slabs[0].shape[0] - tilts * rows
    at = tilts * rows // meta
    scalars = pl.BlockSpec(memory_space=pltpu.SMEM)
    return pl.pallas_call(
        functools.partial(
            back_kernel, depth=depth, tilts=tilts, boxes=boxes, groups=groups, scale=scale
        ),
        out_shape=jax.ShapeDtypeStruct((rows, depth, width), F32),
        grid=(depth // layers,),
        in_specs=[scalars]
        + [pl.BlockSpec(cuts.shape, lambda i: (0, 0, 0))]
        + [pl.BlockSpec((meta, width), lambda i: (at, 0))] * groups,
        out_specs=pl.BlockSpec((rows, layers, width), lambda i: (0, i, 0)),
        scratch_shapes=[
            pltpu.VMEM((rows, groups * tilts * width), BF),
            pltpu.VMEM((groups * tilts, 8, width), F32),
        ],
        compiler_params=GRANT,
        name="back_project",
    )(angles, cuts, *slabs)


def pack_kernel(row_ref, col_ref, *refs, groups, tile_count, strip_rows, capacity, slab_rows):
    slabs, outs = refs[:groups], refs[groups : groups + tile_count]
    item_ref, within_ref, left_ref = refs[groups + tile_count :]
    _, boxes = row_ref.shape
    width = slabs[0].shape[1]
    height = slab_rows * groups
    my_tilt, my_tile = lax.axis_index("tilt"), lax.axis_index("tile")
    strips, slots = slots_of_items(row_ref, strip_rows, capacity)
    margin = 2 * capacity

    def clear(i, carry):
        item_ref[i] = -1
        within_ref[i] = ABSENT
        left_ref[i] = 0
        return carry

    lax.fori_loop(0, tile_count * capacity + 2 * margin, clear, 0)
    for n, (strip, slot) in enumerate(zip(strips, slots, strict=True)):
        t, b = n // boxes, n % boxes
        item_ref[slot + margin] = n
        within_ref[slot + margin] = row_ref[t, b] - strip * strip_rows + t * strip_rows
        left_ref[slot + margin] = col_ref[t, b]
    sources = [my_tilt ^ k for k in range(groups)]

    def slab_of(k, item, begin, size):
        start = pl.multiple_of(jnp.maximum(item, 0) * slab_rows + begin, 16)
        block = slabs[k][pl.ds(start, size), :]
        return jnp.where(item >= 0, block, jnp.zeros_like(block))

    for d in range(tile_count):
        out = outs[d]
        strip = lax.rem(my_tile + d, tile_count)
        metas = []

        def item_at(offset, r):
            spot = (strip + offset + 2) * capacity + r
            metas.append(within_ref[spot])
            metas.append(left_ref[spot])
            return item_ref[spot]

        for r in range(capacity):
            item = item_at(0, r)
            for k in range(groups):
                begin = pl.multiple_of(r * height + sources[k] * slab_rows, slab_rows)
                out[pl.ds(begin, slab_rows), :] = slab_of(k, item, 0, slab_rows)
        base = capacity * height
        for offset, wanted, begin in ((2, 0, 0), (-2, groups - 1, slab_rows - REACH)):
            for r in range(capacity):
                item = item_at(offset, r)
                block = slab_of(0, item, begin, REACH)
                for k in range(1, groups):
                    block = jnp.where(sources[k] == wanted, slab_of(k, item, begin, REACH), block)
                out[base : base + REACH, :] = block
                base += REACH
        out[base:, :] = splat_rows(metas, out.shape[0] - base, width)


def pack(slabs, rows_of, cols_of, slab_rows, tile_count, strip_rows, capacity):
    groups = len(slabs)
    width = slabs[0].shape[1]
    meta_rows = -(-6 * capacity // 16) * 16
    length = capacity * (slab_rows * groups + 2 * REACH) + meta_rows
    slots = (tile_count + 4) * capacity
    return pl.pallas_call(
        functools.partial(
            pack_kernel,
            groups=groups,
            tile_count=tile_count,
            strip_rows=strip_rows,
            capacity=capacity,
            slab_rows=slab_rows,
        ),
        out_shape=[jax.ShapeDtypeStruct((length, width), BF)] * tile_count,
        in_specs=[pl.BlockSpec(memory_space=pltpu.SMEM)] * 2
        + [pl.BlockSpec(memory_space=pltpu.VMEM)] * groups,
        out_specs=[pl.BlockSpec(memory_space=pltpu.VMEM)] * tile_count,
        scratch_shapes=[pltpu.SMEM((slots,), jnp.int32)] * 3,
        compiler_params=GRANT,
        name="pack",
    )(rows_of, cols_of, slabs[0], *[near(slab) for slab in slabs[1:]])


def hi_lo(block):
    high = block.astype(BF)
    return high, (block - high.astype(F32)).astype(BF)


def place_kernel(measured_ref, after_ref, *refs, tilts, strip_rows, height, capacity, tile_count):
    parcels = refs[:tile_count]
    canvas_ref, next_ref, prev_ref, placed, onehot = refs[tile_count:]
    _, width = parcels[0].shape
    rows, image_width = canvas_ref.shape[1:]
    column = iota_apart((width, image_width), 1, 0)
    apart = iota_apart((rows, height), 0, 1)
    edge_apart = iota_apart((REACH, REACH), 0, 1)
    base = capacity * height
    meta = base + 2 * capacity * REACH

    def spread_out(parcel, begin, size, q):
        left = parcel[meta + 2 * q + 1 : meta + 2 * q + 2, :1]
        picks = ones_where(column == left)
        return jnp.dot(parcel[begin : begin + size, :], picks, preferred_element_type=F32).astype(BF)

    def row_of(parcel, q, t):
        own = parcel[meta + 2 * q : meta + 2 * q + 1, :].astype(F32) - float(t * strip_rows)
        return jnp.where((own >= 0) & (own < strip_rows), own, float(ABSENT))

    index = 0
    for parcel in parcels:
        for r in range(capacity):
            placed[index * height : (index + 1) * height, :] = spread_out(parcel, r * height, height, r)
            for t in range(tilts):
                target = (row_of(parcel, r, t) + float(REACH)).astype(BF)
                onehot[t * rows : (t + 1) * rows, index * height : (index + 1) * height] = (
                    ones_where(apart == target)
                )
            index += 1
    total = jnp.dot(onehot[...], placed[...], preferred_element_type=F32)
    for t in range(tilts):
        canvas_ref[t] = total[t * rows : (t + 1) * rows]
    for side in range(2):
        blocks = [[] for _ in range(tilts)]
        values = []
        for parcel in parcels:
            for r in range(capacity):
                q = (1 + side) * capacity + r
                begin = base + side * capacity * REACH + r * REACH
                values.append(spread_out(parcel, begin, REACH, q))
                for t in range(tilts):
                    target = row_of(parcel, q, t)[:, :REACH]
                    if side == 1:
                        target = target + float(height - 2 * strip_rows)
                    blocks[t].append(ones_where(edge_apart == target.astype(BF)))
        tall = jnp.concatenate(values, axis=0)
        for t in range(tilts):
            picks = jnp.concatenate(blocks[t], axis=1)
            edge = jnp.dot(picks, tall, preferred_element_type=F32)
            begin = rows - REACH if side == 0 else 0
            canvas_ref[t, begin : begin + REACH, :] = edge
    reach = strip_rows + REACH
    for t in range(tilts):
        next_ref[t, :reach, :] = canvas_ref[t, strip_rows : strip_rows + reach, :].astype(BF)
        prev_ref[t, :reach, :] = canvas_ref[t, REACH : REACH + reach, :].astype(BF)
        high, low = hi_lo(measured_ref[t, strip_rows - HR :, :])
        next_ref[t, reach:, :] = jnp.concatenate([high, low], axis=0)
        high, low = hi_lo(after_ref[t, :HR, :])
        prev_ref[t, reach:, :] = jnp.concatenate([high, low], axis=0)


def place(measured, after, parcels, height, capacity):
    tilts, strip_rows, image_width = measured.shape
    tile_count = len(parcels)
    rows = 2 * strip_rows + 2 * REACH
    halo = strip_rows + REACH + 2 * HR
    whole = pl.BlockSpec(memory_space=pltpu.VMEM)
    return pl.pallas_call(
        functools.partial(
            place_kernel,
            tilts=tilts,
            strip_rows=strip_rows,
            height=height,
            capacity=capacity,
            tile_count=tile_count,
        ),
        out_shape=[
            jax.ShapeDtypeStruct((tilts, rows, image_width), F32),
            jax.ShapeDtypeStruct((tilts, halo, image_width), BF),
            jax.ShapeDtypeStruct((tilts, halo, image_width), BF),
        ],
        in_specs=[whole] * (2 + tile_count),
        out_specs=[whole] * 3,
        scratch_shapes=[
            pltpu.VMEM((tile_count * capacity * height, image_width), BF),
            pltpu.VMEM((tilts * rows, tile_count * capacity * height), BF),
        ],
        compiler_params=GRANT,
        name="place",
    )(measured, near(after), parcels[0], *[near(p) for p in parcels[1:]])


def transfer_kernel(defocus_ref, out_ref):
    tilts, _, image_width, _ = out_ref.shape
    lanes = 128
    row = lax.broadcasted_iota(jnp.int32, (8, lanes), 0)
    lane = lax.broadcasted_iota(jnp.int32, (8, lanes), 1)
    down = lax.broadcasted_iota(jnp.int32, (8, lanes), 0)
    for t in range(tilts):
        for i in range(HR + 1):
            rho_sq = (i * i + lane * lane).astype(F32)
            value = jnp.exp(-rho_sq / (2.0 * HR * HR)) * jnp.cos(defocus_ref[t] * rho_sq) / float(HR * HR)
            value = jnp.where(lane <= HR, value, 0.0)
            for begin in range(0, image_width, 16):
                for column in range(0, image_width, lanes):
                    if begin - column > lanes + HR or column - begin > 16 + HR:
                        out_ref[t, i, begin : begin + 16, column : column + lanes] = jnp.zeros(
                            (16, lanes), BF
                        )
                        continue
                    parts = []
                    for half in range(2):
                        apart = jnp.abs(down + (begin + 8 * half - column) - lane)
                        parts.append(
                            jnp.take_along_axis(value, jnp.minimum(apart, lanes - 1), axis=1)
                        )
                    out_ref[t, i, begin : begin + 16, column : column + lanes] = jnp.concatenate(
                        parts, axis=0
                    ).astype(BF)


def transfer_tables(defocus, image_width):
    return pl.pallas_call(
        transfer_kernel,
        out_shape=jax.ShapeDtypeStruct((defocus.shape[0], HR + 1, image_width, image_width), BF),
        in_specs=[pl.BlockSpec(memory_space=pltpu.SMEM)],
        out_specs=pl.BlockSpec(memory_space=pltpu.VMEM),
        compiler_params=GRANT,
        name="transfer",
    )(defocus)


def products(source, parts, table_ref, t):
    def one(i):
        def emit():
            parts[i, : source.shape[0], :] = jnp.dot(
                source[...], table_ref[t, i], preferred_element_type=F32
            )

        return emit

    return [one(i) for i in range(HR + 1)]


def shifted_sums(parts, height, finish):
    def one(begin):
        def emit():
            total = parts[0, HR + begin : HR + begin + 16, :]
            for i in range(1, HR + 1):
                for at in (HR + i + begin, HR - i + begin):
                    total = total + parts[i, at : at + 16, :]
            finish(begin, total)

        return emit

    return [one(begin) for begin in range(0, height, 16)]


def emit_beside(first, second):
    done = 0
    for n, emit in enumerate(first):
        emit()
        upto = len(second) * (n + 1) // len(first)
        for other in second[done:upto]:
            other()
        done = upto


def filter_kernel(
    canvas_ref, above_ref, below_ref, measured_ref, after_ref, table_ref, *refs, height, capacity
):
    tile_count = len(refs) - 7
    parcels = refs[:tile_count]
    residual_ref, out_ref, parts, fields, known, rests, back = refs[tile_count:]
    groups = out_ref.shape[0]
    slab_rows = height // groups
    tilts, strip_rows, image_width = measured_ref.shape
    rows = canvas_ref.shape[1]
    my_tile = lax.axis_index("tile")
    first = my_tile * strip_rows
    image_rows = tile_count * strip_rows
    reach = strip_rows + REACH

    def inside(count, start):
        at = lax.broadcasted_iota(jnp.int32, (count, image_width), 0) + (first + start)
        return (at >= 0) & (at < image_rows)

    at_top, at_end = my_tile == 0, my_tile == tile_count - 1
    for t in range(tilts):
        for half, (edge, none) in enumerate(((above_ref, at_top), (below_ref, at_end))):
            for begin in range(0, reach, 16):
                row = half * reach + begin
                field = jnp.where(none, 0.0, edge[t, begin : begin + 16, :].astype(F32))
                field = jnp.where(
                    inside(16, row - REACH), field + canvas_ref[t, row : row + 16, :], 0.0
                )
                fields[t, row : row + 16, :] = field.astype(BF)
        known[t, :HR, :] = above_ref[t, reach : reach + HR, :].astype(F32) + above_ref[
            t, reach + HR :, :
        ].astype(F32)
        known[t, HR : HR + strip_rows, :] = measured_ref[t]
        known[t, HR + strip_rows : HR + 2 * strip_rows, :] = after_ref[t]
        known[t, HR + 2 * strip_rows :, :] = below_ref[t, reach : reach + HR, :].astype(
            F32
        ) + below_ref[t, reach + HR :, :].astype(F32)
    count = rows - 2 * HR

    def keep_residual(t):
        def finish(begin, total):
            rest = known[t, begin : begin + 16, :] - total
            low, high = max(begin, HR), min(begin + 16, HR + strip_rows)
            if low < high:
                residual_ref[t, low - HR : high - HR, :] = rest[low - begin : high - begin]
            rests[t, begin : begin + 16, :] = jnp.where(
                inside(16, begin - HR), rest, 0.0
            ).astype(BF)

        return finish

    def keep_back(t):
        def finish(begin, total):
            row = t * 2 * strip_rows + begin
            back[row : row + 16, :] = jnp.where(inside(16, begin), total, 0.0).astype(BF)

        return finish

    stages = [
        (
            products(fields.at[t], parts.at[t], table_ref, t),
            shifted_sums(parts.at[t], count, keep_residual(t)),
        )
        for t in range(tilts)
    ]
    stages += [
        (
            products(rests.at[t], parts.at[t], table_ref, t),
            shifted_sums(parts.at[t], count - 2 * HR, keep_back(t)),
        )
        for t in range(tilts)
    ]
    assert tilts > 1
    waiting = []
    for multiply, add in stages:
        emit_beside(multiply, waiting)
        waiting = add
    for emit in waiting:
        emit()
    width = parcels[0].shape[1]
    count = 2 * strip_rows
    apart = iota_apart((height, count), 1, 0)
    column = iota_apart((image_width, width), 0, 1)
    meta = capacity * (height + 2 * REACH)
    for d, parcel in enumerate(parcels):
        sender = lax.rem(my_tile + tile_count - d, tile_count)
        for r in range(capacity):
            top = parcel[meta + 2 * r : meta + 2 * r + 1, :].astype(F32)
            picks = []
            for t in range(tilts):
                own = top - float(t * strip_rows)
                own = jnp.where((own >= 0) & (own < strip_rows), own, float(ABSENT)).astype(BF)
                picks.append(ones_where(apart == own[:, :1]))
            cut = jnp.dot(
                jnp.concatenate(picks, axis=1), back[...], preferred_element_type=F32
            ).astype(BF)
            left = parcel[meta + 2 * r + 1 : meta + 2 * r + 2, :]
            columns = ones_where(column == left)
            window = jnp.dot(cut, columns, preferred_element_type=F32).astype(BF)
            for i in range(groups):
                out_ref[i, sender, r * slab_rows : (r + 1) * slab_rows, :] = window[
                    i * slab_rows : (i + 1) * slab_rows
                ]


def filter_and_cut(canvas, above, below, measured, after, table, parcels, height, capacity, groups):
    tilts, strip_rows, image_width = measured.shape
    tile_count = len(parcels)
    width = parcels[0].shape[1]
    rows = canvas.shape[1]
    whole = pl.BlockSpec(memory_space=pltpu.VMEM)
    slots = (groups, tile_count, capacity * height // groups, width)
    return pl.pallas_call(
        functools.partial(filter_kernel, height=height, capacity=capacity),
        out_shape=[jax.ShapeDtypeStruct(measured.shape, F32), jax.ShapeDtypeStruct(slots, BF)],
        in_specs=[whole] * (6 + tile_count),
        out_specs=[whole] * 2,
        scratch_shapes=[
            pltpu.VMEM((tilts, HR + 1, rows, image_width), F32),
            pltpu.VMEM((tilts, rows, image_width), BF),
            pltpu.VMEM((tilts, rows - 2 * HR, image_width), F32),
            pltpu.VMEM((tilts, rows - 2 * HR, image_width), BF),
            pltpu.VMEM((tilts * 2 * strip_rows, image_width), BF),
        ],
        compiler_params=GRANT,
        name="filter_and_cut",
    )(near(canvas), near(above), near(below), measured, near(after), near(table), parcels[0], *[near(p) for p in parcels[1:]])


def shards(volumes, angles, defocus, row_offsets, col_offsets, measured):
    boxes, slab_rows, depth, width = volumes.shape
    tilts, strip_rows, image_width = measured.shape
    tile_count, groups = lax.axis_size("tile"), lax.axis_size("tilt")
    height, rows = slab_rows * groups, boxes * slab_rows
    capacity = max(2, -(-boxes * tilts // tile_count))
    assert tilts * strip_rows <= 256 and tile_count * capacity <= 256
    rows_of, cols_of, angles = far(row_offsets.T), far(col_offsets.T), far(angles)
    after = ring(measured, "tile", -1)
    kernel = transfer_tables(defocus, image_width)
    slabs = [None] * groups
    volume = far(volumes.reshape(rows, depth, width))
    half = groups // 2 + 1
    early, late = tuple(range(1, half)), (*range(half, groups), 0)
    sizes = (depth, width, strip_rows, capacity)
    *parts, flat = project(volume, rows_of, angles, tilts, groups, early, True, *sizes)
    for k, part in zip(early, parts, strict=True):
        slabs[k] = swap(part, "tilt", k)
    parts = project(flat, rows_of, angles, tilts, groups, late, False, *sizes)
    for k, part in zip(late, parts, strict=True):
        slabs[k] = swap(part, "tilt", k) if k else part
    parcels = pack(slabs, rows_of, cols_of, slab_rows, tile_count, strip_rows, capacity)
    parcels = [p if d == 0 else ring(p, "tile", d) for d, p in enumerate(parcels)]
    canvas, onward, backward = place(measured, after, parcels, height, capacity)
    above, below = ring(onward, "tile", 1), ring(backward, "tile", -1)
    residual, cuts = filter_and_cut(
        canvas, above, below, measured, after, kernel, parcels, height, capacity, groups
    )
    cuts = cuts.reshape(groups * tile_count, capacity * slab_rows, width)
    cuts = lax.all_to_all(cuts, ("tilt", "tile"), split_axis=0, concat_axis=0, tiled=True)
    cuts = cuts.reshape(groups, tile_count * capacity * slab_rows, width)
    step = back_project(cuts, slabs, angles, boxes, tilts, rows, depth, 1.0 / (tilts * groups))
    return residual, step.reshape(boxes, slab_rows, depth, width)


def solution(mesh):
    in_specs = (
        P("tile", "tilt", None, None),
        P(),
        P("tilt"),
        P("tile", "tilt"),
        P("tile", "tilt"),
        P("tilt", "tile", None),
    )
    out_specs = (P("tilt", "tile", None), P("tile", "tilt", None, None))

    return jax.shard_map(shards, mesh=mesh, in_specs=in_specs, out_specs=out_specs, check_vma=False)
```

```python
import functools

import jax
import jax.numpy as jnp
from jax import lax
from jax.experimental import pallas as pl
from jax.experimental.pallas import tpu as pltpu
from jax.sharding import PartitionSpec as P

HR = 8
REACH = 2 * HR
BF = jnp.bfloat16
F32 = jnp.float32
ABSENT = -1024
GRANT = pltpu.CompilerParams(vmem_limit_bytes=32 * 1024 * 1024)


def ring(block, axis, distance):
    count = lax.axis_size(axis)
    return lax.ppermute(block, axis, [(i, (i + distance) % count) for i in range(count)])


def swap(block, axis, distance):
    count = lax.axis_size(axis)
    assert count & (count - 1) == 0
    return lax.ppermute(block, axis, [(i, i ^ distance) for i in range(count)])


def far(block):
    return pltpu.with_memory_space_constraint(block, pltpu.HBM)


def near(block):
    return pltpu.with_memory_space_constraint(block, pltpu.VMEM)


def quotient(value, size):
    if size & (size - 1) == 0:
        return lax.shift_right_logical(value, size.bit_length() - 1)
    return lax.div(value, size)


def ones_where(mask):
    return jnp.where(mask, jnp.ones(mask.shape, BF), jnp.zeros(mask.shape, BF))


def iota_apart(shape, plus, minus):
    ahead = lax.broadcasted_iota(jnp.int32, shape, plus)
    behind = lax.broadcasted_iota(jnp.int32, shape, minus)
    return (ahead - behind).astype(F32).astype(BF)


def note_sines(angle_ref, sine_ref):
    for t in range(sine_ref.shape[0]):
        sine_ref[t] = jnp.sin(jnp.full(sine_ref.shape[1:], angle_ref[t], F32))


def tap_block(apart, sine, layer, depth):
    shift = (layer.astype(F32) - (depth - 1) / 2.0) * sine
    lower = jnp.floor(shift)
    copies = apart.shape[0] // (2 * sine.shape[0])

    def filled(value):
        return jnp.concatenate([jnp.concatenate([value] * 2, axis=0).astype(BF)] * copies, axis=0)

    def weight(offset):
        return filled(jnp.maximum(0.0, 1.0 - jnp.abs(offset - shift)))

    beyond = jnp.where(
        apart == filled(lower + 1.0), weight(lower + 1.0), jnp.zeros(apart.shape, BF)
    )
    return jnp.where(apart == filled(lower), weight(lower), beyond)


def slots_of_items(row_ref, strip_rows, capacity):
    tilts, boxes = row_ref.shape
    strips = [quotient(row_ref[t, b], strip_rows) for t in range(tilts) for b in range(boxes)]
    slots = []
    for n, strip in enumerate(strips):
        place = strip * capacity
        for other in strips[:n]:
            place = place + jnp.where(other == strip, 1, 0)
        slots.append(place)
    return strips, slots


def splat_rows(values, rows, width):
    row_at = lax.broadcasted_iota(jnp.int32, (rows, width), 0)
    block = jnp.zeros((rows, width), F32)
    for i, value in enumerate(values):
        block = jnp.where(row_at == i, value.astype(F32), block)
    return block.astype(BF)


def project_kernel(
    row_ref, angle_ref, vol_ref, *refs, depth, tilts, groups, ks, first, strip_rows, capacity
):
    outs, (total, sines) = refs[: len(ks)], refs[-2:]
    step = pl.program_id(0)
    me = lax.axis_index("tilt")
    if first:
        lhs, wide = refs[len(ks)], refs[len(ks) + 1]
        rows, layers, width = vol_ref.shape
        wide[...] = vol_ref[...].reshape(rows * layers, width).astype(F32)

        def pair_at(z):
            pair = [wide[pl.ds(z + h, rows, stride=layers), :].astype(BF) for h in range(2)]
            pair = jnp.concatenate(pair, axis=1)
            lhs[:, z * width : (z + 2) * width] = pair
            return pair
    else:
        lhs = vol_ref
        rows = lhs.shape[0]
        width = outs[0].shape[1]
        layers = lhs.shape[1] // width

        def pair_at(z):
            return lhs[:, z * width : (z + 2) * width]

    @pl.when(step == 0)
    def _():
        total[...] = jnp.zeros_like(total)
        note_sines(angle_ref, sines)

    apart = iota_apart((width, width), 1, 0)

    def block(k, z, t):
        sine = sines[(me ^ k) * tilts + t]
        return tap_block(apart, sine, step * layers + z, depth)

    following = pair_at(0)
    for z in range(0, layers, 2):
        pair = following
        if z + 2 < layers:
            following = pair_at(z + 2)
        for i, k in enumerate(ks):
            table = jnp.concatenate(
                [
                    jnp.concatenate([block(k, z + half, t) for t in range(tilts)], axis=1)
                    for half in range(2)
                ],
                axis=0,
            )
            span = slice(i * tilts * width, (i + 1) * tilts * width)
            total[:, span] += jnp.dot(pair, table, preferred_element_type=F32)

    @pl.when(step == pl.num_programs(0) - 1)
    def _():
        _, slots = slots_of_items(row_ref, strip_rows, capacity)
        meta = splat_rows(slots, outs[0].shape[0] - tilts * rows, width)
        for i in range(len(ks)):
            for t in range(tilts):
                start = (i * tilts + t) * width
                outs[i][t * rows : (t + 1) * rows, :] = total[:, start : start + width].astype(BF)
            outs[i][tilts * rows :, :] = meta


def project(volume, rows_of, angles, tilts, groups, ks, first, depth, width, strip_rows, capacity):
    rows = volume.shape[0]
    layers = min(16, depth)
    length = tilts * rows + -(-tilts * rows_of.shape[1] // 16) * 16
    scalars = pl.BlockSpec(memory_space=pltpu.SMEM)
    flat = pl.BlockSpec((rows, layers * width), lambda i: (0, i))
    source = pl.BlockSpec((rows, layers, width), lambda i: (0, i, 0)) if first else flat
    return pl.pallas_call(
        functools.partial(
            project_kernel,
            depth=depth,
            tilts=tilts,
            groups=groups,
            ks=ks,
            first=first,
            strip_rows=strip_rows,
            capacity=capacity,
        ),
        out_shape=[jax.ShapeDtypeStruct((length, width), BF)] * len(ks)
        + ([jax.ShapeDtypeStruct((rows, depth * width), BF)] if first else []),
        grid=(depth // layers,),
        in_specs=[scalars] * 2 + [source],
        out_specs=[pl.BlockSpec((length, width), lambda i: (0, 0))] * len(ks)
        + ([flat] if first else []),
        scratch_shapes=([pltpu.VMEM((rows * layers, width), F32)] if first else [])
        + [
            pltpu.VMEM((rows, len(ks) * tilts * width), F32),
            pltpu.VMEM((groups * tilts, 8, width), F32),
        ],
        compiler_params=GRANT,
        name="project_first" if first else "project_rest",
    )(rows_of, angles, volume)


def back_kernel(
    angle_ref, cut_ref, *refs, depth, tilts, boxes, groups, scale
):
    metas, (out_ref, lhs, sines) = refs[:groups], refs[groups:]
    step = pl.program_id(0)
    me = lax.axis_index("tilt")
    rows, layers, width = out_ref.shape
    slab_rows, length = rows // boxes, cut_ref.shape[1]
    apart = iota_apart((width, width), 0, 1)

    @pl.when(step == 0)
    def _():
        note_sines(angle_ref, sines)
        ahead = lax.broadcasted_iota(jnp.int32, (slab_rows, length), 1)
        ahead = (ahead - lax.broadcasted_iota(jnp.int32, (slab_rows, length), 0)).astype(F32)
        for k in range(groups):
            group = (me ^ k)
            for t in range(tilts):
                picks = []
                for b in range(boxes):
                    slot = metas[k][t * boxes + b : t * boxes + b + 1, :1].astype(F32)
                    picks.append(ones_where(ahead == slot * float(slab_rows)))
                start = (k * tilts + t) * width
                lhs[:, start : start + width] = jnp.dot(
                    jnp.concatenate(picks, axis=0), cut_ref[group], preferred_element_type=F32
                ).astype(BF)

    def block(k, t, z):
        sine = sines[(me ^ k) * tilts + t]
        return tap_block(apart, sine, step * layers + z, depth)

    flat = out_ref.reshape(rows * layers, width)
    for z in range(0, layers, 2):
        table = jnp.concatenate(
            [
                jnp.concatenate([block(k, t, z + half) for half in range(2)], axis=1)
                for k in range(groups)
                for t in range(tilts)
            ],
            axis=0,
        )
        result = jnp.dot(lhs[...], table, preferred_element_type=F32) * scale
        for half in range(2):
            flat[pl.ds(z + half, rows, stride=layers), :] = result[
                :, half * width : (half + 1) * width
            ]


def back_project(cuts, slabs, angles, boxes, tilts, rows, depth, scale):
    groups, _, width = cuts.shape
    layers = min(8, depth)
    meta = slabs[0].shape[0] - tilts * rows
    at = tilts * rows // meta
    scalars = pl.BlockSpec(memory_space=pltpu.SMEM)
    return pl.pallas_call(
        functools.partial(
            back_kernel, depth=depth, tilts=tilts, boxes=boxes, groups=groups, scale=scale
        ),
        out_shape=jax.ShapeDtypeStruct((rows, depth, width), F32),
        grid=(depth // layers,),
        in_specs=[scalars]
        + [pl.BlockSpec(cuts.shape, lambda i: (0, 0, 0))]
        + [pl.BlockSpec((meta, width), lambda i: (at, 0))] * groups,
        out_specs=pl.BlockSpec((rows, layers, width), lambda i: (0, i, 0)),
        scratch_shapes=[
            pltpu.VMEM((rows, groups * tilts * width), BF),
            pltpu.VMEM((groups * tilts, 8, width), F32),
        ],
        compiler_params=GRANT,
        name="back_project",
    )(angles, cuts, *slabs)


def pack_kernel(row_ref, col_ref, *refs, groups, tile_count, strip_rows, capacity, slab_rows):
    slabs, outs = refs[:groups], refs[groups : groups + tile_count]
    item_ref, within_ref, left_ref = refs[groups + tile_count :]
    _, boxes = row_ref.shape
    width = slabs[0].shape[1]
    height = slab_rows * groups
    my_tilt, my_tile = lax.axis_index("tilt"), lax.axis_index("tile")
    strips, slots = slots_of_items(row_ref, strip_rows, capacity)
    margin = 2 * capacity

    def clear(i, carry):
        item_ref[i] = -1
        within_ref[i] = ABSENT
        left_ref[i] = 0
        return carry

    lax.fori_loop(0, tile_count * capacity + 2 * margin, clear, 0)
    for n, (strip, slot) in enumerate(zip(strips, slots, strict=True)):
        t, b = n // boxes, n % boxes
        item_ref[slot + margin] = n
        within_ref[slot + margin] = row_ref[t, b] - strip * strip_rows + t * strip_rows
        left_ref[slot + margin] = col_ref[t, b]
    sources = [my_tilt ^ k for k in range(groups)]

    def slab_of(k, item, begin, size):
        start = pl.multiple_of(jnp.maximum(item, 0) * slab_rows + begin, 16)
        block = slabs[k][pl.ds(start, size), :]
        return jnp.where(item >= 0, block, jnp.zeros_like(block))

    for d in range(tile_count):
        out = outs[d]
        strip = lax.rem(my_tile + d, tile_count)
        metas = []

        def item_at(offset, r):
            spot = (strip + offset + 2) * capacity + r
            metas.append(within_ref[spot])
            metas.append(left_ref[spot])
            return item_ref[spot]

        for r in range(capacity):
            item = item_at(0, r)
            for k in range(groups):
                begin = pl.multiple_of(r * height + sources[k] * slab_rows, slab_rows)
                out[pl.ds(begin, slab_rows), :] = slab_of(k, item, 0, slab_rows)
        base = capacity * height
        for offset, wanted, begin in ((2, 0, 0), (-2, groups - 1, slab_rows - REACH)):
            for r in range(capacity):
                item = item_at(offset, r)
                block = slab_of(0, item, begin, REACH)
                for k in range(1, groups):
                    block = jnp.where(sources[k] == wanted, slab_of(k, item, begin, REACH), block)
                out[base : base + REACH, :] = block
                base += REACH
        out[base:, :] = splat_rows(metas, out.shape[0] - base, width)


def pack(slabs, rows_of, cols_of, slab_rows, tile_count, strip_rows, capacity):
    groups = len(slabs)
    width = slabs[0].shape[1]
    meta_rows = -(-6 * capacity // 16) * 16
    length = capacity * (slab_rows * groups + 2 * REACH) + meta_rows
    slots = (tile_count + 4) * capacity
    return pl.pallas_call(
        functools.partial(
            pack_kernel,
            groups=groups,
            tile_count=tile_count,
            strip_rows=strip_rows,
            capacity=capacity,
            slab_rows=slab_rows,
        ),
        out_shape=[jax.ShapeDtypeStruct((length, width), BF)] * tile_count,
        in_specs=[pl.BlockSpec(memory_space=pltpu.SMEM)] * 2
        + [pl.BlockSpec(memory_space=pltpu.VMEM)] * groups,
        out_specs=[pl.BlockSpec(memory_space=pltpu.VMEM)] * tile_count,
        scratch_shapes=[pltpu.SMEM((slots,), jnp.int32)] * 3,
        compiler_params=GRANT,
        name="pack",
    )(rows_of, cols_of, slabs[0], *[near(slab) for slab in slabs[1:]])


def hi_lo(block):
    high = block.astype(BF)
    return high, (block - high.astype(F32)).astype(BF)


def place_kernel(measured_ref, after_ref, *refs, tilts, strip_rows, height, capacity, tile_count):
    parcels = refs[:tile_count]
    canvas_ref, next_ref, prev_ref, placed, onehot = refs[tile_count:]
    _, width = parcels[0].shape
    rows, image_width = canvas_ref.shape[1:]
    column = iota_apart((width, image_width), 1, 0)
    apart = iota_apart((rows, height), 0, 1)
    edge_apart = iota_apart((REACH, REACH), 0, 1)
    base = capacity * height
    meta = base + 2 * capacity * REACH

    def spread_out(parcel, begin, size, q):
        left = parcel[meta + 2 * q + 1 : meta + 2 * q + 2, :1]
        picks = ones_where(column == left)
        return jnp.dot(parcel[begin : begin + size, :], picks, preferred_element_type=F32).astype(BF)

    def row_of(parcel, q, t):
        own = parcel[meta + 2 * q : meta + 2 * q + 1, :].astype(F32) - float(t * strip_rows)
        return jnp.where((own >= 0) & (own < strip_rows), own, float(ABSENT))

    index = 0
    for parcel in parcels:
        for r in range(capacity):
            placed[index * height : (index + 1) * height, :] = spread_out(parcel, r * height, height, r)
            for t in range(tilts):
                target = (row_of(parcel, r, t) + float(REACH)).astype(BF)
                onehot[t * rows : (t + 1) * rows, index * height : (index + 1) * height] = (
                    ones_where(apart == target)
                )
            index += 1
    total = jnp.dot(onehot[...], placed[...], preferred_element_type=F32)
    for t in range(tilts):
        canvas_ref[t] = total[t * rows : (t + 1) * rows]
    for side in range(2):
        blocks = [[] for _ in range(tilts)]
        values = []
        for parcel in parcels:
            for r in range(capacity):
                q = (1 + side) * capacity + r
                begin = base + side * capacity * REACH + r * REACH
                values.append(spread_out(parcel, begin, REACH, q))
                for t in range(tilts):
                    target = row_of(parcel, q, t)[:, :REACH]
                    if side == 1:
                        target = target + float(height - 2 * strip_rows)
                    blocks[t].append(ones_where(edge_apart == target.astype(BF)))
        tall = jnp.concatenate(values, axis=0)
        for t in range(tilts):
            picks = jnp.concatenate(blocks[t], axis=1)
            edge = jnp.dot(picks, tall, preferred_element_type=F32)
            begin = rows - REACH if side == 0 else 0
            canvas_ref[t, begin : begin + REACH, :] = edge
    reach = strip_rows + REACH
    for t in range(tilts):
        next_ref[t, :reach, :] = canvas_ref[t, strip_rows : strip_rows + reach, :].astype(BF)
        prev_ref[t, :reach, :] = canvas_ref[t, REACH : REACH + reach, :].astype(BF)
        high, low = hi_lo(measured_ref[t, strip_rows - HR :, :])
        next_ref[t, reach:, :] = jnp.concatenate([high, low], axis=0)
        high, low = hi_lo(after_ref[t, :HR, :])
        prev_ref[t, reach:, :] = jnp.concatenate([high, low], axis=0)


def place(measured, after, parcels, height, capacity):
    tilts, strip_rows, image_width = measured.shape
    tile_count = len(parcels)
    rows = 2 * strip_rows + 2 * REACH
    halo = strip_rows + REACH + 2 * HR
    whole = pl.BlockSpec(memory_space=pltpu.VMEM)
    return pl.pallas_call(
        functools.partial(
            place_kernel,
            tilts=tilts,
            strip_rows=strip_rows,
            height=height,
            capacity=capacity,
            tile_count=tile_count,
        ),
        out_shape=[
            jax.ShapeDtypeStruct((tilts, rows, image_width), F32),
            jax.ShapeDtypeStruct((tilts, halo, image_width), BF),
            jax.ShapeDtypeStruct((tilts, halo, image_width), BF),
        ],
        in_specs=[whole] * (2 + tile_count),
        out_specs=[whole] * 3,
        scratch_shapes=[
            pltpu.VMEM((tile_count * capacity * height, image_width), BF),
            pltpu.VMEM((tilts * rows, tile_count * capacity * height), BF),
        ],
        compiler_params=GRANT,
        name="place",
    )(measured, near(after), parcels[0], *[near(p) for p in parcels[1:]])


def transfer_kernel(defocus_ref, out_ref):
    tilts, _, image_width, _ = out_ref.shape
    lanes = 128
    row = lax.broadcasted_iota(jnp.int32, (8, lanes), 0)
    lane = lax.broadcasted_iota(jnp.int32, (8, lanes), 1)
    down = lax.broadcasted_iota(jnp.int32, (8, lanes), 0)
    for t in range(tilts):
        for i in range(HR + 1):
            rho_sq = (i * i + lane * lane).astype(F32)
            value = jnp.exp(-rho_sq / (2.0 * HR * HR)) * jnp.cos(defocus_ref[t] * rho_sq) / float(HR * HR)
            value = jnp.where(lane <= HR, value, 0.0)
            for begin in range(0, image_width, 16):
                for column in range(0, image_width, lanes):
                    if begin - column > lanes + HR or column - begin > 16 + HR:
                        out_ref[t, i, begin : begin + 16, column : column + lanes] = jnp.zeros(
                            (16, lanes), BF
                        )
                        continue
                    parts = []
                    for half in range(2):
                        apart = jnp.abs(down + (begin + 8 * half - column) - lane)
                        parts.append(
                            jnp.take_along_axis(value, jnp.minimum(apart, lanes - 1), axis=1)
                        )
                    out_ref[t, i, begin : begin + 16, column : column + lanes] = jnp.concatenate(
                        parts, axis=0
                    ).astype(BF)


def transfer_tables(defocus, image_width):
    return pl.pallas_call(
        transfer_kernel,
        out_shape=jax.ShapeDtypeStruct((defocus.shape[0], HR + 1, image_width, image_width), BF),
        in_specs=[pl.BlockSpec(memory_space=pltpu.SMEM)],
        out_specs=pl.BlockSpec(memory_space=pltpu.VMEM),
        compiler_params=GRANT,
        name="transfer",
    )(defocus)


def convolve(source, parts, table_ref, t, height):
    rows = source.shape[0]
    for i in range(HR + 1):
        parts[i, :rows, :] = jnp.dot(source, table_ref[t, i], preferred_element_type=F32)
    total = parts[0, HR : HR + height, :]
    for i in range(1, HR + 1):
        total = total + (
            parts[i, HR + i : HR + i + height, :] + parts[i, HR - i : HR - i + height, :]
        )
    return total


def filter_kernel(
    canvas_ref, above_ref, below_ref, measured_ref, after_ref, table_ref, *refs, height, capacity
):
    tile_count = len(refs) - 4
    parcels, (residual_ref, out_ref, parts, back) = refs[:tile_count], refs[tile_count:]
    groups = out_ref.shape[0]
    slab_rows = height // groups
    tilts, strip_rows, image_width = measured_ref.shape
    rows = canvas_ref.shape[1]
    my_tile = lax.axis_index("tile")
    first = my_tile * strip_rows
    image_rows = tile_count * strip_rows
    reach = strip_rows + REACH

    def inside(count, start):
        at = lax.broadcasted_iota(jnp.int32, (count, image_width), 0) + (first + start)
        return (at >= 0) & (at < image_rows)

    at_top, at_end = my_tile == 0, my_tile == tile_count - 1
    for t in range(tilts):
        upper = jnp.where(at_top, 0.0, above_ref[t, :reach, :].astype(F32))
        lower = jnp.where(at_end, 0.0, below_ref[t, :reach, :].astype(F32))
        field = canvas_ref[t] + jnp.concatenate([upper, lower], axis=0)
        field = jnp.where(inside(rows, -REACH), field, 0.0)
        known = jnp.concatenate(
            [
                above_ref[t, reach : reach + HR, :].astype(F32)
                + above_ref[t, reach + HR :, :].astype(F32),
                measured_ref[t],
                after_ref[t],
                below_ref[t, reach : reach + HR, :].astype(F32)
                + below_ref[t, reach + HR :, :].astype(F32),
            ],
            axis=0,
        )
        count = rows - 2 * HR
        rest = known - convolve(field.astype(BF), parts, table_ref, t, count)
        residual_ref[t] = rest[HR : HR + strip_rows]
        rest = jnp.where(inside(count, -HR), rest, 0.0)
        count -= 2 * HR
        image = convolve(rest.astype(BF), parts, table_ref, t, count)
        back[t * count : (t + 1) * count, :] = jnp.where(inside(count, 0), image, 0.0).astype(BF)
    width = parcels[0].shape[1]
    count = 2 * strip_rows
    apart = iota_apart((height, count), 1, 0)
    column = iota_apart((image_width, width), 0, 1)
    meta = capacity * (height + 2 * REACH)
    for d, parcel in enumerate(parcels):
        sender = lax.rem(my_tile + tile_count - d, tile_count)
        for r in range(capacity):
            top = parcel[meta + 2 * r : meta + 2 * r + 1, :].astype(F32)
            picks = []
            for t in range(tilts):
                own = top - float(t * strip_rows)
                own = jnp.where((own >= 0) & (own < strip_rows), own, float(ABSENT)).astype(BF)
                picks.append(ones_where(apart == own[:, :1]))
            cut = jnp.dot(
                jnp.concatenate(picks, axis=1), back[...], preferred_element_type=F32
            ).astype(BF)
            left = parcel[meta + 2 * r + 1 : meta + 2 * r + 2, :]
            columns = ones_where(column == left)
            window = jnp.dot(cut, columns, preferred_element_type=F32).astype(BF)
            for i in range(groups):
                out_ref[i, sender, r * slab_rows : (r + 1) * slab_rows, :] = window[
                    i * slab_rows : (i + 1) * slab_rows
                ]


def filter_and_cut(canvas, above, below, measured, after, table, parcels, height, capacity, groups):
    tilts, strip_rows, image_width = measured.shape
    tile_count = len(parcels)
    width = parcels[0].shape[1]
    rows = canvas.shape[1]
    whole = pl.BlockSpec(memory_space=pltpu.VMEM)
    slots = (groups, tile_count, capacity * height // groups, width)
    return pl.pallas_call(
        functools.partial(filter_kernel, height=height, capacity=capacity),
        out_shape=[jax.ShapeDtypeStruct(measured.shape, F32), jax.ShapeDtypeStruct(slots, BF)],
        in_specs=[whole] * (6 + tile_count),
        out_specs=[whole] * 2,
        scratch_shapes=[
            pltpu.VMEM((HR + 1, rows, image_width), F32),
            pltpu.VMEM((tilts * 2 * strip_rows, image_width), BF),
        ],
        compiler_params=GRANT,
        name="filter_and_cut",
    )(near(canvas), near(above), near(below), measured, near(after), near(table), parcels[0], *[near(p) for p in parcels[1:]])


def shards(volumes, angles, defocus, row_offsets, col_offsets, measured):
    boxes, slab_rows, depth, width = volumes.shape
    tilts, strip_rows, image_width = measured.shape
    tile_count, groups = lax.axis_size("tile"), lax.axis_size("tilt")
    height, rows = slab_rows * groups, boxes * slab_rows
    capacity = max(2, -(-boxes * tilts // tile_count))
    assert tilts * strip_rows <= 256 and tile_count * capacity <= 256
    rows_of, cols_of, angles = far(row_offsets.T), far(col_offsets.T), far(angles)
    after = ring(measured, "tile", -1)
    kernel = transfer_tables(defocus, image_width)
    slabs = [None] * groups
    volume = far(volumes.reshape(rows, depth, width))
    half = groups // 2 + 1
    early, middle = tuple(range(1, half)), tuple(range(half, groups))
    sizes = (depth, width, strip_rows, capacity)
    *parts, flat = project(volume, rows_of, angles, tilts, groups, early, True, *sizes)
    for k, part in zip(early, parts, strict=True):
        slabs[k] = swap(part, "tilt", k)
    if middle:
        parts = project(flat, rows_of, angles, tilts, groups, middle, False, *sizes)
        for k, part in zip(middle, parts, strict=True):
            slabs[k] = swap(part, "tilt", k)
    (slabs[0],) = project(flat, rows_of, angles, tilts, groups, (0,), False, *sizes)
    parcels = pack(slabs, rows_of, cols_of, slab_rows, tile_count, strip_rows, capacity)
    parcels = [p if d == 0 else ring(p, "tile", d) for d, p in enumerate(parcels)]
    canvas, onward, backward = place(measured, after, parcels, height, capacity)
    above, below = ring(onward, "tile", 1), ring(backward, "tile", -1)
    residual, cuts = filter_and_cut(
        canvas, above, below, measured, after, kernel, parcels, height, capacity, groups
    )
    cuts = cuts.reshape(groups * tile_count, capacity * slab_rows, width)
    cuts = lax.all_to_all(cuts, ("tilt", "tile"), split_axis=0, concat_axis=0, tiled=True)
    cuts = cuts.reshape(groups, tile_count * capacity * slab_rows, width)
    step = back_project(cuts, slabs, angles, boxes, tilts, rows, depth, 1.0 / (tilts * groups))
    return residual, step.reshape(boxes, slab_rows, depth, width)


def solution(mesh):
    in_specs = (
        P("tile", "tilt", None, None),
        P(),
        P("tilt"),
        P("tile", "tilt"),
        P("tile", "tilt"),
        P("tilt", "tile", None),
    )
    out_specs = (P("tilt", "tile", None), P("tile", "tilt", None, None))

    return jax.shard_map(shards, mesh=mesh, in_specs=in_specs, out_specs=out_specs, check_vma=False)
```

```python
import functools

import jax
import jax.numpy as jnp
from jax import lax
from jax.experimental import pallas as pl
from jax.experimental.pallas import tpu as pltpu
from jax.sharding import PartitionSpec as P

HR = 8
REACH = 2 * HR
BF = jnp.bfloat16
F32 = jnp.float32
ABSENT = -1024
GRANT = pltpu.CompilerParams(vmem_limit_bytes=32 * 1024 * 1024)


def ring(block, axis, distance):
    count = lax.axis_size(axis)
    return lax.ppermute(block, axis, [(i, (i + distance) % count) for i in range(count)])


def swap(block, axis, distance):
    count = lax.axis_size(axis)
    assert count & (count - 1) == 0
    return lax.ppermute(block, axis, [(i, i ^ distance) for i in range(count)])


def far(block):
    return pltpu.with_memory_space_constraint(block, pltpu.HBM)


def near(block):
    return pltpu.with_memory_space_constraint(block, pltpu.VMEM)


def quotient(value, size):
    if size & (size - 1) == 0:
        return lax.shift_right_logical(value, size.bit_length() - 1)
    return lax.div(value, size)


def ones_where(mask):
    return jnp.where(mask, jnp.ones(mask.shape, BF), jnp.zeros(mask.shape, BF))


def iota_apart(shape, plus, minus):
    ahead = lax.broadcasted_iota(jnp.int32, shape, plus)
    behind = lax.broadcasted_iota(jnp.int32, shape, minus)
    return (ahead - behind).astype(F32).astype(BF)


def note_sines(angle_ref, sine_ref):
    for t in range(sine_ref.shape[0]):
        sine_ref[t] = jnp.sin(jnp.full(sine_ref.shape[1:], angle_ref[t], F32))


def tap_block(apart, sine, layer, depth):
    shift = (layer.astype(F32) - (depth - 1) / 2.0) * sine
    lower = jnp.floor(shift)
    copies = apart.shape[0] // (2 * sine.shape[0])

    def filled(value):
        return jnp.concatenate([jnp.concatenate([value] * 2, axis=0).astype(BF)] * copies, axis=0)

    def weight(offset):
        return filled(jnp.maximum(0.0, 1.0 - jnp.abs(offset - shift)))

    beyond = jnp.where(
        apart == filled(lower + 1.0), weight(lower + 1.0), jnp.zeros(apart.shape, BF)
    )
    return jnp.where(apart == filled(lower), weight(lower), beyond)


def slots_of_items(row_ref, strip_rows, capacity):
    tilts, boxes = row_ref.shape
    strips = [quotient(row_ref[t, b], strip_rows) for t in range(tilts) for b in range(boxes)]
    slots = []
    for n, strip in enumerate(strips):
        place = strip * capacity
        for other in strips[:n]:
            place = place + jnp.where(other == strip, 1, 0)
        slots.append(place)
    return strips, slots


def splat_rows(values, rows, width):
    row_at = lax.broadcasted_iota(jnp.int32, (rows, width), 0)
    block = jnp.zeros((rows, width), F32)
    for i, value in enumerate(values):
        block = jnp.where(row_at == i, value.astype(F32), block)
    return block.astype(BF)


def add_products(step, pair_at, total, sines, ks, tilts, layers, depth):
    width = sines.shape[2]
    me = lax.axis_index("tilt")
    apart = iota_apart((width, width), 1, 0)

    def block(k, z, t):
        return tap_block(apart, sines[(me ^ k) * tilts + t], step * layers + z, depth)

    following = pair_at(0)
    for z in range(0, layers, 2):
        pair = following
        if z + 2 < layers:
            following = pair_at(z + 2)
        for i, k in enumerate(ks):
            table = jnp.concatenate(
                [
                    jnp.concatenate([block(k, z + half, t) for t in range(tilts)], axis=1)
                    for half in range(2)
                ],
                axis=0,
            )
            span = slice(i * tilts * width, (i + 1) * tilts * width)
            total[:, span] += jnp.dot(pair, table, preferred_element_type=F32)


def write_slabs(row_ref, total, outs, tilts, strip_rows, capacity):
    rows, width = total.shape[0], outs[0].shape[1]
    _, slots = slots_of_items(row_ref, strip_rows, capacity)
    meta = splat_rows(slots, outs[0].shape[0] - tilts * rows, width)
    for i, out in enumerate(outs):
        for t in range(tilts):
            start = (i * tilts + t) * width
            out[t * rows : (t + 1) * rows, :] = total[:, start : start + width].astype(BF)
        out[tilts * rows :, :] = meta


def project_first_kernel(
    row_ref, angle_ref, vol_ref, *refs, depth, tilts, ks, strip_rows, capacity
):
    outs, (lhs, wide, total, sines) = refs[: len(ks)], refs[len(ks) :]
    step = pl.program_id(0)
    rows, layers, width = vol_ref.shape
    wide[...] = vol_ref[...].reshape(rows * layers, width).astype(F32)

    def pair_at(z):
        pair = [wide[pl.ds(z + h, rows, stride=layers), :].astype(BF) for h in range(2)]
        pair = jnp.concatenate(pair, axis=1)
        lhs[:, z * width : (z + 2) * width] = pair
        return pair

    @pl.when(step == 0)
    def _():
        total[...] = jnp.zeros_like(total)
        note_sines(angle_ref, sines)

    add_products(step, pair_at, total, sines, ks, tilts, layers, depth)

    @pl.when(step == pl.num_programs(0) - 1)
    def _():
        write_slabs(row_ref, total, outs, tilts, strip_rows, capacity)


def project_rest_kernel(
    row_ref, angle_ref, lhs, *refs, depth, tilts, ks, layers, strip_rows, capacity
):
    outs, (total, sines) = refs[: len(ks)], refs[len(ks) :]
    width = sines.shape[2]
    total[...] = jnp.zeros_like(total)
    note_sines(angle_ref, sines)

    def some_layers(step, carry):
        def pair_at(z):
            start = pl.multiple_of((step * layers + z) * width, 2 * width)
            return lhs[:, pl.ds(start, 2 * width)]

        add_products(step, pair_at, total, sines, ks, tilts, layers, depth)
        return carry

    lax.fori_loop(0, depth // layers, some_layers, 0)
    write_slabs(row_ref, total, outs, tilts, strip_rows, capacity)


def project(volume, rows_of, angles, tilts, groups, ks, first, depth, width, strip_rows, capacity):
    rows = volume.shape[0]
    layers = min(16, depth)
    length = tilts * rows + -(-tilts * rows_of.shape[1] // 16) * 16
    scalars = pl.BlockSpec(memory_space=pltpu.SMEM)
    whole = pl.BlockSpec(memory_space=pltpu.VMEM)
    sizes = dict(depth=depth, tilts=tilts, ks=ks, strip_rows=strip_rows, capacity=capacity)
    slabs = [jax.ShapeDtypeStruct((length, width), BF)] * len(ks)
    sums = [
        pltpu.VMEM((rows, len(ks) * tilts * width), F32),
        pltpu.VMEM((groups * tilts, 8, width), F32),
    ]
    if not first:
        return pl.pallas_call(
            functools.partial(project_rest_kernel, layers=layers, **sizes),
            out_shape=slabs,
            in_specs=[scalars] * 2 + [whole],
            out_specs=[whole] * len(ks),
            scratch_shapes=sums,
            compiler_params=GRANT,
            name="project_rest",
        )(rows_of, angles, near(volume))
    return pl.pallas_call(
        functools.partial(project_first_kernel, **sizes),
        out_shape=slabs + [jax.ShapeDtypeStruct((rows, depth * width), BF)],
        grid=(depth // layers,),
        in_specs=[scalars] * 2 + [pl.BlockSpec((rows, layers, width), lambda i: (0, i, 0))],
        out_specs=[pl.BlockSpec((length, width), lambda i: (0, 0))] * len(ks)
        + [pl.BlockSpec((rows, layers * width), lambda i: (0, i))],
        scratch_shapes=[pltpu.VMEM((rows * layers, width), F32), *sums],
        compiler_params=GRANT,
        name="project_first",
    )(rows_of, angles, volume)


def back_kernel(
    angle_ref, cut_ref, *refs, depth, tilts, boxes, groups, scale
):
    metas, (out_ref, lhs, sines) = refs[:groups], refs[groups:]
    step = pl.program_id(0)
    me = lax.axis_index("tilt")
    rows, layers, width = out_ref.shape
    slab_rows, length = rows // boxes, cut_ref.shape[1]
    apart = iota_apart((width, width), 0, 1)

    @pl.when(step == 0)
    def _():
        note_sines(angle_ref, sines)
        ahead = lax.broadcasted_iota(jnp.int32, (slab_rows, length), 1)
        ahead = (ahead - lax.broadcasted_iota(jnp.int32, (slab_rows, length), 0)).astype(F32)
        for k in range(groups):
            group = (me ^ k)
            for t in range(tilts):
                picks = []
                for b in range(boxes):
                    slot = metas[k][t * boxes + b : t * boxes + b + 1, :1].astype(F32)
                    picks.append(ones_where(ahead == slot * float(slab_rows)))
                start = (k * tilts + t) * width
                lhs[:, start : start + width] = jnp.dot(
                    jnp.concatenate(picks, axis=0), cut_ref[group], preferred_element_type=F32
                ).astype(BF)

    def block(k, t, z):
        sine = sines[(me ^ k) * tilts + t]
        return tap_block(apart, sine, step * layers + z, depth)

    flat = out_ref.reshape(rows * layers, width)
    for z in range(0, layers, 2):
        table = jnp.concatenate(
            [
                jnp.concatenate([block(k, t, z + half) for half in range(2)], axis=1)
                for k in range(groups)
                for t in range(tilts)
            ],
            axis=0,
        )
        result = jnp.dot(lhs[...], table, preferred_element_type=F32) * scale
        for half in range(2):
            flat[pl.ds(z + half, rows, stride=layers), :] = result[
                :, half * width : (half + 1) * width
            ]


def back_project(cuts, slabs, angles, boxes, tilts, rows, depth, scale):
    groups, _, width = cuts.shape
    layers = min(8, depth)
    meta = slabs[0].shape[0] - tilts * rows
    at = tilts * rows // meta
    scalars = pl.BlockSpec(memory_space=pltpu.SMEM)
    return pl.pallas_call(
        functools.partial(
            back_kernel, depth=depth, tilts=tilts, boxes=boxes, groups=groups, scale=scale
        ),
        out_shape=jax.ShapeDtypeStruct((rows, depth, width), F32),
        grid=(depth // layers,),
        in_specs=[scalars]
        + [pl.BlockSpec(cuts.shape, lambda i: (0, 0, 0))]
        + [pl.BlockSpec((meta, width), lambda i: (at, 0))] * groups,
        out_specs=pl.BlockSpec((rows, layers, width), lambda i: (0, i, 0)),
        scratch_shapes=[
            pltpu.VMEM((rows, groups * tilts * width), BF),
            pltpu.VMEM((groups * tilts, 8, width), F32),
        ],
        compiler_params=GRANT,
        name="back_project",
    )(angles, cuts, *slabs)


def pack_kernel(row_ref, col_ref, *refs, groups, tile_count, strip_rows, capacity, slab_rows):
    slabs, outs = refs[:groups], refs[groups : groups + tile_count]
    item_ref, within_ref, left_ref = refs[groups + tile_count :]
    _, boxes = row_ref.shape
    width = slabs[0].shape[1]
    height = slab_rows * groups
    my_tilt, my_tile = lax.axis_index("tilt"), lax.axis_index("tile")
    strips, slots = slots_of_items(row_ref, strip_rows, capacity)
    margin = 2 * capacity

    def clear(i, carry):
        item_ref[i] = -1
        within_ref[i] = ABSENT
        left_ref[i] = 0
        return carry

    lax.fori_loop(0, tile_count * capacity + 2 * margin, clear, 0)
    for n, (strip, slot) in enumerate(zip(strips, slots, strict=True)):
        t, b = n // boxes, n % boxes
        item_ref[slot + margin] = n
        within_ref[slot + margin] = row_ref[t, b] - strip * strip_rows + t * strip_rows
        left_ref[slot + margin] = col_ref[t, b]
    sources = [my_tilt ^ k for k in range(groups)]

    def slab_of(k, item, begin, size):
        start = pl.multiple_of(jnp.maximum(item, 0) * slab_rows + begin, 16)
        block = slabs[k][pl.ds(start, size), :]
        return jnp.where(item >= 0, block, jnp.zeros_like(block))

    for d in range(tile_count):
        out = outs[d]
        strip = lax.rem(my_tile + d, tile_count)
        metas = []

        def item_at(offset, r):
            spot = (strip + offset + 2) * capacity + r
            metas.append(within_ref[spot])
            metas.append(left_ref[spot])
            return item_ref[spot]

        for r in range(capacity):
            item = item_at(0, r)
            for k in range(groups):
                begin = pl.multiple_of(r * height + sources[k] * slab_rows, slab_rows)
                out[pl.ds(begin, slab_rows), :] = slab_of(k, item, 0, slab_rows)
        base = capacity * height
        for offset, wanted, begin in ((2, 0, 0), (-2, groups - 1, slab_rows - REACH)):
            for r in range(capacity):
                item = item_at(offset, r)
                block = slab_of(0, item, begin, REACH)
                for k in range(1, groups):
                    block = jnp.where(sources[k] == wanted, slab_of(k, item, begin, REACH), block)
                out[base : base + REACH, :] = block
                base += REACH
        out[base:, :] = splat_rows(metas, out.shape[0] - base, width)


def pack(slabs, rows_of, cols_of, slab_rows, tile_count, strip_rows, capacity):
    groups = len(slabs)
    width = slabs[0].shape[1]
    meta_rows = -(-6 * capacity // 16) * 16
    length = capacity * (slab_rows * groups + 2 * REACH) + meta_rows
    slots = (tile_count + 4) * capacity
    return pl.pallas_call(
        functools.partial(
            pack_kernel,
            groups=groups,
            tile_count=tile_count,
            strip_rows=strip_rows,
            capacity=capacity,
            slab_rows=slab_rows,
        ),
        out_shape=[jax.ShapeDtypeStruct((length, width), BF)] * tile_count,
        in_specs=[pl.BlockSpec(memory_space=pltpu.SMEM)] * 2
        + [pl.BlockSpec(memory_space=pltpu.VMEM)] * groups,
        out_specs=[pl.BlockSpec(memory_space=pltpu.VMEM)] * tile_count,
        scratch_shapes=[pltpu.SMEM((slots,), jnp.int32)] * 3,
        compiler_params=GRANT,
        name="pack",
    )(rows_of, cols_of, slabs[0], *[near(slab) for slab in slabs[1:]])


def hi_lo(block):
    high = block.astype(BF)
    return high, (block - high.astype(F32)).astype(BF)


def place_kernel(measured_ref, after_ref, *refs, tilts, strip_rows, height, capacity, tile_count):
    parcels = refs[:tile_count]
    canvas_ref, next_ref, prev_ref, placed, onehot = refs[tile_count:]
    _, width = parcels[0].shape
    rows, image_width = canvas_ref.shape[1:]
    column = iota_apart((width, image_width), 1, 0)
    apart = iota_apart((rows, height), 0, 1)
    edge_apart = iota_apart((REACH, REACH), 0, 1)
    base = capacity * height
    meta = base + 2 * capacity * REACH

    def spread_out(parcel, begin, size, q):
        left = parcel[meta + 2 * q + 1 : meta + 2 * q + 2, :1]
        picks = ones_where(column == left)
        return jnp.dot(parcel[begin : begin + size, :], picks, preferred_element_type=F32).astype(BF)

    def row_of(parcel, q, t):
        own = parcel[meta + 2 * q : meta + 2 * q + 1, :].astype(F32) - float(t * strip_rows)
        return jnp.where((own >= 0) & (own < strip_rows), own, float(ABSENT))

    index = 0
    for parcel in parcels:
        for r in range(capacity):
            placed[index * height : (index + 1) * height, :] = spread_out(parcel, r * height, height, r)
            for t in range(tilts):
                target = (row_of(parcel, r, t) + float(REACH)).astype(BF)
                onehot[t * rows : (t + 1) * rows, index * height : (index + 1) * height] = (
                    ones_where(apart == target)
                )
            index += 1
    total = jnp.dot(onehot[...], placed[...], preferred_element_type=F32)
    for t in range(tilts):
        canvas_ref[t] = total[t * rows : (t + 1) * rows]
    for side in range(2):
        blocks = [[] for _ in range(tilts)]
        values = []
        for parcel in parcels:
            for r in range(capacity):
                q = (1 + side) * capacity + r
                begin = base + side * capacity * REACH + r * REACH
                values.append(spread_out(parcel, begin, REACH, q))
                for t in range(tilts):
                    target = row_of(parcel, q, t)[:, :REACH]
                    if side == 1:
                        target = target + float(height - 2 * strip_rows)
                    blocks[t].append(ones_where(edge_apart == target.astype(BF)))
        tall = jnp.concatenate(values, axis=0)
        for t in range(tilts):
            picks = jnp.concatenate(blocks[t], axis=1)
            edge = jnp.dot(picks, tall, preferred_element_type=F32)
            begin = rows - REACH if side == 0 else 0
            canvas_ref[t, begin : begin + REACH, :] = edge
    reach = strip_rows + REACH
    for t in range(tilts):
        next_ref[t, :reach, :] = canvas_ref[t, strip_rows : strip_rows + reach, :].astype(BF)
        prev_ref[t, :reach, :] = canvas_ref[t, REACH : REACH + reach, :].astype(BF)
        high, low = hi_lo(measured_ref[t, strip_rows - HR :, :])
        next_ref[t, reach:, :] = jnp.concatenate([high, low], axis=0)
        high, low = hi_lo(after_ref[t, :HR, :])
        prev_ref[t, reach:, :] = jnp.concatenate([high, low], axis=0)


def place(measured, after, parcels, height, capacity):
    tilts, strip_rows, image_width = measured.shape
    tile_count = len(parcels)
    rows = 2 * strip_rows + 2 * REACH
    halo = strip_rows + REACH + 2 * HR
    whole = pl.BlockSpec(memory_space=pltpu.VMEM)
    return pl.pallas_call(
        functools.partial(
            place_kernel,
            tilts=tilts,
            strip_rows=strip_rows,
            height=height,
            capacity=capacity,
            tile_count=tile_count,
        ),
        out_shape=[
            jax.ShapeDtypeStruct((tilts, rows, image_width), F32),
            jax.ShapeDtypeStruct((tilts, halo, image_width), BF),
            jax.ShapeDtypeStruct((tilts, halo, image_width), BF),
        ],
        in_specs=[whole] * (2 + tile_count),
        out_specs=[whole] * 3,
        scratch_shapes=[
            pltpu.VMEM((tile_count * capacity * height, image_width), BF),
            pltpu.VMEM((tilts * rows, tile_count * capacity * height), BF),
        ],
        compiler_params=GRANT,
        name="place",
    )(measured, near(after), parcels[0], *[near(p) for p in parcels[1:]])


def transfer_kernel(defocus_ref, out_ref):
    tilts, _, image_width, _ = out_ref.shape
    lanes = 128
    row = lax.broadcasted_iota(jnp.int32, (8, lanes), 0)
    lane = lax.broadcasted_iota(jnp.int32, (8, lanes), 1)
    down = lax.broadcasted_iota(jnp.int32, (8, lanes), 0)
    for t in range(tilts):
        for i in range(HR + 1):
            rho_sq = (i * i + lane * lane).astype(F32)
            value = jnp.exp(-rho_sq / (2.0 * HR * HR)) * jnp.cos(defocus_ref[t] * rho_sq) / float(HR * HR)
            value = jnp.where(lane <= HR, value, 0.0)
            for begin in range(0, image_width, 16):
                for column in range(0, image_width, lanes):
                    if begin - column > lanes + HR or column - begin > 16 + HR:
                        out_ref[t, i, begin : begin + 16, column : column + lanes] = jnp.zeros(
                            (16, lanes), BF
                        )
                        continue
                    parts = []
                    for half in range(2):
                        apart = jnp.abs(down + (begin + 8 * half - column) - lane)
                        parts.append(
                            jnp.take_along_axis(value, jnp.minimum(apart, lanes - 1), axis=1)
                        )
                    out_ref[t, i, begin : begin + 16, column : column + lanes] = jnp.concatenate(
                        parts, axis=0
                    ).astype(BF)


def transfer_tables(defocus, image_width):
    return pl.pallas_call(
        transfer_kernel,
        out_shape=jax.ShapeDtypeStruct((defocus.shape[0], HR + 1, image_width, image_width), BF),
        in_specs=[pl.BlockSpec(memory_space=pltpu.SMEM)],
        out_specs=pl.BlockSpec(memory_space=pltpu.VMEM),
        compiler_params=GRANT,
        name="transfer",
    )(defocus)


def convolve(source, parts, table_ref, t, height):
    rows = source.shape[0]
    for i in range(HR + 1):
        parts[i, :rows, :] = jnp.dot(source, table_ref[t, i], preferred_element_type=F32)
    total = parts[0, HR : HR + height, :]
    for i in range(1, HR + 1):
        total = total + (
            parts[i, HR + i : HR + i + height, :] + parts[i, HR - i : HR - i + height, :]
        )
    return total


def filter_kernel(
    canvas_ref, above_ref, below_ref, measured_ref, after_ref, table_ref, *refs, height, capacity
):
    tile_count = len(refs) - 4
    parcels, (residual_ref, out_ref, parts, back) = refs[:tile_count], refs[tile_count:]
    groups = out_ref.shape[0]
    slab_rows = height // groups
    tilts, strip_rows, image_width = measured_ref.shape
    rows = canvas_ref.shape[1]
    my_tile = lax.axis_index("tile")
    first = my_tile * strip_rows
    image_rows = tile_count * strip_rows
    reach = strip_rows + REACH

    def inside(count, start):
        at = lax.broadcasted_iota(jnp.int32, (count, image_width), 0) + (first + start)
        return (at >= 0) & (at < image_rows)

    at_top, at_end = my_tile == 0, my_tile == tile_count - 1
    for t in range(tilts):
        upper = jnp.where(at_top, 0.0, above_ref[t, :reach, :].astype(F32))
        lower = jnp.where(at_end, 0.0, below_ref[t, :reach, :].astype(F32))
        field = canvas_ref[t] + jnp.concatenate([upper, lower], axis=0)
        field = jnp.where(inside(rows, -REACH), field, 0.0)
        known = jnp.concatenate(
            [
                above_ref[t, reach : reach + HR, :].astype(F32)
                + above_ref[t, reach + HR :, :].astype(F32),
                measured_ref[t],
                after_ref[t],
                below_ref[t, reach : reach + HR, :].astype(F32)
                + below_ref[t, reach + HR :, :].astype(F32),
            ],
            axis=0,
        )
        count = rows - 2 * HR
        rest = known - convolve(field.astype(BF), parts, table_ref, t, count)
        residual_ref[t] = rest[HR : HR + strip_rows]
        rest = jnp.where(inside(count, -HR), rest, 0.0)
        count -= 2 * HR
        image = convolve(rest.astype(BF), parts, table_ref, t, count)
        back[t * count : (t + 1) * count, :] = jnp.where(inside(count, 0), image, 0.0).astype(BF)
    width = parcels[0].shape[1]
    count = 2 * strip_rows
    apart = iota_apart((height, count), 1, 0)
    column = iota_apart((image_width, width), 0, 1)
    meta = capacity * (height + 2 * REACH)
    for d, parcel in enumerate(parcels):
        sender = lax.rem(my_tile + tile_count - d, tile_count)
        for r in range(capacity):
            top = parcel[meta + 2 * r : meta + 2 * r + 1, :].astype(F32)
            picks = []
            for t in range(tilts):
                own = top - float(t * strip_rows)
                own = jnp.where((own >= 0) & (own < strip_rows), own, float(ABSENT)).astype(BF)
                picks.append(ones_where(apart == own[:, :1]))
            cut = jnp.dot(
                jnp.concatenate(picks, axis=1), back[...], preferred_element_type=F32
            ).astype(BF)
            left = parcel[meta + 2 * r + 1 : meta + 2 * r + 2, :]
            columns = ones_where(column == left)
            window = jnp.dot(cut, columns, preferred_element_type=F32).astype(BF)
            for i in range(groups):
                out_ref[i, sender, r * slab_rows : (r + 1) * slab_rows, :] = window[
                    i * slab_rows : (i + 1) * slab_rows
                ]


def filter_and_cut(canvas, above, below, measured, after, table, parcels, height, capacity, groups):
    tilts, strip_rows, image_width = measured.shape
    tile_count = len(parcels)
    width = parcels[0].shape[1]
    rows = canvas.shape[1]
    whole = pl.BlockSpec(memory_space=pltpu.VMEM)
    slots = (groups, tile_count, capacity * height // groups, width)
    return pl.pallas_call(
        functools.partial(filter_kernel, height=height, capacity=capacity),
        out_shape=[jax.ShapeDtypeStruct(measured.shape, F32), jax.ShapeDtypeStruct(slots, BF)],
        in_specs=[whole] * (6 + tile_count),
        out_specs=[whole] * 2,
        scratch_shapes=[
            pltpu.VMEM((HR + 1, rows, image_width), F32),
            pltpu.VMEM((tilts * 2 * strip_rows, image_width), BF),
        ],
        compiler_params=GRANT,
        name="filter_and_cut",
    )(near(canvas), near(above), near(below), measured, near(after), near(table), parcels[0], *[near(p) for p in parcels[1:]])


def shards(volumes, angles, defocus, row_offsets, col_offsets, measured):
    boxes, slab_rows, depth, width = volumes.shape
    tilts, strip_rows, image_width = measured.shape
    tile_count, groups = lax.axis_size("tile"), lax.axis_size("tilt")
    height, rows = slab_rows * groups, boxes * slab_rows
    capacity = max(2, -(-boxes * tilts // tile_count))
    assert tilts * strip_rows <= 256 and tile_count * capacity <= 256
    rows_of, cols_of, angles = far(row_offsets.T), far(col_offsets.T), far(angles)
    after = ring(measured, "tile", -1)
    kernel = transfer_tables(defocus, image_width)
    slabs = [None] * groups
    volume = far(volumes.reshape(rows, depth, width))
    half = groups // 2 + 1
    early, middle = tuple(range(1, half)), tuple(range(half, groups))
    sizes = (depth, width, strip_rows, capacity)
    *parts, flat = project(volume, rows_of, angles, tilts, groups, early, True, *sizes)
    for k, part in zip(early, parts, strict=True):
        slabs[k] = swap(part, "tilt", k)
    if middle:
        parts = project(flat, rows_of, angles, tilts, groups, middle, False, *sizes)
        for k, part in zip(middle, parts, strict=True):
            slabs[k] = swap(part, "tilt", k)
    (slabs[0],) = project(flat, rows_of, angles, tilts, groups, (0,), False, *sizes)
    parcels = pack(slabs, rows_of, cols_of, slab_rows, tile_count, strip_rows, capacity)
    parcels = [p if d == 0 else ring(p, "tile", d) for d, p in enumerate(parcels)]
    canvas, onward, backward = place(measured, after, parcels, height, capacity)
    above, below = ring(onward, "tile", 1), ring(backward, "tile", -1)
    residual, cuts = filter_and_cut(
        canvas, above, below, measured, after, kernel, parcels, height, capacity, groups
    )
    cuts = cuts.reshape(groups * tile_count, capacity * slab_rows, width)
    cuts = lax.all_to_all(cuts, ("tilt", "tile"), split_axis=0, concat_axis=0, tiled=True)
    cuts = cuts.reshape(groups, tile_count * capacity * slab_rows, width)
    step = back_project(cuts, slabs, angles, boxes, tilts, rows, depth, 1.0 / (tilts * groups))
    return residual, step.reshape(boxes, slab_rows, depth, width)


def solution(mesh):
    in_specs = (
        P("tile", "tilt", None, None),
        P(),
        P("tilt"),
        P("tile", "tilt"),
        P("tile", "tilt"),
        P("tilt", "tile", None),
    )
    out_specs = (P("tilt", "tile", None), P("tile", "tilt", None, None))

    return jax.shard_map(shards, mesh=mesh, in_specs=in_specs, out_specs=out_specs, check_vma=False)
```

```python
import functools

import jax
import jax.numpy as jnp
from jax import lax
from jax.experimental import pallas as pl
from jax.experimental.pallas import tpu as pltpu
from jax.sharding import PartitionSpec as P

HR = 8
REACH = 2 * HR
BF = jnp.bfloat16
F32 = jnp.float32
ABSENT = -1024
CHUNK = 8
LAYERS = 64
GRANT = pltpu.CompilerParams(vmem_limit_bytes=32 * 1024 * 1024)


def ring(block, axis, distance):
    count = lax.axis_size(axis)
    return lax.ppermute(block, axis, [(i, (i + distance) % count) for i in range(count)])


def swap(block, axis, distance):
    count = lax.axis_size(axis)
    assert count & (count - 1) == 0
    return lax.ppermute(block, axis, [(i, i ^ distance) for i in range(count)])


def far(block):
    return pltpu.with_memory_space_constraint(block, pltpu.HBM)


def near(block):
    return pltpu.with_memory_space_constraint(block, pltpu.VMEM)


def quotient(value, size):
    if size & (size - 1) == 0:
        return lax.shift_right_logical(value, size.bit_length() - 1)
    return lax.div(value, size)


def ones_where(mask):
    return jnp.where(mask, jnp.ones(mask.shape, BF), jnp.zeros(mask.shape, BF))


def iota_apart(shape, plus, minus):
    ahead = lax.broadcasted_iota(jnp.int32, shape, plus)
    behind = lax.broadcasted_iota(jnp.int32, shape, minus)
    return (ahead - behind).astype(F32).astype(BF)


def note_sines(angle_ref, sine_ref):
    count, rows, width = sine_ref.shape
    shape = (-(-count // 8) * 8, width)
    row_at = lax.broadcasted_iota(jnp.int32, shape, 0)
    angles = jnp.zeros(shape, F32)
    for t in range(count):
        angles = jnp.where(row_at == t, angle_ref[t], angles)
    sines = jnp.sin(angles)
    for t in range(count):
        sine_ref[t] = jnp.broadcast_to(sines[t : t + 1], (rows, width))


def tap_block(apart, sine, layer, depth):
    shift = (layer.astype(F32) - (depth - 1) / 2.0) * sine
    lower = jnp.floor(shift)
    copies = apart.shape[0] // (2 * sine.shape[0])

    def filled(value):
        return jnp.concatenate([jnp.concatenate([value] * 2, axis=0).astype(BF)] * copies, axis=0)

    def weight(offset):
        return filled(jnp.maximum(0.0, 1.0 - jnp.abs(offset - shift)))

    beyond = jnp.where(
        apart == filled(lower + 1.0), weight(lower + 1.0), jnp.zeros(apart.shape, BF)
    )
    return jnp.where(apart == filled(lower), weight(lower), beyond)


def slots_of_items(row_ref, strip_rows, capacity):
    tilts, boxes = row_ref.shape
    strips = [quotient(row_ref[t, b], strip_rows) for t in range(tilts) for b in range(boxes)]
    slots = []
    for n, strip in enumerate(strips):
        place = strip * capacity
        for other in strips[:n]:
            place = place + jnp.where(other == strip, 1, 0)
        slots.append(place)
    return strips, slots


def splat_rows(values, rows, width):
    row_at = lax.broadcasted_iota(jnp.int32, (rows, width), 0)
    block = jnp.zeros((rows, width), F32)
    for i, value in enumerate(values):
        block = jnp.where(row_at == i, value.astype(F32), block)
    return block.astype(BF)


def add_products(step, layers_at, total, sines, ks, tilts, layers, depth, chunk):
    width = sines.shape[2]
    me = lax.axis_index("tilt")
    apart = iota_apart((width, width), 1, 0)

    def block(k, z, t):
        return tap_block(apart, sines[(me ^ k) * tilts + t], step * layers + z, depth)

    following = layers_at(0)
    for z in range(0, layers, chunk):
        some = following
        if z + chunk < layers:
            following = layers_at(z + chunk)
        for i, k in enumerate(ks):
            table = jnp.concatenate(
                [
                    jnp.concatenate([block(k, z + n, t) for t in range(tilts)], axis=1)
                    for n in range(chunk)
                ],
                axis=0,
            )
            span = slice(i * tilts * width, (i + 1) * tilts * width)
            total[:, span] += jnp.dot(some, table, preferred_element_type=F32)


def write_slabs(row_ref, total, outs, tilts, strip_rows, capacity):
    rows, width = total.shape[0], outs[0].shape[1]
    _, slots = slots_of_items(row_ref, strip_rows, capacity)
    meta = splat_rows(slots, outs[0].shape[0] - tilts * rows, width)
    for i, out in enumerate(outs):
        for t in range(tilts):
            start = (i * tilts + t) * width
            out[t * rows : (t + 1) * rows, :] = total[:, start : start + width].astype(BF)
        out[tilts * rows :, :] = meta


def project_first_kernel(
    row_ref, angle_ref, vol_ref, *refs, depth, tilts, ks, strip_rows, capacity
):
    outs, (lhs, wide, total, sines) = refs[: len(ks)], refs[len(ks) :]
    step = pl.program_id(0)
    rows, layers, width = vol_ref.shape
    wide[...] = vol_ref[...].reshape(rows * layers, width).astype(F32)

    def pair_at(z):
        pair = [wide[pl.ds(z + h, rows, stride=layers), :].astype(BF) for h in range(2)]
        pair = jnp.concatenate(pair, axis=1)
        lhs[:, z * width : (z + 2) * width] = pair
        return pair

    @pl.when(step == 0)
    def _():
        total[...] = jnp.zeros_like(total)
        note_sines(angle_ref, sines)

    add_products(step, pair_at, total, sines, ks, tilts, layers, depth, 2)

    @pl.when(step == pl.num_programs(0) - 1)
    def _():
        write_slabs(row_ref, total, outs, tilts, strip_rows, capacity)


def project_rest_kernel(
    row_ref, angle_ref, lhs, *refs, depth, tilts, ks, layers, strip_rows, capacity
):
    outs, (total, sines) = refs[: len(ks)], refs[len(ks) :]
    width = sines.shape[2]
    chunk = min(CHUNK, layers)
    total[...] = jnp.zeros_like(total)
    note_sines(angle_ref, sines)

    def some_layers(step, carry):
        def layers_at(z):
            start = pl.multiple_of((step * layers + z) * width, chunk * width)
            return lhs[:, pl.ds(start, chunk * width)]

        add_products(step, layers_at, total, sines, ks, tilts, layers, depth, chunk)
        return carry

    lax.fori_loop(0, depth // layers, some_layers, 0)
    write_slabs(row_ref, total, outs, tilts, strip_rows, capacity)


def project(volume, rows_of, angles, tilts, groups, ks, first, depth, width, strip_rows, capacity):
    rows = volume.shape[0]
    layers = min(16, depth)
    length = tilts * rows + -(-tilts * rows_of.shape[1] // 16) * 16
    scalars = pl.BlockSpec(memory_space=pltpu.SMEM)
    whole = pl.BlockSpec(memory_space=pltpu.VMEM)
    sizes = dict(depth=depth, tilts=tilts, ks=ks, strip_rows=strip_rows, capacity=capacity)
    slabs = [jax.ShapeDtypeStruct((length, width), BF)] * len(ks)
    sums = [
        pltpu.VMEM((rows, len(ks) * tilts * width), F32),
        pltpu.VMEM((groups * tilts, 8, width), F32),
    ]
    if not first:
        return pl.pallas_call(
            functools.partial(project_rest_kernel, layers=min(LAYERS, depth), **sizes),
            out_shape=slabs,
            in_specs=[scalars] * 2 + [whole],
            out_specs=[whole] * len(ks),
            scratch_shapes=sums,
            compiler_params=GRANT,
            name="project_rest",
        )(rows_of, angles, near(volume))
    return pl.pallas_call(
        functools.partial(project_first_kernel, **sizes),
        out_shape=slabs + [jax.ShapeDtypeStruct((rows, depth * width), BF)],
        grid=(depth // layers,),
        in_specs=[scalars] * 2 + [pl.BlockSpec((rows, layers, width), lambda i: (0, i, 0))],
        out_specs=[pl.BlockSpec((length, width), lambda i: (0, 0))] * len(ks)
        + [pl.BlockSpec((rows, layers * width), lambda i: (0, i))],
        scratch_shapes=[pltpu.VMEM((rows * layers, width), F32), *sums],
        compiler_params=GRANT,
        name="project_first",
    )(rows_of, angles, volume)


def back_kernel(
    angle_ref, cut_ref, *refs, depth, tilts, boxes, groups, scale
):
    metas, (out_ref, lhs, sines) = refs[:groups], refs[groups:]
    step = pl.program_id(0)
    me = lax.axis_index("tilt")
    rows, layers, width = out_ref.shape
    slab_rows, length = rows // boxes, cut_ref.shape[1]
    apart = iota_apart((width, width), 0, 1)

    @pl.when(step == 0)
    def _():
        note_sines(angle_ref, sines)
        ahead = lax.broadcasted_iota(jnp.int32, (slab_rows, length), 1)
        ahead = (ahead - lax.broadcasted_iota(jnp.int32, (slab_rows, length), 0)).astype(F32)
        for k in range(groups):
            group = (me ^ k)
            for t in range(tilts):
                picks = []
                for b in range(boxes):
                    slot = metas[k][t * boxes + b : t * boxes + b + 1, :1].astype(F32)
                    picks.append(ones_where(ahead == slot * float(slab_rows)))
                start = (k * tilts + t) * width
                lhs[:, start : start + width] = jnp.dot(
                    jnp.concatenate(picks, axis=0), cut_ref[group], preferred_element_type=F32
                ).astype(BF)

    def block(k, t, z):
        sine = sines[(me ^ k) * tilts + t]
        return tap_block(apart, sine, step * layers + z, depth)

    flat = out_ref.reshape(rows * layers, width)
    for z in range(0, layers, 2):
        table = jnp.concatenate(
            [
                jnp.concatenate([block(k, t, z + half) for half in range(2)], axis=1)
                for k in range(groups)
                for t in range(tilts)
            ],
            axis=0,
        )
        result = jnp.dot(lhs[...], table, preferred_element_type=F32) * scale
        for half in range(2):
            flat[pl.ds(z + half, rows, stride=layers), :] = result[
                :, half * width : (half + 1) * width
            ]


def back_project(cuts, slabs, angles, boxes, tilts, rows, depth, scale):
    groups, _, width = cuts.shape
    layers = min(8, depth)
    meta = slabs[0].shape[0] - tilts * rows
    at = tilts * rows // meta
    scalars = pl.BlockSpec(memory_space=pltpu.SMEM)
    return pl.pallas_call(
        functools.partial(
            back_kernel, depth=depth, tilts=tilts, boxes=boxes, groups=groups, scale=scale
        ),
        out_shape=jax.ShapeDtypeStruct((rows, depth, width), F32),
        grid=(depth // layers,),
        in_specs=[scalars]
        + [pl.BlockSpec(cuts.shape, lambda i: (0, 0, 0))]
        + [pl.BlockSpec((meta, width), lambda i: (at, 0))] * groups,
        out_specs=pl.BlockSpec((rows, layers, width), lambda i: (0, i, 0)),
        scratch_shapes=[
            pltpu.VMEM((rows, groups * tilts * width), BF),
            pltpu.VMEM((groups * tilts, 8, width), F32),
        ],
        compiler_params=GRANT,
        name="back_project",
    )(angles, cuts, *slabs)


def pack_kernel(row_ref, col_ref, *refs, groups, tile_count, strip_rows, capacity, slab_rows):
    slabs, outs = refs[:groups], refs[groups : groups + tile_count]
    item_ref, within_ref, left_ref = refs[groups + tile_count :]
    _, boxes = row_ref.shape
    width = slabs[0].shape[1]
    height = slab_rows * groups
    my_tilt, my_tile = lax.axis_index("tilt"), lax.axis_index("tile")
    strips, slots = slots_of_items(row_ref, strip_rows, capacity)
    margin = 2 * capacity

    def clear(i, carry):
        item_ref[i] = -1
        within_ref[i] = ABSENT
        left_ref[i] = 0
        return carry

    lax.fori_loop(0, tile_count * capacity + 2 * margin, clear, 0)
    for n, (strip, slot) in enumerate(zip(strips, slots, strict=True)):
        t, b = n // boxes, n % boxes
        item_ref[slot + margin] = n
        within_ref[slot + margin] = row_ref[t, b] - strip * strip_rows + t * strip_rows
        left_ref[slot + margin] = col_ref[t, b]
    sources = [my_tilt ^ k for k in range(groups)]

    def slab_of(k, item, begin, size):
        start = pl.multiple_of(jnp.maximum(item, 0) * slab_rows + begin, 16)
        block = slabs[k][pl.ds(start, size), :]
        return jnp.where(item >= 0, block, jnp.zeros_like(block))

    for d in range(tile_count):
        out = outs[d]
        strip = lax.rem(my_tile + d, tile_count)
        metas = []

        def item_at(offset, r):
            spot = (strip + offset + 2) * capacity + r
            metas.append(within_ref[spot])
            metas.append(left_ref[spot])
            return item_ref[spot]

        for r in range(capacity):
            item = item_at(0, r)
            for k in range(groups):
                begin = pl.multiple_of(r * height + sources[k] * slab_rows, slab_rows)
                out[pl.ds(begin, slab_rows), :] = slab_of(k, item, 0, slab_rows)
        base = capacity * height
        for offset, wanted, begin in ((2, 0, 0), (-2, groups - 1, slab_rows - REACH)):
            for r in range(capacity):
                item = item_at(offset, r)
                block = slab_of(0, item, begin, REACH)
                for k in range(1, groups):
                    block = jnp.where(sources[k] == wanted, slab_of(k, item, begin, REACH), block)
                out[base : base + REACH, :] = block
                base += REACH
        out[base:, :] = splat_rows(metas, out.shape[0] - base, width)


def pack(slabs, rows_of, cols_of, slab_rows, tile_count, strip_rows, capacity):
    groups = len(slabs)
    width = slabs[0].shape[1]
    meta_rows = -(-6 * capacity // 16) * 16
    length = capacity * (slab_rows * groups + 2 * REACH) + meta_rows
    slots = (tile_count + 4) * capacity
    return pl.pallas_call(
        functools.partial(
            pack_kernel,
            groups=groups,
            tile_count=tile_count,
            strip_rows=strip_rows,
            capacity=capacity,
            slab_rows=slab_rows,
        ),
        out_shape=[jax.ShapeDtypeStruct((length, width), BF)] * tile_count,
        in_specs=[pl.BlockSpec(memory_space=pltpu.SMEM)] * 2
        + [pl.BlockSpec(memory_space=pltpu.VMEM)] * groups,
        out_specs=[pl.BlockSpec(memory_space=pltpu.VMEM)] * tile_count,
        scratch_shapes=[pltpu.SMEM((slots,), jnp.int32)] * 3,
        compiler_params=GRANT,
        name="pack",
    )(rows_of, cols_of, slabs[0], *[near(slab) for slab in slabs[1:]])


def hi_lo(block):
    high = block.astype(BF)
    return high, (block - high.astype(F32)).astype(BF)


def place_kernel(measured_ref, after_ref, *refs, tilts, strip_rows, height, capacity, tile_count):
    parcels = refs[:tile_count]
    canvas_ref, next_ref, prev_ref, placed, onehot = refs[tile_count:]
    _, width = parcels[0].shape
    rows, image_width = canvas_ref.shape[1:]
    column = iota_apart((width, image_width), 1, 0)
    apart = iota_apart((rows, height), 0, 1)
    edge_apart = iota_apart((REACH, REACH), 0, 1)
    base = capacity * height
    meta = base + 2 * capacity * REACH

    def spread_out(parcel, begin, size, q):
        left = parcel[meta + 2 * q + 1 : meta + 2 * q + 2, :1]
        picks = ones_where(column == left)
        return jnp.dot(parcel[begin : begin + size, :], picks, preferred_element_type=F32).astype(BF)

    def row_of(parcel, q, t):
        own = parcel[meta + 2 * q : meta + 2 * q + 1, :].astype(F32) - float(t * strip_rows)
        return jnp.where((own >= 0) & (own < strip_rows), own, float(ABSENT))

    index = 0
    for parcel in parcels:
        for r in range(capacity):
            placed[index * height : (index + 1) * height, :] = spread_out(parcel, r * height, height, r)
            for t in range(tilts):
                target = (row_of(parcel, r, t) + float(REACH)).astype(BF)
                onehot[t * rows : (t + 1) * rows, index * height : (index + 1) * height] = (
                    ones_where(apart == target)
                )
            index += 1
    total = jnp.dot(onehot[...], placed[...], preferred_element_type=F32)
    for t in range(tilts):
        canvas_ref[t] = total[t * rows : (t + 1) * rows]
    for side in range(2):
        blocks = [[] for _ in range(tilts)]
        values = []
        for parcel in parcels:
            for r in range(capacity):
                q = (1 + side) * capacity + r
                begin = base + side * capacity * REACH + r * REACH
                values.append(spread_out(parcel, begin, REACH, q))
                for t in range(tilts):
                    target = row_of(parcel, q, t)[:, :REACH]
                    if side == 1:
                        target = target + float(height - 2 * strip_rows)
                    blocks[t].append(ones_where(edge_apart == target.astype(BF)))
        tall = jnp.concatenate(values, axis=0)
        for t in range(tilts):
            picks = jnp.concatenate(blocks[t], axis=1)
            edge = jnp.dot(picks, tall, preferred_element_type=F32)
            begin = rows - REACH if side == 0 else 0
            canvas_ref[t, begin : begin + REACH, :] = edge
    reach = strip_rows + REACH
    for t in range(tilts):
        next_ref[t, :reach, :] = canvas_ref[t, strip_rows : strip_rows + reach, :].astype(BF)
        prev_ref[t, :reach, :] = canvas_ref[t, REACH : REACH + reach, :].astype(BF)
        high, low = hi_lo(measured_ref[t, strip_rows - HR :, :])
        next_ref[t, reach:, :] = jnp.concatenate([high, low], axis=0)
        high, low = hi_lo(after_ref[t, :HR, :])
        prev_ref[t, reach:, :] = jnp.concatenate([high, low], axis=0)


def place(measured, after, parcels, height, capacity):
    tilts, strip_rows, image_width = measured.shape
    tile_count = len(parcels)
    rows = 2 * strip_rows + 2 * REACH
    halo = strip_rows + REACH + 2 * HR
    whole = pl.BlockSpec(memory_space=pltpu.VMEM)
    return pl.pallas_call(
        functools.partial(
            place_kernel,
            tilts=tilts,
            strip_rows=strip_rows,
            height=height,
            capacity=capacity,
            tile_count=tile_count,
        ),
        out_shape=[
            jax.ShapeDtypeStruct((tilts, rows, image_width), F32),
            jax.ShapeDtypeStruct((tilts, halo, image_width), BF),
            jax.ShapeDtypeStruct((tilts, halo, image_width), BF),
        ],
        in_specs=[whole] * (2 + tile_count),
        out_specs=[whole] * 3,
        scratch_shapes=[
            pltpu.VMEM((tile_count * capacity * height, image_width), BF),
            pltpu.VMEM((tilts * rows, tile_count * capacity * height), BF),
        ],
        compiler_params=GRANT,
        name="place",
    )(measured, near(after), parcels[0], *[near(p) for p in parcels[1:]])


def transfer_kernel(defocus_ref, out_ref):
    tilts, _, image_width, _ = out_ref.shape
    lanes = 128
    row = lax.broadcasted_iota(jnp.int32, (8, lanes), 0)
    lane = lax.broadcasted_iota(jnp.int32, (8, lanes), 1)
    down = lax.broadcasted_iota(jnp.int32, (8, lanes), 0)
    for t in range(tilts):
        for i in range(HR + 1):
            rho_sq = (i * i + lane * lane).astype(F32)
            value = jnp.exp(-rho_sq / (2.0 * HR * HR)) * jnp.cos(defocus_ref[t] * rho_sq) / float(HR * HR)
            value = jnp.where(lane <= HR, value, 0.0)
            for begin in range(0, image_width, 16):
                for column in range(0, image_width, lanes):
                    if begin - column > lanes + HR or column - begin > 16 + HR:
                        out_ref[t, i, begin : begin + 16, column : column + lanes] = jnp.zeros(
                            (16, lanes), BF
                        )
                        continue
                    parts = []
                    for half in range(2):
                        apart = jnp.abs(down + (begin + 8 * half - column) - lane)
                        parts.append(
                            jnp.take_along_axis(value, jnp.minimum(apart, lanes - 1), axis=1)
                        )
                    out_ref[t, i, begin : begin + 16, column : column + lanes] = jnp.concatenate(
                        parts, axis=0
                    ).astype(BF)


def transfer_tables(defocus, image_width):
    return pl.pallas_call(
        transfer_kernel,
        out_shape=jax.ShapeDtypeStruct((defocus.shape[0], HR + 1, image_width, image_width), BF),
        in_specs=[pl.BlockSpec(memory_space=pltpu.SMEM)],
        out_specs=pl.BlockSpec(memory_space=pltpu.VMEM),
        compiler_params=GRANT,
        name="transfer",
    )(defocus)


def convolve(source, parts, table_ref, t, height):
    rows = source.shape[0]
    for i in range(HR + 1):
        parts[i, :rows, :] = jnp.dot(source, table_ref[t, i], preferred_element_type=F32)
    total = parts[0, HR : HR + height, :]
    for i in range(1, HR + 1):
        total = total + (
            parts[i, HR + i : HR + i + height, :] + parts[i, HR - i : HR - i + height, :]
        )
    return total


def filter_kernel(
    canvas_ref, above_ref, below_ref, measured_ref, after_ref, table_ref, *refs, height, capacity
):
    tile_count = len(refs) - 4
    parcels, (residual_ref, out_ref, parts, back) = refs[:tile_count], refs[tile_count:]
    groups = out_ref.shape[0]
    slab_rows = height // groups
    tilts, strip_rows, image_width = measured_ref.shape
    rows = canvas_ref.shape[1]
    my_tile = lax.axis_index("tile")
    first = my_tile * strip_rows
    image_rows = tile_count * strip_rows
    reach = strip_rows + REACH

    def inside(count, start):
        at = lax.broadcasted_iota(jnp.int32, (count, image_width), 0) + (first + start)
        return (at >= 0) & (at < image_rows)

    at_top, at_end = my_tile == 0, my_tile == tile_count - 1
    for t in range(tilts):
        upper = jnp.where(at_top, 0.0, above_ref[t, :reach, :].astype(F32))
        lower = jnp.where(at_end, 0.0, below_ref[t, :reach, :].astype(F32))
        field = canvas_ref[t] + jnp.concatenate([upper, lower], axis=0)
        field = jnp.where(inside(rows, -REACH), field, 0.0)
        known = jnp.concatenate(
            [
                above_ref[t, reach : reach + HR, :].astype(F32)
                + above_ref[t, reach + HR :, :].astype(F32),
                measured_ref[t],
                after_ref[t],
                below_ref[t, reach : reach + HR, :].astype(F32)
                + below_ref[t, reach + HR :, :].astype(F32),
            ],
            axis=0,
        )
        count = rows - 2 * HR
        rest = known - convolve(field.astype(BF), parts, table_ref, t, count)
        residual_ref[t] = rest[HR : HR + strip_rows]
        rest = jnp.where(inside(count, -HR), rest, 0.0)
        count -= 2 * HR
        image = convolve(rest.astype(BF), parts, table_ref, t, count)
        back[t * count : (t + 1) * count, :] = jnp.where(inside(count, 0), image, 0.0).astype(BF)
    width = parcels[0].shape[1]
    count = 2 * strip_rows
    apart = iota_apart((height, count), 1, 0)
    column = iota_apart((image_width, width), 0, 1)
    meta = capacity * (height + 2 * REACH)
    for d, parcel in enumerate(parcels):
        sender = lax.rem(my_tile + tile_count - d, tile_count)
        for r in range(capacity):
            top = parcel[meta + 2 * r : meta + 2 * r + 1, :].astype(F32)
            picks = []
            for t in range(tilts):
                own = top - float(t * strip_rows)
                own = jnp.where((own >= 0) & (own < strip_rows), own, float(ABSENT)).astype(BF)
                picks.append(ones_where(apart == own[:, :1]))
            cut = jnp.dot(
                jnp.concatenate(picks, axis=1), back[...], preferred_element_type=F32
            ).astype(BF)
            left = parcel[meta + 2 * r + 1 : meta + 2 * r + 2, :]
            columns = ones_where(column == left)
            window = jnp.dot(cut, columns, preferred_element_type=F32).astype(BF)
            for i in range(groups):
                out_ref[i, sender, r * slab_rows : (r + 1) * slab_rows, :] = window[
                    i * slab_rows : (i + 1) * slab_rows
                ]


def filter_and_cut(canvas, above, below, measured, after, table, parcels, height, capacity, groups):
    tilts, strip_rows, image_width = measured.shape
    tile_count = len(parcels)
    width = parcels[0].shape[1]
    rows = canvas.shape[1]
    whole = pl.BlockSpec(memory_space=pltpu.VMEM)
    slots = (groups, tile_count, capacity * height // groups, width)
    return pl.pallas_call(
        functools.partial(filter_kernel, height=height, capacity=capacity),
        out_shape=[jax.ShapeDtypeStruct(measured.shape, F32), jax.ShapeDtypeStruct(slots, BF)],
        in_specs=[whole] * (6 + tile_count),
        out_specs=[whole] * 2,
        scratch_shapes=[
            pltpu.VMEM((HR + 1, rows, image_width), F32),
            pltpu.VMEM((tilts * 2 * strip_rows, image_width), BF),
        ],
        compiler_params=GRANT,
        name="filter_and_cut",
    )(near(canvas), near(above), near(below), measured, near(after), near(table), parcels[0], *[near(p) for p in parcels[1:]])


def shards(volumes, angles, defocus, row_offsets, col_offsets, measured):
    boxes, slab_rows, depth, width = volumes.shape
    tilts, strip_rows, image_width = measured.shape
    tile_count, groups = lax.axis_size("tile"), lax.axis_size("tilt")
    height, rows = slab_rows * groups, boxes * slab_rows
    capacity = max(2, -(-boxes * tilts // tile_count))
    assert tilts * strip_rows <= 256 and tile_count * capacity <= 256
    rows_of, cols_of, angles = far(row_offsets.T), far(col_offsets.T), far(angles)
    kernel = transfer_tables(defocus, image_width)
    slabs = [None] * groups
    volume = far(volumes.reshape(rows, depth, width))
    half = groups // 2 + 1
    early, middle = tuple(range(1, half)), tuple(range(half, groups))
    sizes = (depth, width, strip_rows, capacity)
    *parts, flat = project(volume, rows_of, angles, tilts, groups, early, True, *sizes)
    sent = measured
    for k, part in zip(early, parts, strict=True):
        slabs[k] = swap(part, "tilt", k)
    if middle:
        parts = project(flat, rows_of, angles, tilts, groups, middle, False, *sizes)
        sent, *parts = lax.optimization_barrier((measured, *parts))
        for k, part in zip(middle, parts, strict=True):
            slabs[k] = swap(part, "tilt", k)
    after = ring(sent, "tile", -1)
    (slabs[0],) = project(flat, rows_of, angles, tilts, groups, (0,), False, *sizes)
    parcels = pack(slabs, rows_of, cols_of, slab_rows, tile_count, strip_rows, capacity)
    parcels = [p if d == 0 else ring(p, "tile", d) for d, p in enumerate(parcels)]
    canvas, onward, backward = place(measured, after, parcels, height, capacity)
    above, below = ring(onward, "tile", 1), ring(backward, "tile", -1)
    residual, cuts = filter_and_cut(
        canvas, above, below, measured, after, kernel, parcels, height, capacity, groups
    )
    cuts = cuts.reshape(groups * tile_count, capacity * slab_rows, width)
    cuts = lax.all_to_all(cuts, ("tilt", "tile"), split_axis=0, concat_axis=0, tiled=True)
    cuts = cuts.reshape(groups, tile_count * capacity * slab_rows, width)
    step = back_project(cuts, slabs, angles, boxes, tilts, rows, depth, 1.0 / (tilts * groups))
    return residual, step.reshape(boxes, slab_rows, depth, width)


def solution(mesh):
    in_specs = (
        P("tile", "tilt", None, None),
        P(),
        P("tilt"),
        P("tile", "tilt"),
        P("tile", "tilt"),
        P("tilt", "tile", None),
    )
    out_specs = (P("tilt", "tile", None), P("tile", "tilt", None, None))

    return jax.shard_map(shards, mesh=mesh, in_specs=in_specs, out_specs=out_specs, check_vma=False)
```
